32 devices in a mesh: dp: 4 (over y, x), ctx: 2 (over core), tp: 4 (over z).
Axes of the slice: x: 2, y: 2, z: 4, core: 2. Of those that a mesh axis runs over, the one named last changes fastest.
Arguments:
- tokens: bfloat16 [4, 1024, 768], P('dp', 'ctx'), may hold values from -42 to 42
- lengths: int32 [4], P('dp'), may hold values from 2 to 8, as said below
- w_query: bfloat16 [768, 512], P(None, 'tp'), may hold values from -0.21650635 to 0.21650635
- w_key: bfloat16 [768, 512], P(None, 'tp'), may hold values from -0.21650635 to 0.21650635
- w_value: bfloat16 [768, 512], P(None, 'tp'), may hold values from -0.21875 to 0.21875
- w_out: bfloat16 [512, 768], P('tp'), may hold values from -0.25 to 0.25
- grad_out: bfloat16 [4, 1024, 768], P('dp', 'ctx'), may hold values from -6 to 6
Outputs:
- grad_tokens: bfloat16 [4, 1024, 768], P('dp', ('ctx', 'tp'))
- grad_query: float32 [768, 512], P(None, 'tp')
- grad_key: float32 [768, 512], P(None, 'tp')
- grad_value: float32 [768, 512], P(None, 'tp')
- grad_w_out: float32 [512, 768], P('tp')
The draws below stay inside these ranges and needn't reach their ends.
Inputs may be any that keep to these rules, and one draw needn't show every extreme that they name: lengths[c] counts the valid blocks of 128 positions at the start of conversation c; one conversation is valid over its whole length and one over exactly a quarter of its blocks.
All inputs are finite; a program needn't handle non-finite values.
Results may differ from the reference program's by a relative error of at most 0.017.
Values may be sent and summed in bfloat16 or wider, within the bound.
A program may use at most 128 MiB of HBM per device.

```python
import jax
import jax.numpy as jnp
from jax import lax

D = 768
HEAD = 128
BLOCK = 128
LEVELS = 8
HEADS = 4
CONV = 4
SEQ = 1024
N_TP = 4


def draw_tokens(key, part):
    drawn_draw = jax.random.truncated_normal(jax.random.fold_in(key, 11), -6.0, 6.0, (CONV, SEQ, D), jnp.float32)
    return drawn_draw.astype(jnp.bfloat16)


def pair_weights(key):
    seeded = jax.random.fold_in(key, 21)
    primary = jax.random.truncated_normal(jax.random.fold_in(seeded, 1), -4.0, 4.0, (D, HEADS * HEAD), jnp.float32)
    secondary = jax.random.truncated_normal(jax.random.fold_in(seeded, 2), -4.0, 4.0, (D, HEADS * HEAD), jnp.float32)
    return (primary, secondary)


def draw_w_query(key, part):
    primary, secondary = pair_weights(key)
    return (primary * D ** (-0.5)).astype(jnp.bfloat16)


def draw_w_key(key, part):
    primary, secondary = pair_weights(key)
    return (secondary * D ** (-0.5)).astype(jnp.bfloat16)


def draw_lengths(key, part):
    blocks = SEQ // BLOCK
    picked = jax.random.randint(jax.random.fold_in(key, 31), (CONV,), blocks // 4, blocks + 1, jnp.int32)
    shuffled = jax.random.permutation(jax.random.fold_in(key, 32), CONV)
    picked = picked.at[shuffled[0]].set(blocks)
    picked = picked.at[shuffled[1]].set(blocks // 4)
    return picked


def level_of(rng, extent, pieces, smallest, largest):
    factor_of, own = 1.0, jax.random.fold_in(rng, 6)
    for position, shards_of in pieces:
        draws = jnp.exp(jax.random.uniform(jax.random.fold_in(own, position), (shards_of,), jnp.float32, smallest / len(pieces), largest / len(pieces)))
        factor_of = factor_of * jnp.repeat(draws, extent[position] // shards_of).reshape([-1 if axis == position else 1 for axis in range(len(extent))])
    return factor_of


def scatter_about(rng, dims, scale, reach, shards=(), held_as=jnp.bfloat16):
    array = jax.random.normal(rng, dims, jnp.float32) * scale
    if len(shards) > 0:
        array = level_of(rng, dims, shards, -0.22, 0.18) * array
    return jnp.clip(array, min=-reach, max=reach).astype(held_as)


def setup_inputs(seed: int = 0) -> dict:
    key_list = jax.random.split(jax.random.key(seed), 8)
    tokens = draw_tokens(jax.random.fold_in(key_list[7], 71), 0)
    lengths = draw_lengths(jax.random.fold_in(key_list[7], 71), 0)
    w_query = draw_w_query(jax.random.fold_in(key_list[7], 71), 0)
    w_key = draw_w_key(jax.random.fold_in(key_list[7], 71), 0)
    w_value = scatter_about(key_list[4], (D, HEADS * HEAD), D ** -0.5, 0.21875, ((1, 4),))
    w_out = scatter_about(key_list[5], (HEADS * HEAD, D), (HEADS * HEAD) ** -0.5, 0.25, ((0, 4),))
    grad_out = scatter_about(key_list[6], (CONV, SEQ, D), 1.0, 6.0, ((0, 4), (1, 2)))
    return {"tokens": tokens, "lengths": lengths, "w_query": w_query, "w_key": w_key, "w_value": w_value, "w_out": w_out, "grad_out": grad_out}


precise = lax.Precision.HIGHEST
very_low = -1e+30

def level_stats(queries, key_rows, values, query_pos, key_pos, height, block, weight):
    scores = jnp.einsum('nqe,nke->nqk', queries, key_rows, precision=precise) * queries.shape[-1] ** (-0.5)
    query_at = query_pos[:, :, None]
    key_at = key_pos[:, None, :]
    allowed = (query_at // block - key_at // block <= 1) & (key_at >= 0)
    if height == 0:
        allowed = allowed & (key_at <= query_at)
    else:
        half_block = block // 2
        allowed = allowed & (query_at // half_block - key_at // half_block >= 2)
    masked = jnp.where(allowed, scores, very_low)
    row_max = lax.optimization_barrier(jnp.max(masked, axis=-1))
    exp_scores = jnp.where(allowed, jnp.exp(masked - row_max[..., None]), 0.0)
    weighted = jnp.einsum('nqk,nke->nqe', exp_scores, values, precision=precise)
    totals = lax.optimization_barrier(jnp.sum(exp_scores, axis=-1)) * weight
    return (row_max, weighted, totals)

def coarse(field_data, group_size, summed):
    grouped = field_data.reshape(field_data.shape[:-2] + (field_data.shape[-2] // group_size, group_size, field_data.shape[-1]))
    if summed:
        return lax.optimization_barrier(jnp.sum(grouped, axis=-2))
    return lax.optimization_barrier(jnp.mean(grouped, axis=-2))

def merge_levels(stats_list):
    best_max, running, mass_sum = stats_list[0]
    for row_max, weighted, totals in stats_list[1:]:
        new_best = jnp.maximum(best_max, row_max)
        keep_old = jnp.exp(best_max - new_best)
        gain_new = jnp.exp(row_max - new_best)
        running = running * keep_old[..., None] + weighted * gain_new[..., None]
        mass_sum = mass_sum * keep_old + totals * gain_new
        best_max = new_best
    return running / mass_sum[..., None]

def attend_sequence(queries, key_rows, values):
    seq_length = queries.shape[0]
    stats_list = []
    for height in range(LEVELS):
        group_size = 2 ** height
        coarse_rows = seq_length // group_size
        block_span = min(coarse_rows, BLOCK)
        block_count = coarse_rows // block_span
        coarse_query = coarse(queries, group_size, False).reshape(block_count, block_span, -1)
        coarse_key = coarse(key_rows, group_size, False).reshape(block_count, block_span, -1)
        coarse_value = coarse(values, group_size, True).reshape(block_count, block_span, -1)
        zero_block = jnp.zeros_like(coarse_key[:1])
        key_win = jnp.concatenate([jnp.concatenate([zero_block, coarse_key[:-1]], 0), coarse_key], 1)
        value_win = jnp.concatenate([jnp.concatenate([zero_block, coarse_value[:-1]], 0), coarse_value], 1)
        query_pos = jnp.arange(coarse_rows, dtype=jnp.int32).reshape(block_count, block_span)
        key_pos = jnp.concatenate([query_pos - block_span, query_pos], 1)
        row_max, weighted, totals = level_stats(coarse_query, key_win, value_win, query_pos, key_pos, height, BLOCK, float(group_size))
        stats_list.append((jnp.repeat(row_max.reshape(coarse_rows), group_size, 0), jnp.repeat(weighted.reshape(coarse_rows, -1), group_size, 0), jnp.repeat(totals.reshape(coarse_rows), group_size, 0)))
    return merge_levels(stats_list)

def reference(tokens, lengths, w_query, w_key, w_value, w_out, grad_out):
    conversations, seq_length, model_width = tokens.shape
    flat_tokens = tokens.reshape(conversations * seq_length, model_width)
    head_count = w_query.shape[1] // HEAD

    def split_heads(matrix):
        return matrix.reshape(conversations, seq_length, head_count, HEAD).transpose(0, 2, 1, 3).reshape(conversations * head_count, seq_length, HEAD)

    def join_heads(field_data):
        return field_data.reshape(conversations, head_count, seq_length, HEAD).transpose(0, 2, 1, 3).reshape(conversations * seq_length, head_count * HEAD)
    queries = split_heads(jnp.dot(flat_tokens, w_query, preferred_element_type=jnp.float32))
    key_rows = split_heads(jnp.dot(flat_tokens, w_key, preferred_element_type=jnp.float32))
    values = split_heads(jnp.dot(flat_tokens, w_value, preferred_element_type=jnp.float32))

    def attend_all(all_queries, all_keys, all_values):
        return lax.map(lambda triple: attend_sequence(triple[0], triple[1], triple[2]), (all_queries, all_keys, all_values))
    attended, pullback = jax.vjp(attend_all, queries, key_rows, values)
    mixed_heads = join_heads(attended).astype(jnp.bfloat16)
    places = jnp.arange(seq_length, dtype=jnp.int32)
    valid_rows = places[None, :] < lengths[:, None] * BLOCK
    cotangent = jnp.where(valid_rows[:, :, None], grad_out, jnp.zeros_like(grad_out)).reshape(conversations * seq_length, model_width)
    grad_scale = float(conversations * seq_length) ** (-0.5)
    grad_mixed = jnp.dot(cotangent, w_out.T, preferred_element_type=jnp.float32)
    grad_q, grad_k, grad_v = pullback(split_heads(grad_mixed))
    rounded = [join_heads(grad_field).astype(jnp.bfloat16) for grad_field in (grad_q, grad_k, grad_v)]
    per_group = head_count * HEAD // N_TP
    grad_tokens = jnp.zeros((conversations * seq_length, model_width), jnp.float32)
    for group_index in range(N_TP):
        columns = slice(group_index * per_group, (group_index + 1) * per_group)
        partial_term = jnp.dot(rounded[0][:, columns], w_query[:, columns].T, preferred_element_type=jnp.float32) + jnp.dot(rounded[1][:, columns], w_key[:, columns].T, preferred_element_type=jnp.float32) + jnp.dot(rounded[2][:, columns], w_value[:, columns].T, preferred_element_type=jnp.float32)
        partial_inputs = lax.optimization_barrier(partial_term.astype(jnp.bfloat16))
        grad_tokens = grad_tokens + partial_inputs.astype(jnp.float32)
    grad_tokens = grad_tokens.astype(jnp.bfloat16).reshape(conversations, seq_length, model_width)
    grad_query = jnp.dot(flat_tokens.T, rounded[0], preferred_element_type=jnp.float32) * grad_scale
    grad_key = jnp.dot(flat_tokens.T, rounded[1], preferred_element_type=jnp.float32) * grad_scale
    grad_value = jnp.dot(flat_tokens.T, rounded[2], preferred_element_type=jnp.float32) * grad_scale
    grad_w_out = jnp.dot(mixed_heads.T, cotangent, preferred_element_type=jnp.float32) * grad_scale
    return (grad_tokens, grad_query, grad_key, grad_value, grad_w_out)
```

```python
from functools import partial

import jax
import jax.numpy as jnp
from jax import lax
from jax.experimental import pallas as pl
from jax.experimental.pallas import tpu as pltpu
from jax.sharding import PartitionSpec as P

HEAD = 128
BLOCK = 128
LEVELS = 8


precise = lax.Precision.HIGHEST
very_low = -1e30


def passed_along(value, axis, steps):
    count = lax.axis_size(axis)
    first, last = (max(0, -steps), min(count, count - steps))
    return lax.ppermute(value, axis, [(source, source + steps) for source in range(first, last)])


def level_stats(queries, key_rows, values, query_pos, key_pos, height, block, weight):
    scores = jnp.einsum("nqe,nke->nqk", queries, key_rows, precision=precise) * queries.shape[
        -1
    ] ** (-0.5)
    query_at = query_pos[:, :, None]
    key_at = key_pos[:, None, :]
    allowed = (query_at // block - key_at // block <= 1) & (key_at >= 0)
    if height == 0:
        allowed = allowed & (key_at <= query_at)
    else:
        half_block = block // 2
        allowed = allowed & (query_at // half_block - key_at // half_block >= 2)
    masked = jnp.where(allowed, scores, very_low)
    row_max = jnp.max(masked, axis=-1)
    exp_scores = jnp.where(allowed, jnp.exp(masked - row_max[..., None]), 0.0)
    weighted = jnp.einsum("nqk,nke->nqe", exp_scores, values, precision=precise)
    totals = jnp.sum(exp_scores, axis=-1) * weight
    return (row_max, weighted, totals)


def head_stats(queries, key_rows, values, query_pos, key_pos, height, block, weight):
    single = partial(level_stats, height=height, block=block, weight=weight)
    return jax.vmap(single, in_axes=(0, 0, 0, None, None))(
        queries, key_rows, values, query_pos, key_pos
    )


def coarse(field_data, group_size, summed):
    grouped = field_data.reshape(
        field_data.shape[:-2]
        + (field_data.shape[-2] // group_size, group_size, field_data.shape[-1])
    )
    if summed:
        return jnp.sum(grouped, axis=-2)
    return jnp.mean(grouped, axis=-2)


def merge_levels(stats_list):
    best_max, running, mass_sum = stats_list[0]
    for row_max, weighted, totals in stats_list[1:]:
        new_best = jnp.maximum(best_max, row_max)
        keep_old = jnp.exp(best_max - new_best)
        gain_new = jnp.exp(row_max - new_best)
        running = running * keep_old[..., None] + weighted * gain_new[..., None]
        mass_sum = mass_sum * keep_old + totals * gain_new
        best_max = new_best
    return running / mass_sum[..., None]


def earlier(payload, distance):
    return passed_along(payload.astype(jnp.bfloat16), "ctx", distance).astype(payload.dtype)


def returned(payload, distance):
    return passed_along(payload.astype(jnp.bfloat16), "ctx", -distance).astype(payload.dtype)


def local(tokens, lengths, w_query, w_key, w_value, w_out, grad_out):
    devices = lax.axis_size("ctx")
    ctx_index = lax.axis_index("ctx")
    local_rows = tokens.shape[1]
    token_total = lax.axis_size("dp") * devices * local_rows
    grad_scale = float(token_total) ** (-0.5)
    flat_tokens = tokens[0]
    head_count = w_query.shape[1] // HEAD

    def split_heads(matrix):
        return matrix.reshape(local_rows, head_count, HEAD).transpose(1, 0, 2)

    def join_heads(field_data):
        return field_data.transpose(1, 0, 2).reshape(local_rows, head_count * HEAD)

    queries = split_heads(jnp.dot(flat_tokens, w_query, preferred_element_type=jnp.float32))
    key_rows = split_heads(jnp.dot(flat_tokens, w_key, preferred_element_type=jnp.float32))
    values = split_heads(jnp.dot(flat_tokens, w_value, preferred_element_type=jnp.float32))
    group_sizes = [2**height for height in range(LEVELS)]
    fine_levels = [height for height in range(LEVELS) if local_rows // group_sizes[height] >= BLOCK]
    rough_levels = [height for height in range(LEVELS) if local_rows // group_sizes[height] < BLOCK]

    def coarsen(all_queries, all_keys, all_values):
        return (
            [coarse(all_queries, group_sizes[height], False) for height in range(LEVELS)],
            [coarse(all_keys, group_sizes[height], False) for height in range(LEVELS)],
            [coarse(all_values, group_sizes[height], True) for height in range(LEVELS)],
        )

    (coarse_query, coarse_key, coarse_value), coarse_pull = jax.vjp(
        coarsen, queries, key_rows, values
    )
    tail_rows = jnp.stack(
        [
            jnp.concatenate([coarse_key[height][:, -BLOCK:] for height in fine_levels], 1),
            jnp.concatenate([coarse_value[height][:, -BLOCK:] for height in fine_levels], 1),
        ],
        0,
    )
    coarse_pack = jnp.stack(
        [
            jnp.concatenate([coarse_key[height] for height in rough_levels], 1),
            jnp.concatenate([coarse_value[height] for height in rough_levels], 1),
        ],
        0,
    )
    tail_count = tail_rows.shape[2]
    reach_devs = 2 * BLOCK // (local_rows // group_sizes[rough_levels[-1]])
    step_count = reach_devs.bit_length() - 1
    first_move = earlier(jnp.concatenate([tail_rows, coarse_pack], 2), 1)
    prior_tails = first_move[:, :, :tail_count]
    window = jnp.stack([first_move[:, :, tail_count:], coarse_pack], 0)
    for bit_pos in range(1, step_count):
        distance = 2**bit_pos
        if distance < devices:
            moved_rows = earlier(window, distance)
        else:
            moved_rows = jnp.zeros_like(window)
        window = jnp.concatenate([moved_rows, window], 0)
    prior_in = window[:-1]

    def attend_local(query_list, key_list, value_list, tails_in, rows_in):
        stats_list = []
        tail_at = 0
        rough_at = 0
        for height in range(LEVELS):
            group_size = group_sizes[height]
            coarse_rows = local_rows // group_size
            own_pos = ctx_index * coarse_rows + jnp.arange(coarse_rows, dtype=jnp.int32)
            if height in fine_levels:
                blocks = coarse_rows // BLOCK
                query_blocks = query_list[height].reshape(head_count, blocks, BLOCK, -1)
                key_blocks = key_list[height].reshape(head_count, blocks, BLOCK, -1)
                value_blocks = value_list[height].reshape(head_count, blocks, BLOCK, -1)
                prev_keys = tails_in[0][:, tail_at : tail_at + BLOCK][:, None]
                prev_values = tails_in[1][:, tail_at : tail_at + BLOCK][:, None]
                key_win = jnp.concatenate(
                    [jnp.concatenate([prev_keys, key_blocks[:, :-1]], 1), key_blocks], 2
                )
                value_win = jnp.concatenate(
                    [jnp.concatenate([prev_values, value_blocks[:, :-1]], 1), value_blocks], 2
                )
                query_pos = own_pos.reshape(blocks, BLOCK)
                key_pos = jnp.concatenate([query_pos - BLOCK, query_pos], 1)
                tail_at += BLOCK
            else:
                query_blocks = query_list[height][:, None]
                query_pos = own_pos[None]
                need_devs = 2 * BLOCK // coarse_rows
                earlier_keys = rows_in[
                    rows_in.shape[0] - (need_devs - 1) :, 0, :, rough_at : rough_at + coarse_rows
                ]
                earlier_values = rows_in[
                    rows_in.shape[0] - (need_devs - 1) :, 1, :, rough_at : rough_at + coarse_rows
                ]
                key_win = jnp.concatenate(
                    [
                        earlier_keys.transpose(1, 0, 2, 3).reshape(
                            head_count, (need_devs - 1) * coarse_rows, -1
                        ),
                        key_list[height],
                    ],
                    1,
                )[:, None]
                value_win = jnp.concatenate(
                    [
                        earlier_values.transpose(1, 0, 2, 3).reshape(
                            head_count, (need_devs - 1) * coarse_rows, -1
                        ),
                        value_list[height],
                    ],
                    1,
                )[:, None]
                key_pos = (
                    (ctx_index + 1) * coarse_rows
                    - need_devs * coarse_rows
                    + jnp.arange(need_devs * coarse_rows, dtype=jnp.int32)
                )[None]
                rough_at += coarse_rows
            row_max, weighted, totals = head_stats(
                query_blocks,
                key_win,
                value_win,
                query_pos,
                key_pos,
                height,
                BLOCK,
                float(group_size),
            )
            stats_list.append(
                (
                    jnp.repeat(row_max.reshape(head_count, coarse_rows), group_size, 1),
                    jnp.repeat(weighted.reshape(head_count, coarse_rows, -1), group_size, 1),
                    jnp.repeat(totals.reshape(head_count, coarse_rows), group_size, 1),
                )
            )
        return merge_levels(stats_list)

    attended, attend_pull = jax.vjp(
        attend_local, coarse_query, coarse_key, coarse_value, prior_tails, prior_in
    )
    mixed_heads = join_heads(attended).astype(jnp.bfloat16)
    positions = ctx_index * local_rows + jnp.arange(local_rows, dtype=jnp.int32)
    valid_rows = positions < lengths[0] * BLOCK
    cotangent = jnp.where(valid_rows[:, None], grad_out[0], jnp.zeros_like(grad_out[0]))
    grad_mixed = jnp.dot(cotangent, w_out.T, preferred_element_type=jnp.float32)
    grad_cquery, grad_ckey, grad_cvalue, grad_tails, grad_prior = attend_pull(
        split_heads(grad_mixed)
    )
    grad_cquery = list(grad_cquery)
    grad_ckey = list(grad_ckey)
    grad_cvalue = list(grad_cvalue)
    gradient = jnp.concatenate([grad_prior, jnp.zeros_like(coarse_pack)[None]], 0)
    for bit_pos in range(step_count - 1, 0, -1):
        distance = 2**bit_pos
        upper_part = gradient[distance:]
        if distance < devices:
            upper_part = upper_part + returned(gradient[:distance], distance)
        gradient = upper_part
    sent_back = returned(jnp.concatenate([grad_tails, gradient[0]], 2), 1)
    tails_back = sent_back[:, :, :tail_count]
    pack_back = sent_back[:, :, tail_count:] + gradient[1]
    tail_at = 0
    for height in fine_levels:
        grad_ckey[height] = (
            grad_ckey[height].at[:, -BLOCK:].add(tails_back[0, :, tail_at : tail_at + BLOCK])
        )
        grad_cvalue[height] = (
            grad_cvalue[height].at[:, -BLOCK:].add(tails_back[1, :, tail_at : tail_at + BLOCK])
        )
        tail_at += BLOCK
    rough_at = 0
    for height in rough_levels:
        coarse_rows = local_rows // group_sizes[height]
        grad_ckey[height] = grad_ckey[height] + pack_back[0, :, rough_at : rough_at + coarse_rows]
        grad_cvalue[height] = (
            grad_cvalue[height] + pack_back[1, :, rough_at : rough_at + coarse_rows]
        )
        rough_at += coarse_rows
    grad_q, grad_k, grad_v = coarse_pull((grad_cquery, grad_ckey, grad_cvalue))
    rounded_q = join_heads(grad_q).astype(jnp.bfloat16)
    rounded_k = join_heads(grad_k).astype(jnp.bfloat16)
    rounded_v = join_heads(grad_v).astype(jnp.bfloat16)
    partial_term = (
        jnp.dot(rounded_q, w_query.T, preferred_element_type=jnp.float32)
        + jnp.dot(rounded_k, w_key.T, preferred_element_type=jnp.float32)
        + jnp.dot(rounded_v, w_value.T, preferred_element_type=jnp.float32)
    )
    grad_tokens = lax.psum_scatter(
        partial_term.astype(jnp.bfloat16), "tp", scatter_dimension=0, tiled=True
    )[None]
    stacked_in = jnp.concatenate([rounded_q, rounded_k, rounded_v], 1)
    grads_in = jnp.einsum("rc,rh->ch", flat_tokens, stacked_in, preferred_element_type=jnp.float32)
    grads_out = jnp.einsum("rc,rh->ch", cotangent, mixed_heads, preferred_element_type=jnp.float32)
    summed = lax.psum(jnp.concatenate([grads_in, grads_out], 1) * grad_scale, ("dp", "ctx"))
    head_cols = head_count * HEAD
    grad_query = summed[:, :head_cols]
    grad_key = summed[:, head_cols : 2 * head_cols]
    grad_value = summed[:, 2 * head_cols : 3 * head_cols]
    grad_w_out = summed[:, 3 * head_cols :].T
    return (grad_tokens, grad_query, grad_key, grad_value, grad_w_out)


F32 = jnp.float32
BF16 = jnp.bfloat16
NT = (((1,), (1,)), ((), ()))
NN = (((1,), (0,)), ((), ()))
TN = (((0,), (0,)), ((), ()))


def mm(a, b, dims):
    return lax.dot_general(a.astype(BF16), b.astype(BF16), dims, preferred_element_type=F32)


def mm3(a, b, dims):
    a_hi, b_hi = a.astype(BF16), b.astype(BF16)
    a_lo = (a - a_hi.astype(F32)).astype(BF16)
    b_lo = (b - b_hi.astype(F32)).astype(BF16)
    dot = partial(lax.dot_general, dimension_numbers=dims, preferred_element_type=F32)
    return dot(a_hi, b_hi) + (dot(a_hi, b_lo) + dot(a_lo, b_hi))


def pairs(ref, start, count):
    return ref[pl.ds(start, count, stride=2), :], ref[pl.ds(start + 1, count, stride=2), :]


def doubled(ref, value):
    count = value.shape[0]
    ref[pl.ds(0, count, stride=2), :] = value
    ref[pl.ds(1, count, stride=2), :] = value
    return ref[pl.ds(0, 2 * count), :]


def halved(ref, value):
    count = value.shape[0]
    ref[pl.ds(0, count), :] = value
    first, second = pairs(ref, 0, count // 2)
    return first + second


def level_sizes(rows, total):
    return [rows >> h for h in range(LEVELS) if h == 0 or (total >> h) > BLOCK]


def coarsen_keys(sizes, kw, vw):
    for h in range(1, len(sizes)):
        first, second = pairs(kw[h - 1], BLOCK, sizes[h])
        kw[h][pl.ds(BLOCK, sizes[h]), :] = (first + second) * 0.5
        first, second = pairs(vw[h - 1], BLOCK, sizes[h])
        vw[h][pl.ds(BLOCK, sizes[h]), :] = first + second


def coarsen_queries(sizes, qs):
    for h in range(1, len(sizes)):
        first, second = pairs(qs[h - 1], 0, sizes[h])
        qs[h][...] = (first + second) * 0.5


def span(h):
    return 2 * BLOCK if h == 0 else BLOCK


def block_mask(h, block, has_prior):
    row = lax.broadcasted_iota(jnp.int32, (BLOCK, span(h)), 0)
    col = lax.broadcasted_iota(jnp.int32, (BLOCK, span(h)), 1)
    if h == 0:
        allowed = col <= row + BLOCK
        if block == 0:
            allowed = allowed & ((col >= BLOCK) | has_prior)
    else:
        allowed = (row >= BLOCK // 2) | (col < BLOCK // 2)
        if block == 0:
            allowed = allowed & has_prior
    return allowed


def attend_block(h, block, has_prior, qs, kw, vw, probs, tops, nums, dens):
    rows = pl.ds(block * BLOCK, BLOCK)
    window = pl.ds(block * BLOCK, span(h))
    allowed = block_mask(h, block, has_prior)
    scores = mm3(qs[h][rows, :] * HEAD ** (-0.5), kw[h][window, :], NT)
    masked = jnp.where(allowed, scores, very_low)
    top = jnp.max(masked, axis=-1, keepdims=True)
    p = jnp.where(allowed, jnp.exp(masked - top), 0.0)
    probs[h][block] = p
    tops[h][rows, :] = jnp.broadcast_to(top, (BLOCK, HEAD))
    nums[h][rows, :] = mm3(p, vw[h][window, :], NN)
    dens[h][rows, :] = jnp.broadcast_to(
        jnp.sum(p, axis=-1, keepdims=True) * float(2**h), (BLOCK, HEAD)
    )


def merge(sizes, tops, nums, dens, keeps, gains, temp):
    last = len(sizes) - 1
    top, num, den = tops[last][...], nums[last][...], dens[last][...]
    keeps[last][...] = jnp.ones_like(top)
    for h in range(last - 1, -1, -1):
        top, num, den = (doubled(t, x) for t, x in zip(temp, (top, num, den)))
        own = tops[h][...]
        best = jnp.maximum(own, top)
        keep, gain = jnp.exp(own - best), jnp.exp(top - best)
        keeps[h][...] = keep
        gains[h][...] = gain
        num = nums[h][...] * keep + num * gain
        den = dens[h][...] * keep + den * gain
        top = best
    inverse = 1.0 / den
    return num * inverse, inverse


def back_stats(sizes, attended, inverse, grad_mixed, keeps, gains, gs, ds, temp):
    delta = jnp.sum(attended * grad_mixed, axis=-1, keepdims=True)
    flow, part = grad_mixed * inverse, delta * inverse
    for h in range(len(sizes)):
        gs[h][...] = flow * keeps[h][...]
        ds[h][...] = part * keeps[h][...]
        if h + 1 < len(sizes):
            flow = halved(temp[0], flow * gains[h][...])
            part = halved(temp[1], part * gains[h][...])


def back_block(h, block, qs, kw, vw, probs, gs, ds, dq, dk, dv):
    rows = pl.ds(block * BLOCK, BLOCK)
    window = pl.ds(block * BLOCK, span(h))
    p, grad = probs[h][block], gs[h][rows, :]
    loss = ds[h][rows, :] * float(2**h)
    if h == 0:
        loss = jnp.concatenate([loss, loss], 1)
    dscore = p * (mm3(grad, vw[h][window, :], NT) - loss) * HEAD ** (-0.5)
    dq[h][rows, :] = mm(dscore, kw[h][window, :], NN)
    dk[h][window, :] += mm(dscore, qs[h][rows, :], TN)
    dv[h][window, :] += mm(p, grad, TN)


def spread_down(sizes, own, factor, temp):
    total = own(len(sizes) - 1)
    for h in range(len(sizes) - 2, -1, -1):
        total = own(h) + doubled(temp, total * factor)
    return total


def level_scratch(sizes, extra=0):
    return [pltpu.VMEM((size + extra, HEAD), F32) for size in sizes]


def attend_scratch(sizes):
    per_level = lambda extra=0: level_scratch(sizes, extra)
    return dict(
        qs=per_level(),
        kw=per_level(BLOCK),
        vw=per_level(BLOCK),
        probs=[
            pltpu.VMEM((size // BLOCK, BLOCK, span(h)), F32) for h, size in enumerate(sizes)
        ],
        tops=per_level(),
        nums=per_level(),
        dens=per_level(),
        keeps=per_level(),
        gains=per_level(),
        gs=per_level(),
        ds=per_level(),
        dq=per_level(),
        dk=per_level(BLOCK),
        dv=per_level(BLOCK),
        temp=[pltpu.VMEM((sizes[0], HEAD), F32)] * 3,
    )
MESH = pl.DeviceIdType.MESH
PIECES = 2


def at(index, size):
    return pl.ds(pl.multiple_of(index * size, size), size)


def layer_kernel(
    sizes, scale, n_dp, n_tp,
    length, tok, wq, wk, wv, w_out, grad_out,
    tokens_out, query_out, key_out, value_out, wout_out,
    *, qs, kw, vw, probs, tops, nums, dens, keeps, gains, gs, ds, dq, dk, dv, temp,
    tails_s, tails_r, back_s, back_r, part_s, lines, acc, line_send, line_recv, groups, send_sem, recv_sem,
):
    rows, width = tok.shape
    levels = len(sizes)
    dp, me, tp = lax.axis_index("dp"), lax.axis_index("ctx"), lax.axis_index("tp")
    other = 1 - me
    has_prior = me > 0
    barrier = pltpu.get_barrier_semaphore()
    dp_peers = [lax.rem(dp + o, n_dp) for o in range(1, n_dp)]
    tp_peers = [lax.rem(tp + o, n_tp) for o in range(1, n_tp)]
    everyone = [{"ctx": other}] + [{"dp": p} for p in dp_peers] + [{"tp": p} for p in tp_peers]
    for device in everyone:
        pl.semaphore_signal(barrier, inc=1, device_id=device, device_id_type=MESH)
    started = []
    share = rows // n_tp
    flows = ((0, tp, tp + 1), (1, n_tp - 1 - tp, tp - 1))

    def line_copy(flow, source, slot, piece, onto):
        return pltpu.make_async_remote_copy(
            src_ref=source, dst_ref=lines[2 * flow].at[slot, piece],
            send_sem=line_send.at[flow, slot, piece], recv_sem=line_recv.at[flow, slot, piece],
            device_id={"tp": onto}, device_id_type=MESH,
        )

    def line_piece(flow, slot, piece):
        mine = slot if flow else n_tp - 1 - slot
        return at(mine * PIECES + piece, share // PIECES)

    def line_start():
        for slot in range(n_tp - 1):
            for piece in range(PIECES):
                for flow, place, onto in flows:

                    @pl.when(place == 0)
                    def _():
                        own = part_s.at[line_piece(flow, slot, piece), :]
                        line_copy(flow, own, slot, piece, onto).start()

    def line_step(step):
        for piece in range(PIECES):
            for flow, place, onto in flows:
                slot = step - place
                arrived, summed = lines[2 * flow], lines[2 * flow + 1]

                @pl.when((slot >= 0) & (place > 0))
                def _():
                    line_copy(flow, arrived.at[slot, piece], slot, piece, onto).wait_recv()
                    if step < n_tp - 1:
                        own = part_s[line_piece(flow, slot, piece), :].astype(F32)
                        summed[slot, piece] = (own + arrived[slot, piece].astype(F32)).astype(BF16)
                        line_copy(flow, summed.at[slot, piece], slot, piece, onto).start()
                    else:
                        acc[at(piece, share // PIECES), :] += arrived[slot, piece].astype(F32)

    def line_end():
        for step in range(n_tp - 1):
            for piece in range(PIECES):
                for flow, place, onto in flows:
                    slot = step - place

                    @pl.when(slot >= 0)
                    def _():
                        source = lines[2 * flow + 1].at[slot, piece]
                        line_copy(flow, source, slot, piece, onto).wait_send()

    def send(src, dst, **device):
        slot = len(started)
        copy = pltpu.make_async_remote_copy(
            src_ref=src, dst_ref=dst, send_sem=send_sem.at[slot], recv_sem=recv_sem.at[slot],
            device_id=device, device_id_type=MESH,
        )
        copy.start()
        started.append(copy)
        return copy

    def swap_cores(group, full):
        group["full"][...] = full
        half = group["full"].shape[0] // 2
        group["s1"][...] = group["full"][at(other, half), :].astype(BF16)
        return [send(group["s1"], group["r1"], ctx=other)]

    def swap_chips(group, copies):
        half = group["full"].shape[0] // 2
        size = half // n_dp
        copies[0].wait_recv()
        total = group["full"][at(me, half), :] + group["r1"][...].astype(F32)
        group["sum"][...] = total
        group["s2"][...] = total.astype(BF16)
        return [
            send(group["s2"].at[at(p, size), :], group["r2"].at[o], dp=p)
            for o, p in enumerate(dp_peers)
        ]

    def gather_chips(group, copies):
        size = group["sum"].shape[0] // n_dp
        total = group["sum"][at(dp, size), :]
        for o, copy in enumerate(copies):
            copy.wait_recv()
            total = total + group["r2"][o].astype(F32)
        mine = at(me * n_dp + dp, size)
        group["res"][mine, :] = total.astype(BF16)
        piece = group["res"].at[mine, :]
        return [send(piece, piece, dp=p) for p in dp_peers], [send(piece, piece, ctx=other)]

    def gather_cores(group, copies):
        size = group["sum"].shape[0] // n_dp
        around, across = copies
        for o, copy in enumerate(around):
            copy.wait_recv()
            owner = lax.rem(dp + n_dp - 1 - o, n_dp)
            piece = group["res"].at[at(me * n_dp + owner, size), :]
            across.append(send(piece, piece, ctx=other))
        return across

    def gathered(group, copies):
        for copy in copies:
            copy.wait_recv()
        return group["res"][...]

    kw[0][pl.ds(BLOCK, rows), :] = jnp.dot(tok[...], wk[...], preferred_element_type=F32)
    vw[0][pl.ds(BLOCK, rows), :] = jnp.dot(tok[...], wv[...], preferred_element_type=F32)
    coarsen_keys(sizes, kw, vw)
    for h, size in enumerate(sizes):
        tails_s[h] = kw[h][pl.ds(size, BLOCK), :].astype(BF16)
        tails_s[levels + h] = vw[h][pl.ds(size, BLOCK), :].astype(BF16)
    pl.semaphore_wait(barrier, len(everyone))
    tails = send(tails_s, tails_r, ctx=other)

    qs[0][...] = jnp.dot(tok[...], wq[...], preferred_element_type=F32)
    coarsen_queries(sizes, qs)
    positions = me * rows + lax.broadcasted_iota(jnp.int32, (rows, width), 0)
    cot = jnp.where(positions < length[0] * BLOCK, grad_out[...], jnp.zeros((), BF16))
    grad_mixed = mm(cot, w_out[...], NT)
    later = [(h, b) for h, size in enumerate(sizes) for b in range(1, size // BLOCK)]
    first = [(h, 0) for h in range(levels)]
    for h, block in later:
        attend_block(h, block, has_prior, qs, kw, vw, probs, tops, nums, dens)
    tails.wait_recv()
    for h in range(levels):
        kw[h][pl.ds(0, BLOCK), :] = tails_r[h].astype(F32)
        vw[h][pl.ds(0, BLOCK), :] = tails_r[levels + h].astype(F32)
    for h, block in first:
        attend_block(h, block, has_prior, qs, kw, vw, probs, tops, nums, dens)
    attended, inverse = merge(sizes, tops, nums, dens, keeps, gains, temp)
    back_stats(sizes, attended, inverse, grad_mixed, keeps, gains, gs, ds, temp)
    for h in range(levels):
        dk[h][...] = jnp.zeros_like(dk[h])
        dv[h][...] = jnp.zeros_like(dv[h])
    for h, block in first:
        back_block(h, block, qs, kw, vw, probs, gs, ds, dq, dk, dv)
        back_s[h] = dk[h][pl.ds(0, BLOCK), :].astype(BF16)
        back_s[levels + h] = dv[h][pl.ds(0, BLOCK), :].astype(BF16)
    back = send(back_s, back_r, ctx=other)
    out_copies = swap_cores(groups[0], mm(attended, cot, TN) * scale)
    for h, block in later:
        back_block(h, block, qs, kw, vw, probs, gs, ds, dq, dk, dv)
    rq = spread_down(sizes, lambda h: dq[h][...], 0.5, temp[0]).astype(BF16)
    query_copies = swap_cores(groups[1], mm(tok[...], rq, TN) * scale)
    out_copies = swap_chips(groups[0], out_copies)
    back.wait_recv()
    for h, size in enumerate(sizes):
        dk[h][pl.ds(size, BLOCK), :] += back_r[h].astype(F32)
        dv[h][pl.ds(size, BLOCK), :] += back_r[levels + h].astype(F32)
    own = lambda d: lambda h: d[h][pl.ds(BLOCK, sizes[h]), :]
    rk = spread_down(sizes, own(dk), 0.5, temp[0]).astype(BF16)
    rv = spread_down(sizes, own(dv), 1.0, temp[1]).astype(BF16)
    part_s[...] = (mm(rq, wq[...], NT) + mm(rk, wk[...], NT) + mm(rv, wv[...], NT)).astype(BF16)
    acc[...] = part_s[at(tp, share), :].astype(F32)
    line_start()
    both_copies = swap_cores(
        groups[2], mm(tok[...], jnp.concatenate([rk, rv], 1), TN) * scale
    )
    query_copies = swap_chips(groups[1], query_copies)
    both_copies = swap_chips(groups[2], both_copies)
    out_copies = gather_chips(groups[0], out_copies)
    for step in range(1, n_tp - 2):
        line_step(step)
    query_copies = gather_chips(groups[1], query_copies)
    both_copies = gather_chips(groups[2], both_copies)
    if n_tp > 2:
        line_step(n_tp - 2)
    out_copies = gather_cores(groups[0], out_copies)
    query_copies = gather_cores(groups[1], query_copies)
    both_copies = gather_cores(groups[2], both_copies)
    wout_out[...] = gathered(groups[0], out_copies).astype(F32)
    query_out[...] = gathered(groups[1], query_copies).astype(F32)
    both = gathered(groups[2], both_copies).astype(F32)
    key_out[...] = both[:, :HEAD]
    value_out[...] = both[:, HEAD:]
    if n_tp > 1:
        line_step(n_tp - 1)
    tokens_out[...] = acc[...].astype(BF16)
    for copy in started:
        copy.wait_send()
    line_end()


def store_kernel(*refs):
    sem = refs[-1]
    copies = [pltpu.make_async_copy(refs[i], refs[5 + i], sem.at[i]) for i in range(5)]
    for copy in copies:
        copy.start()
    for copy in copies:
        copy.wait()


def fast(tokens, lengths, w_query, w_key, w_value, w_out, grad_out):
    rows, width = tokens.shape[1:]
    n_dp, n_tp = lax.axis_size("dp"), lax.axis_size("tp")
    total = rows * lax.axis_size("ctx")
    sizes = level_sizes(rows, total)
    levels = len(sizes)
    scale = float(n_dp * total) ** (-0.5)
    tail = pltpu.VMEM((2 * levels, BLOCK, HEAD), BF16)

    def group(count, columns):
        half = count // 2
        return dict(
            full=pltpu.VMEM((count, columns), F32),
            s1=pltpu.VMEM((half, columns), BF16),
            r1=pltpu.VMEM((half, columns), BF16),
            sum=pltpu.VMEM((half, columns), F32),
            s2=pltpu.VMEM((half, columns), BF16),
            r2=pltpu.VMEM((n_dp - 1, half // n_dp, columns), BF16),
            res=pltpu.VMEM((count, columns), BF16),
        )

    copies = 2 + 3 * (1 + 3 * (n_dp - 1) + 1)
    vm = pl.BlockSpec(memory_space=pltpu.VMEM)
    hbm = pl.BlockSpec(memory_space=pl.ANY)
    shapes = [((rows // n_tp, width), BF16)] + [((width, HEAD), F32)] * 3 + [((HEAD, width), F32)]
    summed = pl.pallas_call(
        partial(layer_kernel, sizes, scale, n_dp, n_tp),
        out_shape=tuple(pltpu.VMEM(*s) for s in shapes),
        in_specs=[pl.BlockSpec(memory_space=pltpu.SMEM)] + [vm] * 6,
        out_specs=[vm] * 5,
        scratch_shapes=dict(
            attend_scratch(sizes),
            tails_s=tail,
            tails_r=tail,
            back_s=tail,
            back_r=tail,
            part_s=pltpu.VMEM((rows, width), BF16),
            lines=[pltpu.VMEM((n_tp, PIECES, rows // n_tp // PIECES, width), BF16)] * 4,
            acc=pltpu.VMEM((rows // n_tp, width), F32),
            line_send=pltpu.SemaphoreType.DMA((2, n_tp, PIECES)),
            line_recv=pltpu.SemaphoreType.DMA((2, n_tp, PIECES)),
            groups=[group(HEAD, width), group(width, HEAD), group(width, 2 * HEAD)],
            send_sem=pltpu.SemaphoreType.DMA((copies,)),
            recv_sem=pltpu.SemaphoreType.DMA((copies,)),
        ),
        compiler_params=pltpu.CompilerParams(
            vmem_limit_bytes=58 * 2**20, collective_id=0, has_side_effects=True
        ),
    )(lengths, tokens[0], w_query, w_key, w_value, w_out, grad_out[0])
    grad_tokens, grad_query, grad_key, grad_value, grad_w_out = pl.pallas_call(
        store_kernel,
        out_shape=tuple(jax.ShapeDtypeStruct(*s) for s in shapes),
        in_specs=[hbm] * 5,
        out_specs=[hbm] * 5,
        scratch_shapes=[pltpu.SemaphoreType.DMA((5,))],
        compiler_params=pltpu.CompilerParams(vmem_limit_bytes=2 * 2**20),
    )(*summed)
    return (grad_tokens[None], grad_query, grad_key, grad_value, grad_w_out)


def body(*args):
    rows = args[0].shape[1]
    sizes = level_sizes(rows, rows * lax.axis_size("ctx"))
    if sizes[-1] < BLOCK or sizes[0] % BLOCK or lax.axis_size("ctx") != 2:
        return local(*args)
    return fast(*args)

def solution(mesh):
    placed = (
        P("dp", "ctx", None),
        P("dp"),
        P(None, "tp"),
        P(None, "tp"),
        P(None, "tp"),
        P("tp", None),
        P("dp", "ctx", None),
    )
    return jax.shard_map(
        body,
        mesh=mesh,
        in_specs=placed,
        out_specs=(
            P("dp", ("ctx", "tp"), None),
            P(None, "tp"),
            P(None, "tp"),
            P(None, "tp"),
            P("tp", None),
        ),
        check_vma=False,
    )
```

```python
from functools import partial

import jax
import jax.numpy as jnp
from jax import lax
from jax.experimental import pallas as pl
from jax.experimental.pallas import tpu as pltpu
from jax.sharding import PartitionSpec as P

HEAD = 128
BLOCK = 128
LEVELS = 8


precise = lax.Precision.HIGHEST
very_low = -1e30


def passed_along(value, axis, steps):
    count = lax.axis_size(axis)
    first, last = (max(0, -steps), min(count, count - steps))
    return lax.ppermute(value, axis, [(source, source + steps) for source in range(first, last)])


def level_stats(queries, key_rows, values, query_pos, key_pos, height, block, weight):
    scores = jnp.einsum("nqe,nke->nqk", queries, key_rows, precision=precise) * queries.shape[
        -1
    ] ** (-0.5)
    query_at = query_pos[:, :, None]
    key_at = key_pos[:, None, :]
    allowed = (query_at // block - key_at // block <= 1) & (key_at >= 0)
    if height == 0:
        allowed = allowed & (key_at <= query_at)
    else:
        half_block = block // 2
        allowed = allowed & (query_at // half_block - key_at // half_block >= 2)
    masked = jnp.where(allowed, scores, very_low)
    row_max = jnp.max(masked, axis=-1)
    exp_scores = jnp.where(allowed, jnp.exp(masked - row_max[..., None]), 0.0)
    weighted = jnp.einsum("nqk,nke->nqe", exp_scores, values, precision=precise)
    totals = jnp.sum(exp_scores, axis=-1) * weight
    return (row_max, weighted, totals)


def head_stats(queries, key_rows, values, query_pos, key_pos, height, block, weight):
    single = partial(level_stats, height=height, block=block, weight=weight)
    return jax.vmap(single, in_axes=(0, 0, 0, None, None))(
        queries, key_rows, values, query_pos, key_pos
    )


def coarse(field_data, group_size, summed):
    grouped = field_data.reshape(
        field_data.shape[:-2]
        + (field_data.shape[-2] // group_size, group_size, field_data.shape[-1])
    )
    if summed:
        return jnp.sum(grouped, axis=-2)
    return jnp.mean(grouped, axis=-2)


def merge_levels(stats_list):
    best_max, running, mass_sum = stats_list[0]
    for row_max, weighted, totals in stats_list[1:]:
        new_best = jnp.maximum(best_max, row_max)
        keep_old = jnp.exp(best_max - new_best)
        gain_new = jnp.exp(row_max - new_best)
        running = running * keep_old[..., None] + weighted * gain_new[..., None]
        mass_sum = mass_sum * keep_old + totals * gain_new
        best_max = new_best
    return running / mass_sum[..., None]


def earlier(payload, distance):
    return passed_along(payload.astype(jnp.bfloat16), "ctx", distance).astype(payload.dtype)


def returned(payload, distance):
    return passed_along(payload.astype(jnp.bfloat16), "ctx", -distance).astype(payload.dtype)


def local(tokens, lengths, w_query, w_key, w_value, w_out, grad_out):
    devices = lax.axis_size("ctx")
    ctx_index = lax.axis_index("ctx")
    local_rows = tokens.shape[1]
    token_total = lax.axis_size("dp") * devices * local_rows
    grad_scale = float(token_total) ** (-0.5)
    flat_tokens = tokens[0]
    head_count = w_query.shape[1] // HEAD

    def split_heads(matrix):
        return matrix.reshape(local_rows, head_count, HEAD).transpose(1, 0, 2)

    def join_heads(field_data):
        return field_data.transpose(1, 0, 2).reshape(local_rows, head_count * HEAD)

    queries = split_heads(jnp.dot(flat_tokens, w_query, preferred_element_type=jnp.float32))
    key_rows = split_heads(jnp.dot(flat_tokens, w_key, preferred_element_type=jnp.float32))
    values = split_heads(jnp.dot(flat_tokens, w_value, preferred_element_type=jnp.float32))
    group_sizes = [2**height for height in range(LEVELS)]
    fine_levels = [height for height in range(LEVELS) if local_rows // group_sizes[height] >= BLOCK]
    rough_levels = [height for height in range(LEVELS) if local_rows // group_sizes[height] < BLOCK]

    def coarsen(all_queries, all_keys, all_values):
        return (
            [coarse(all_queries, group_sizes[height], False) for height in range(LEVELS)],
            [coarse(all_keys, group_sizes[height], False) for height in range(LEVELS)],
            [coarse(all_values, group_sizes[height], True) for height in range(LEVELS)],
        )

    (coarse_query, coarse_key, coarse_value), coarse_pull = jax.vjp(
        coarsen, queries, key_rows, values
    )
    tail_rows = jnp.stack(
        [
            jnp.concatenate([coarse_key[height][:, -BLOCK:] for height in fine_levels], 1),
            jnp.concatenate([coarse_value[height][:, -BLOCK:] for height in fine_levels], 1),
        ],
        0,
    )
    coarse_pack = jnp.stack(
        [
            jnp.concatenate([coarse_key[height] for height in rough_levels], 1),
            jnp.concatenate([coarse_value[height] for height in rough_levels], 1),
        ],
        0,
    )
    tail_count = tail_rows.shape[2]
    reach_devs = 2 * BLOCK // (local_rows // group_sizes[rough_levels[-1]])
    step_count = reach_devs.bit_length() - 1
    first_move = earlier(jnp.concatenate([tail_rows, coarse_pack], 2), 1)
    prior_tails = first_move[:, :, :tail_count]
    window = jnp.stack([first_move[:, :, tail_count:], coarse_pack], 0)
    for bit_pos in range(1, step_count):
        distance = 2**bit_pos
        if distance < devices:
            moved_rows = earlier(window, distance)
        else:
            moved_rows = jnp.zeros_like(window)
        window = jnp.concatenate([moved_rows, window], 0)
    prior_in = window[:-1]

    def attend_local(query_list, key_list, value_list, tails_in, rows_in):
        stats_list = []
        tail_at = 0
        rough_at = 0
        for height in range(LEVELS):
            group_size = group_sizes[height]
            coarse_rows = local_rows // group_size
            own_pos = ctx_index * coarse_rows + jnp.arange(coarse_rows, dtype=jnp.int32)
            if height in fine_levels:
                blocks = coarse_rows // BLOCK
                query_blocks = query_list[height].reshape(head_count, blocks, BLOCK, -1)
                key_blocks = key_list[height].reshape(head_count, blocks, BLOCK, -1)
                value_blocks = value_list[height].reshape(head_count, blocks, BLOCK, -1)
                prev_keys = tails_in[0][:, tail_at : tail_at + BLOCK][:, None]
                prev_values = tails_in[1][:, tail_at : tail_at + BLOCK][:, None]
                key_win = jnp.concatenate(
                    [jnp.concatenate([prev_keys, key_blocks[:, :-1]], 1), key_blocks], 2
                )
                value_win = jnp.concatenate(
                    [jnp.concatenate([prev_values, value_blocks[:, :-1]], 1), value_blocks], 2
                )
                query_pos = own_pos.reshape(blocks, BLOCK)
                key_pos = jnp.concatenate([query_pos - BLOCK, query_pos], 1)
                tail_at += BLOCK
            else:
                query_blocks = query_list[height][:, None]
                query_pos = own_pos[None]
                need_devs = 2 * BLOCK // coarse_rows
                earlier_keys = rows_in[
                    rows_in.shape[0] - (need_devs - 1) :, 0, :, rough_at : rough_at + coarse_rows
                ]
                earlier_values = rows_in[
                    rows_in.shape[0] - (need_devs - 1) :, 1, :, rough_at : rough_at + coarse_rows
                ]
                key_win = jnp.concatenate(
                    [
                        earlier_keys.transpose(1, 0, 2, 3).reshape(
                            head_count, (need_devs - 1) * coarse_rows, -1
                        ),
                        key_list[height],
                    ],
                    1,
                )[:, None]
                value_win = jnp.concatenate(
                    [
                        earlier_values.transpose(1, 0, 2, 3).reshape(
                            head_count, (need_devs - 1) * coarse_rows, -1
                        ),
                        value_list[height],
                    ],
                    1,
                )[:, None]
                key_pos = (
                    (ctx_index + 1) * coarse_rows
                    - need_devs * coarse_rows
                    + jnp.arange(need_devs * coarse_rows, dtype=jnp.int32)
                )[None]
                rough_at += coarse_rows
            row_max, weighted, totals = head_stats(
                query_blocks,
                key_win,
                value_win,
                query_pos,
                key_pos,
                height,
                BLOCK,
                float(group_size),
            )
            stats_list.append(
                (
                    jnp.repeat(row_max.reshape(head_count, coarse_rows), group_size, 1),
                    jnp.repeat(weighted.reshape(head_count, coarse_rows, -1), group_size, 1),
                    jnp.repeat(totals.reshape(head_count, coarse_rows), group_size, 1),
                )
            )
        return merge_levels(stats_list)

    attended, attend_pull = jax.vjp(
        attend_local, coarse_query, coarse_key, coarse_value, prior_tails, prior_in
    )
    mixed_heads = join_heads(attended).astype(jnp.bfloat16)
    positions = ctx_index * local_rows + jnp.arange(local_rows, dtype=jnp.int32)
    valid_rows = positions < lengths[0] * BLOCK
    cotangent = jnp.where(valid_rows[:, None], grad_out[0], jnp.zeros_like(grad_out[0]))
    grad_mixed = jnp.dot(cotangent, w_out.T, preferred_element_type=jnp.float32)
    grad_cquery, grad_ckey, grad_cvalue, grad_tails, grad_prior = attend_pull(
        split_heads(grad_mixed)
    )
    grad_cquery = list(grad_cquery)
    grad_ckey = list(grad_ckey)
    grad_cvalue = list(grad_cvalue)
    gradient = jnp.concatenate([grad_prior, jnp.zeros_like(coarse_pack)[None]], 0)
    for bit_pos in range(step_count - 1, 0, -1):
        distance = 2**bit_pos
        upper_part = gradient[distance:]
        if distance < devices:
            upper_part = upper_part + returned(gradient[:distance], distance)
        gradient = upper_part
    sent_back = returned(jnp.concatenate([grad_tails, gradient[0]], 2), 1)
    tails_back = sent_back[:, :, :tail_count]
    pack_back = sent_back[:, :, tail_count:] + gradient[1]
    tail_at = 0
    for height in fine_levels:
        grad_ckey[height] = (
            grad_ckey[height].at[:, -BLOCK:].add(tails_back[0, :, tail_at : tail_at + BLOCK])
        )
        grad_cvalue[height] = (
            grad_cvalue[height].at[:, -BLOCK:].add(tails_back[1, :, tail_at : tail_at + BLOCK])
        )
        tail_at += BLOCK
    rough_at = 0
    for height in rough_levels:
        coarse_rows = local_rows // group_sizes[height]
        grad_ckey[height] = grad_ckey[height] + pack_back[0, :, rough_at : rough_at + coarse_rows]
        grad_cvalue[height] = (
            grad_cvalue[height] + pack_back[1, :, rough_at : rough_at + coarse_rows]
        )
        rough_at += coarse_rows
    grad_q, grad_k, grad_v = coarse_pull((grad_cquery, grad_ckey, grad_cvalue))
    rounded_q = join_heads(grad_q).astype(jnp.bfloat16)
    rounded_k = join_heads(grad_k).astype(jnp.bfloat16)
    rounded_v = join_heads(grad_v).astype(jnp.bfloat16)
    partial_term = (
        jnp.dot(rounded_q, w_query.T, preferred_element_type=jnp.float32)
        + jnp.dot(rounded_k, w_key.T, preferred_element_type=jnp.float32)
        + jnp.dot(rounded_v, w_value.T, preferred_element_type=jnp.float32)
    )
    grad_tokens = lax.psum_scatter(
        partial_term.astype(jnp.bfloat16), "tp", scatter_dimension=0, tiled=True
    )[None]
    stacked_in = jnp.concatenate([rounded_q, rounded_k, rounded_v], 1)
    grads_in = jnp.einsum("rc,rh->ch", flat_tokens, stacked_in, preferred_element_type=jnp.float32)
    grads_out = jnp.einsum("rc,rh->ch", cotangent, mixed_heads, preferred_element_type=jnp.float32)
    summed = lax.psum(jnp.concatenate([grads_in, grads_out], 1) * grad_scale, ("dp", "ctx"))
    head_cols = head_count * HEAD
    grad_query = summed[:, :head_cols]
    grad_key = summed[:, head_cols : 2 * head_cols]
    grad_value = summed[:, 2 * head_cols : 3 * head_cols]
    grad_w_out = summed[:, 3 * head_cols :].T
    return (grad_tokens, grad_query, grad_key, grad_value, grad_w_out)


F32 = jnp.float32
BF16 = jnp.bfloat16
NT = (((1,), (1,)), ((), ()))
NN = (((1,), (0,)), ((), ()))
TN = (((0,), (0,)), ((), ()))


def mm(a, b, dims):
    return lax.dot_general(a.astype(BF16), b.astype(BF16), dims, preferred_element_type=F32)


def mm3(a, b, dims):
    a_hi, b_hi = a.astype(BF16), b.astype(BF16)
    a_lo = (a - a_hi.astype(F32)).astype(BF16)
    b_lo = (b - b_hi.astype(F32)).astype(BF16)
    dot = partial(lax.dot_general, dimension_numbers=dims, preferred_element_type=F32)
    return dot(a_hi, b_hi) + (dot(a_hi, b_lo) + dot(a_lo, b_hi))


def pairs(ref, start, count):
    return ref[pl.ds(start, count, stride=2), :], ref[pl.ds(start + 1, count, stride=2), :]


def doubled(ref, value):
    count = value.shape[0]
    ref[pl.ds(0, count, stride=2), :] = value
    ref[pl.ds(1, count, stride=2), :] = value
    return ref[pl.ds(0, 2 * count), :]


def halved(ref, value):
    count = value.shape[0]
    ref[pl.ds(0, count), :] = value
    first, second = pairs(ref, 0, count // 2)
    return first + second


def level_sizes(rows, total):
    return [rows >> h for h in range(LEVELS) if h == 0 or (total >> h) > BLOCK]


def coarsen_keys(sizes, kw, vw):
    for h in range(1, len(sizes)):
        first, second = pairs(kw[h - 1], BLOCK, sizes[h])
        kw[h][pl.ds(BLOCK, sizes[h]), :] = (first + second) * 0.5
        first, second = pairs(vw[h - 1], BLOCK, sizes[h])
        vw[h][pl.ds(BLOCK, sizes[h]), :] = first + second


def coarsen_queries(sizes, qs):
    for h in range(1, len(sizes)):
        first, second = pairs(qs[h - 1], 0, sizes[h])
        qs[h][...] = (first + second) * 0.5


def span(h):
    return 2 * BLOCK if h == 0 else BLOCK


def block_mask(h, block, has_prior):
    row = lax.broadcasted_iota(jnp.int32, (BLOCK, span(h)), 0)
    col = lax.broadcasted_iota(jnp.int32, (BLOCK, span(h)), 1)
    if h == 0:
        allowed = col <= row + BLOCK
        if block == 0:
            allowed = allowed & ((col >= BLOCK) | has_prior)
    else:
        allowed = (row >= BLOCK // 2) | (col < BLOCK // 2)
        if block == 0:
            allowed = allowed & has_prior
    return allowed


def attend_block(h, block, has_prior, qs, kw, vw, probs, tops, nums, dens):
    rows = pl.ds(block * BLOCK, BLOCK)
    window = pl.ds(block * BLOCK, span(h))
    allowed = block_mask(h, block, has_prior)
    scores = mm3(qs[h][rows, :] * HEAD ** (-0.5), kw[h][window, :], NT)
    masked = jnp.where(allowed, scores, very_low)
    top = jnp.max(masked, axis=-1, keepdims=True)
    p = jnp.where(allowed, jnp.exp(masked - top), 0.0)
    probs[h][block] = p
    tops[h][rows, :] = jnp.broadcast_to(top, (BLOCK, HEAD))
    nums[h][rows, :] = mm3(p, vw[h][window, :], NN)
    dens[h][rows, :] = jnp.broadcast_to(
        jnp.sum(p, axis=-1, keepdims=True) * float(2**h), (BLOCK, HEAD)
    )


def merge(sizes, tops, nums, dens, keeps, gains, temp):
    last = len(sizes) - 1
    top, num, den = tops[last][...], nums[last][...], dens[last][...]
    keeps[last][...] = jnp.ones_like(top)
    for h in range(last - 1, -1, -1):
        top, num, den = (doubled(t, x) for t, x in zip(temp, (top, num, den)))
        own = tops[h][...]
        best = jnp.maximum(own, top)
        keep, gain = jnp.exp(own - best), jnp.exp(top - best)
        keeps[h][...] = keep
        gains[h][...] = gain
        num = nums[h][...] * keep + num * gain
        den = dens[h][...] * keep + den * gain
        top = best
    inverse = 1.0 / den
    return num * inverse, inverse


def back_stats(sizes, attended, inverse, grad_mixed, keeps, gains, gs, ds, temp):
    delta = jnp.sum(attended * grad_mixed, axis=-1, keepdims=True)
    flow, part = grad_mixed * inverse, delta * inverse
    for h in range(len(sizes)):
        gs[h][...] = flow * keeps[h][...]
        ds[h][...] = part * keeps[h][...]
        if h + 1 < len(sizes):
            flow = halved(temp[0], flow * gains[h][...])
            part = halved(temp[1], part * gains[h][...])


def back_block(h, block, qs, kw, vw, probs, gs, ds, dq, dk, dv):
    rows = pl.ds(block * BLOCK, BLOCK)
    window = pl.ds(block * BLOCK, span(h))
    p, grad = probs[h][block], gs[h][rows, :]
    loss = ds[h][rows, :] * float(2**h)
    if h == 0:
        loss = jnp.concatenate([loss, loss], 1)
    dscore = p * (mm3(grad, vw[h][window, :], NT) - loss) * HEAD ** (-0.5)
    dq[h][rows, :] = mm(dscore, kw[h][window, :], NN)
    dk[h][window, :] += mm(dscore, qs[h][rows, :], TN)
    dv[h][window, :] += mm(p, grad, TN)


def spread_down(sizes, own, factor, temp):
    total = own(len(sizes) - 1)
    for h in range(len(sizes) - 2, -1, -1):
        total = own(h) + doubled(temp, total * factor)
    return total


def level_scratch(sizes, extra=0):
    return [pltpu.VMEM((size + extra, HEAD), F32) for size in sizes]


def attend_scratch(sizes):
    per_level = lambda extra=0: level_scratch(sizes, extra)
    return dict(
        qs=per_level(),
        kw=per_level(BLOCK),
        vw=per_level(BLOCK),
        probs=[
            pltpu.VMEM((size // BLOCK, BLOCK, span(h)), F32) for h, size in enumerate(sizes)
        ],
        tops=per_level(),
        nums=per_level(),
        dens=per_level(),
        keeps=per_level(),
        gains=per_level(),
        gs=per_level(),
        ds=per_level(),
        dq=per_level(),
        dk=per_level(BLOCK),
        dv=per_level(BLOCK),
        temp=[pltpu.VMEM((sizes[0], HEAD), F32)] * 3,
    )
MESH = pl.DeviceIdType.MESH
PIECES = 4
TOKEN_LOADS = 2
PART_CHUNKS = 2
GRAD_GROUPS = 2
ORDER = (4, 2, 2, 3)


def at(index, size):
    return pl.ds(pl.multiple_of(index * size, size), size)


def layer_kernel(
    sizes, scale, n_dp, n_tp,
    length, tok_h, wq_h, wk_h, wv_h, wo_h, grad_h,
    tokens_out, query_out, key_out, value_out, wout_out,
    *, tok, tok_t, weights, w_out, cot, r_s, load_sem, qs, kw, vw, probs, tops, nums, dens, keeps, gains, gs, ds, dq, dk, dv, temp,
    tails_s, tails_r, back_s, back_r, part_s, lines, acc, line_send, line_recv, groups, send_sem, recv_sem,
):
    rows, width = tok.shape
    levels = len(sizes)
    dp, me, tp = lax.axis_index("dp"), lax.axis_index("ctx"), lax.axis_index("tp")
    other = 1 - me
    has_prior = me > 0
    barrier = pltpu.get_barrier_semaphore()
    dp_peers = [lax.rem(dp + o, n_dp) for o in range(1, n_dp)]
    tp_peers = [lax.rem(tp + o, n_tp) for o in range(1, n_tp)]
    everyone = [{"ctx": other}] + [{"dp": p} for p in dp_peers] + [{"tp": p} for p in tp_peers]
    for device in everyone:
        pl.semaphore_signal(barrier, inc=1, device_id=device, device_id_type=MESH)
    chunk = rows // TOKEN_LOADS
    column = lambda o: weights.at[:, pl.ds(o * HEAD, HEAD)]
    moves = [(wk_h, column(1)), (wv_h, column(2))]
    for part in range(TOKEN_LOADS):
        here = pl.ds(part * chunk, chunk)
        moves.append((tok_h.at[here, :], tok.at[here, :]))
    moves += [(wq_h, column(0)), (grad_h, cot), (wo_h, w_out)]
    loads = [
        pltpu.make_async_copy(source, target, load_sem.at[o])
        for o, (source, target) in enumerate(moves)
    ]
    for load in loads:
        load.start()
    started = []
    share = rows // n_tp
    flows = ((0, tp, tp + 1), (1, n_tp - 1 - tp, tp - 1))

    def line_copy(flow, source, slot, piece, onto):
        return pltpu.make_async_remote_copy(
            src_ref=source, dst_ref=lines[2 * flow].at[slot, piece],
            send_sem=line_send.at[flow, slot, piece], recv_sem=line_recv.at[flow, slot, piece],
            device_id={"tp": onto}, device_id_type=MESH,
        )

    def line_piece(flow, slot, piece):
        mine = slot if flow else n_tp - 1 - slot
        return at(mine * PIECES + piece, share // PIECES)

    def line_start(slot):
        for piece in range(PIECES):
            for flow, place, onto in flows:

                @pl.when(place == 0)
                def _():
                    own = part_s.at[line_piece(flow, slot, piece), :]
                    line_copy(flow, own, slot, piece, onto).start()

    def line_step(step, pieces=range(PIECES)):
        for piece in pieces:
            for flow, place, onto in flows:
                slot = step - place
                arrived, summed = lines[2 * flow], lines[2 * flow + 1]

                @pl.when((slot >= 0) & (place > 0))
                def _():
                    line_copy(flow, arrived.at[slot, piece], slot, piece, onto).wait_recv()
                    if step < n_tp - 1:
                        own = part_s[line_piece(flow, slot, piece), :].astype(F32)
                        summed[slot, piece] = (own + arrived[slot, piece].astype(F32)).astype(BF16)
                        line_copy(flow, summed.at[slot, piece], slot, piece, onto).start()
                    else:
                        acc[at(piece, share // PIECES), :] += arrived[slot, piece].astype(F32)

    def line_end():
        for step in range(n_tp - 1):
            for piece in range(PIECES):
                for flow, place, onto in flows:
                    slot = step - place

                    @pl.when(slot >= 0)
                    def _():
                        source = lines[2 * flow + 1].at[slot, piece]
                        line_copy(flow, source, slot, piece, onto).wait_send()

    def send(src, dst, **device):
        slot = len(started)
        copy = pltpu.make_async_remote_copy(
            src_ref=src, dst_ref=dst, send_sem=send_sem.at[slot], recv_sem=recv_sem.at[slot],
            device_id=device, device_id_type=MESH,
        )
        copy.start()
        started.append(copy)
        return copy

    def swap_cores(group, full):
        group["full"][...] = full
        half = group["full"].shape[0] // 2
        group["s1"][...] = group["full"][at(other, half), :].astype(BF16)
        return [send(group["s1"], group["r1"], ctx=other)]

    def swap_chips(group, copies):
        half = group["full"].shape[0] // 2
        size = half // n_dp
        copies[0].wait_recv()
        total = group["full"][at(me, half), :] + group["r1"][...].astype(F32)
        group["sum"][...] = total
        group["s2"][...] = total.astype(BF16)
        return [
            send(group["s2"].at[at(p, size), :], group["r2"].at[o], dp=p)
            for o, p in enumerate(dp_peers)
        ]

    def gather_chips(group, copies):
        size = group["sum"].shape[0] // n_dp
        total = group["sum"][at(dp, size), :]
        for o, copy in enumerate(copies):
            copy.wait_recv()
            total = total + group["r2"][o].astype(F32)
        mine = at(me * n_dp + dp, size)
        group["res"][mine, :] = total.astype(BF16)
        piece = group["res"].at[mine, :]
        return [send(piece, piece, dp=p) for p in dp_peers], [send(piece, piece, ctx=other)]

    def gather_cores(group, copies):
        size = group["sum"].shape[0] // n_dp
        around, across = copies
        for o, copy in enumerate(around):
            copy.wait_recv()
            owner = lax.rem(dp + n_dp - 1 - o, n_dp)
            piece = group["res"].at[at(me * n_dp + owner, size), :]
            across.append(send(piece, piece, ctx=other))
        return across

    def gathered(group, copies):
        for copy in copies:
            copy.wait_recv()
        return group["res"][...]

    for load in loads[:2]:
        load.wait()
    for part in range(TOKEN_LOADS):
        loads[2 + part].wait()
        chunk = rows // TOKEN_LOADS
        here = pl.ds(part * chunk, chunk)
        both = jnp.dot(tok[here, :], weights[:, HEAD:], preferred_element_type=F32)
        kw[0][pl.ds(BLOCK + part * chunk, chunk), :] = both[:, :HEAD]
        vw[0][pl.ds(BLOCK + part * chunk, chunk), :] = both[:, HEAD:]
    coarsen_keys(sizes, kw, vw)
    for h, size in enumerate(sizes):
        tails_s[h] = kw[h][pl.ds(size, BLOCK), :].astype(BF16)
        tails_s[levels + h] = vw[h][pl.ds(size, BLOCK), :].astype(BF16)
    loads[-3].wait()
    qs[0][...] = jnp.dot(tok[...], weights[:, :HEAD], preferred_element_type=F32)
    coarsen_queries(sizes, qs)
    later = [(h, b) for h, size in enumerate(sizes) for b in range(1, size // BLOCK)]
    first = [(h, 0) for h in range(levels)]
    for h, block in later:
        attend_block(h, block, has_prior, qs, kw, vw, probs, tops, nums, dens)
    pl.semaphore_wait(barrier, len(everyone))
    tails = send(tails_s, tails_r, ctx=other)

    loads[-2].wait()
    loads[-1].wait()
    positions = me * rows + lax.broadcasted_iota(jnp.int32, (rows, width), 0)
    cot[...] = jnp.where(positions < length[0] * BLOCK, cot[...], jnp.zeros((), BF16))
    grad_mixed = mm(cot[...], w_out[...], NT)
    tok_t[...] = tok[...].T
    for h in range(levels):
        dk[h][...] = jnp.zeros_like(dk[h])
        dv[h][...] = jnp.zeros_like(dv[h])
        kw[h][pl.ds(0, BLOCK), :] = jnp.zeros((BLOCK, HEAD), F32)
        vw[h][pl.ds(0, BLOCK), :] = jnp.zeros((BLOCK, HEAD), F32)

    @pl.when(has_prior)
    def _():
        tails.wait_recv()
        for h in range(levels):
            kw[h][pl.ds(0, BLOCK), :] = tails_r[h].astype(F32)
            vw[h][pl.ds(0, BLOCK), :] = tails_r[levels + h].astype(F32)

    for h, block in first:
        attend_block(h, block, has_prior, qs, kw, vw, probs, tops, nums, dens)
    attended, inverse = merge(sizes, tops, nums, dens, keeps, gains, temp)
    back_stats(sizes, attended, inverse, grad_mixed, keeps, gains, gs, ds, temp)
    for h, block in first:
        back_block(h, block, qs, kw, vw, probs, gs, ds, dq, dk, dv)
        back_s[h] = dk[h][pl.ds(0, BLOCK), :].astype(BF16)
        back_s[levels + h] = dv[h][pl.ds(0, BLOCK), :].astype(BF16)
    back = send(back_s, back_r, ctx=other)
    outs = groups[0]
    out_copies = swap_cores(outs, mm(attended, cot[...], TN) * scale)
    for h, block in later:
        back_block(h, block, qs, kw, vw, probs, gs, ds, dq, dk, dv)
    out_copies = swap_chips(outs, out_copies)
    r_s[:, :HEAD] = spread_down(sizes, lambda h: dq[h][...], 0.5, temp[0]).astype(BF16)

    @pl.when(jnp.logical_not(has_prior))
    def _():
        back.wait_recv()
        for h, size in enumerate(sizes):
            dk[h][pl.ds(size, BLOCK), :] += back_r[h].astype(F32)
            dv[h][pl.ds(size, BLOCK), :] += back_r[levels + h].astype(F32)

    own = lambda d: lambda h: d[h][pl.ds(BLOCK, sizes[h]), :]
    r_s[:, HEAD : 2 * HEAD] = spread_down(sizes, own(dk), 0.5, temp[0]).astype(BF16)
    r_s[:, 2 * HEAD :] = spread_down(sizes, own(dv), 1.0, temp[1]).astype(BF16)
    chunk = rows // PART_CHUNKS
    slots = n_tp // PART_CHUNKS
    for part in range(PART_CHUNKS):
        here = at(jnp.where(2 * tp < n_tp, PART_CHUNKS - 1 - part, part), chunk)
        part_s[here, :] = mm(r_s[here, :], weights[...], NT).astype(BF16)
        for slot in range(part * slots, min((part + 1) * slots, n_tp - 1)):
            line_start(slot)
    acc[...] = part_s[at(tp, share), :].astype(F32)
    copies = []
    for o, group in enumerate(groups[1:]):
        size = group["full"].shape[0]
        copies.append(swap_cores(group, jnp.dot(
            tok_t[pl.ds(o * size, size), :], r_s[...], preferred_element_type=F32
        ) * scale))
    copies = [swap_chips(group, c) for group, c in zip(groups[1:], copies)]
    out_copies = gather_chips(outs, out_copies)
    rounds = [(step, piece) for step in range(1, n_tp) for piece in range(PIECES)]

    def advance(count):
        for step, piece in rounds[:count]:
            line_step(step, [piece])
        del rounds[:count]

    advance(len(rounds) - 3 * PIECES + ORDER[0])
    copies[0] = gather_chips(groups[1], copies[0])
    advance(ORDER[1])
    for o in range(1, GRAD_GROUPS):
        copies[o] = gather_chips(groups[1 + o], copies[o])
    out_copies = gather_cores(outs, out_copies)
    advance(ORDER[2])
    copies[0] = gather_cores(groups[1], copies[0])
    advance(ORDER[3])
    for o in range(1, GRAD_GROUPS):
        copies[o] = gather_cores(groups[1 + o], copies[o])
    wout_out[...] = gathered(outs, out_copies).astype(F32)
    for o, group in enumerate(groups[1:]):
        size = group["full"].shape[0]
        here = pl.ds(o * size, size)
        result = gathered(group, copies[o]).astype(F32)
        query_out[here, :] = result[:, :HEAD]
        key_out[here, :] = result[:, HEAD : 2 * HEAD]
        value_out[here, :] = result[:, 2 * HEAD :]
    advance(len(rounds))
    tokens_out[...] = acc[...].astype(BF16)

    @pl.when(has_prior)
    def _():
        back.wait_recv()

    @pl.when(jnp.logical_not(has_prior))
    def _():
        tails.wait_recv()

    for copy in started:
        copy.wait_send()
    line_end()


def store_kernel(*refs):
    sem = refs[-1]
    copies = [pltpu.make_async_copy(refs[i], refs[5 + i], sem.at[i]) for i in range(5)]
    for copy in copies:
        copy.start()
    for copy in copies:
        copy.wait()


def fast(tokens, lengths, w_query, w_key, w_value, w_out, grad_out):
    rows, width = tokens.shape[1:]
    n_dp, n_tp = lax.axis_size("dp"), lax.axis_size("tp")
    total = rows * lax.axis_size("ctx")
    sizes = level_sizes(rows, total)
    levels = len(sizes)
    scale = float(n_dp * total) ** (-0.5)
    tail = pltpu.VMEM((2 * levels, BLOCK, HEAD), BF16)

    def group(count, columns):
        half = count // 2
        return dict(
            full=pltpu.VMEM((count, columns), F32),
            s1=pltpu.VMEM((half, columns), BF16),
            r1=pltpu.VMEM((half, columns), BF16),
            sum=pltpu.VMEM((half, columns), F32),
            s2=pltpu.VMEM((half, columns), BF16),
            r2=pltpu.VMEM((n_dp - 1, half // n_dp, columns), BF16),
            res=pltpu.VMEM((count, columns), BF16),
        )

    copies = 2 + (1 + GRAD_GROUPS) * (1 + 3 * (n_dp - 1) + 1)
    vm = pl.BlockSpec(memory_space=pltpu.VMEM)
    hbm = pl.BlockSpec(memory_space=pl.ANY)
    shapes = [((rows // n_tp, width), BF16)] + [((width, HEAD), F32)] * 3 + [((HEAD, width), F32)]
    summed = pl.pallas_call(
        partial(layer_kernel, sizes, scale, n_dp, n_tp),
        out_shape=tuple(pltpu.VMEM(*s) for s in shapes),
        in_specs=[pl.BlockSpec(memory_space=pltpu.SMEM)] + [hbm] * 6,
        out_specs=[vm] * 5,
        scratch_shapes=dict(
            attend_scratch(sizes),
            tok=pltpu.VMEM((rows, width), BF16),
            tok_t=pltpu.VMEM((width, rows), BF16),
            weights=pltpu.VMEM((width, 3 * HEAD), BF16),
            w_out=pltpu.VMEM((HEAD, width), BF16),
            cot=pltpu.VMEM((rows, width), BF16),
            r_s=pltpu.VMEM((rows, 3 * HEAD), BF16),
            load_sem=pltpu.SemaphoreType.DMA((5 + TOKEN_LOADS,)),
            tails_s=tail,
            tails_r=tail,
            back_s=tail,
            back_r=tail,
            part_s=pltpu.VMEM((rows, width), BF16),
            lines=[pltpu.VMEM((n_tp, PIECES, rows // n_tp // PIECES, width), BF16)] * 4,
            acc=pltpu.VMEM((rows // n_tp, width), F32),
            line_send=pltpu.SemaphoreType.DMA((2, n_tp, PIECES)),
            line_recv=pltpu.SemaphoreType.DMA((2, n_tp, PIECES)),
            groups=[group(HEAD, width)] + [group(width // GRAD_GROUPS, 3 * HEAD)] * GRAD_GROUPS,
            send_sem=pltpu.SemaphoreType.DMA((copies,)),
            recv_sem=pltpu.SemaphoreType.DMA((copies,)),
        ),
        compiler_params=pltpu.CompilerParams(
            vmem_limit_bytes=58 * 2**20, collective_id=0, has_side_effects=True
        ),
    )(lengths, tokens[0], w_query, w_key, w_value, w_out, grad_out[0])
    grad_tokens, grad_query, grad_key, grad_value, grad_w_out = pl.pallas_call(
        store_kernel,
        out_shape=tuple(jax.ShapeDtypeStruct(*s) for s in shapes),
        in_specs=[hbm] * 5,
        out_specs=[hbm] * 5,
        scratch_shapes=[pltpu.SemaphoreType.DMA((5,))],
        compiler_params=pltpu.CompilerParams(vmem_limit_bytes=2 * 2**20),
    )(*summed)
    return (grad_tokens[None], grad_query, grad_key, grad_value, grad_w_out)


def body(*args):
    rows = args[0].shape[1]
    sizes = level_sizes(rows, rows * lax.axis_size("ctx"))
    if sizes[-1] < BLOCK or sizes[0] % BLOCK or lax.axis_size("ctx") != 2:
        return local(*args)
    return fast(*args)

def solution(mesh):
    placed = (
        P("dp", "ctx", None),
        P("dp"),
        P(None, "tp"),
        P(None, "tp"),
        P(None, "tp"),
        P("tp", None),
        P("dp", "ctx", None),
    )
    return jax.shard_map(
        body,
        mesh=mesh,
        in_specs=placed,
        out_specs=(
            P("dp", ("ctx", "tp"), None),
            P(None, "tp"),
            P(None, "tp"),
            P(None, "tp"),
            P("tp", None),
        ),
        check_vma=False,
    )
```

```python
from functools import partial

import jax
import jax.numpy as jnp
from jax import lax
from jax.experimental import pallas as pl
from jax.experimental.pallas import tpu as pltpu
from jax.sharding import PartitionSpec as P

HEAD = 128
BLOCK = 128
LEVELS = 8


precise = lax.Precision.HIGHEST
very_low = -1e30


def passed_along(value, axis, steps):
    count = lax.axis_size(axis)
    first, last = (max(0, -steps), min(count, count - steps))
    return lax.ppermute(value, axis, [(source, source + steps) for source in range(first, last)])


def level_stats(queries, key_rows, values, query_pos, key_pos, height, block, weight):
    scores = jnp.einsum("nqe,nke->nqk", queries, key_rows, precision=precise) * queries.shape[
        -1
    ] ** (-0.5)
    query_at = query_pos[:, :, None]
    key_at = key_pos[:, None, :]
    allowed = (query_at // block - key_at // block <= 1) & (key_at >= 0)
    if height == 0:
        allowed = allowed & (key_at <= query_at)
    else:
        half_block = block // 2
        allowed = allowed & (query_at // half_block - key_at // half_block >= 2)
    masked = jnp.where(allowed, scores, very_low)
    row_max = jnp.max(masked, axis=-1)
    exp_scores = jnp.where(allowed, jnp.exp(masked - row_max[..., None]), 0.0)
    weighted = jnp.einsum("nqk,nke->nqe", exp_scores, values, precision=precise)
    totals = jnp.sum(exp_scores, axis=-1) * weight
    return (row_max, weighted, totals)


def head_stats(queries, key_rows, values, query_pos, key_pos, height, block, weight):
    single = partial(level_stats, height=height, block=block, weight=weight)
    return jax.vmap(single, in_axes=(0, 0, 0, None, None))(
        queries, key_rows, values, query_pos, key_pos
    )


def coarse(field_data, group_size, summed):
    grouped = field_data.reshape(
        field_data.shape[:-2]
        + (field_data.shape[-2] // group_size, group_size, field_data.shape[-1])
    )
    if summed:
        return jnp.sum(grouped, axis=-2)
    return jnp.mean(grouped, axis=-2)


def merge_levels(stats_list):
    best_max, running, mass_sum = stats_list[0]
    for row_max, weighted, totals in stats_list[1:]:
        new_best = jnp.maximum(best_max, row_max)
        keep_old = jnp.exp(best_max - new_best)
        gain_new = jnp.exp(row_max - new_best)
        running = running * keep_old[..., None] + weighted * gain_new[..., None]
        mass_sum = mass_sum * keep_old + totals * gain_new
        best_max = new_best
    return running / mass_sum[..., None]


def earlier(payload, distance):
    return passed_along(payload.astype(jnp.bfloat16), "ctx", distance).astype(payload.dtype)


def returned(payload, distance):
    return passed_along(payload.astype(jnp.bfloat16), "ctx", -distance).astype(payload.dtype)


def local(tokens, lengths, w_query, w_key, w_value, w_out, grad_out):
    devices = lax.axis_size("ctx")
    ctx_index = lax.axis_index("ctx")
    local_rows = tokens.shape[1]
    token_total = lax.axis_size("dp") * devices * local_rows
    grad_scale = float(token_total) ** (-0.5)
    flat_tokens = tokens[0]
    head_count = w_query.shape[1] // HEAD

    def split_heads(matrix):
        return matrix.reshape(local_rows, head_count, HEAD).transpose(1, 0, 2)

    def join_heads(field_data):
        return field_data.transpose(1, 0, 2).reshape(local_rows, head_count * HEAD)

    queries = split_heads(jnp.dot(flat_tokens, w_query, preferred_element_type=jnp.float32))
    key_rows = split_heads(jnp.dot(flat_tokens, w_key, preferred_element_type=jnp.float32))
    values = split_heads(jnp.dot(flat_tokens, w_value, preferred_element_type=jnp.float32))
    group_sizes = [2**height for height in range(LEVELS)]
    fine_levels = [height for height in range(LEVELS) if local_rows // group_sizes[height] >= BLOCK]
    rough_levels = [height for height in range(LEVELS) if local_rows // group_sizes[height] < BLOCK]

    def coarsen(all_queries, all_keys, all_values):
        return (
            [coarse(all_queries, group_sizes[height], False) for height in range(LEVELS)],
            [coarse(all_keys, group_sizes[height], False) for height in range(LEVELS)],
            [coarse(all_values, group_sizes[height], True) for height in range(LEVELS)],
        )

    (coarse_query, coarse_key, coarse_value), coarse_pull = jax.vjp(
        coarsen, queries, key_rows, values
    )
    tail_rows = jnp.stack(
        [
            jnp.concatenate([coarse_key[height][:, -BLOCK:] for height in fine_levels], 1),
            jnp.concatenate([coarse_value[height][:, -BLOCK:] for height in fine_levels], 1),
        ],
        0,
    )
    coarse_pack = jnp.stack(
        [
            jnp.concatenate([coarse_key[height] for height in rough_levels], 1),
            jnp.concatenate([coarse_value[height] for height in rough_levels], 1),
        ],
        0,
    )
    tail_count = tail_rows.shape[2]
    reach_devs = 2 * BLOCK // (local_rows // group_sizes[rough_levels[-1]])
    step_count = reach_devs.bit_length() - 1
    first_move = earlier(jnp.concatenate([tail_rows, coarse_pack], 2), 1)
    prior_tails = first_move[:, :, :tail_count]
    window = jnp.stack([first_move[:, :, tail_count:], coarse_pack], 0)
    for bit_pos in range(1, step_count):
        distance = 2**bit_pos
        if distance < devices:
            moved_rows = earlier(window, distance)
        else:
            moved_rows = jnp.zeros_like(window)
        window = jnp.concatenate([moved_rows, window], 0)
    prior_in = window[:-1]

    def attend_local(query_list, key_list, value_list, tails_in, rows_in):
        stats_list = []
        tail_at = 0
        rough_at = 0
        for height in range(LEVELS):
            group_size = group_sizes[height]
            coarse_rows = local_rows // group_size
            own_pos = ctx_index * coarse_rows + jnp.arange(coarse_rows, dtype=jnp.int32)
            if height in fine_levels:
                blocks = coarse_rows // BLOCK
                query_blocks = query_list[height].reshape(head_count, blocks, BLOCK, -1)
                key_blocks = key_list[height].reshape(head_count, blocks, BLOCK, -1)
                value_blocks = value_list[height].reshape(head_count, blocks, BLOCK, -1)
                prev_keys = tails_in[0][:, tail_at : tail_at + BLOCK][:, None]
                prev_values = tails_in[1][:, tail_at : tail_at + BLOCK][:, None]
                key_win = jnp.concatenate(
                    [jnp.concatenate([prev_keys, key_blocks[:, :-1]], 1), key_blocks], 2
                )
                value_win = jnp.concatenate(
                    [jnp.concatenate([prev_values, value_blocks[:, :-1]], 1), value_blocks], 2
                )
                query_pos = own_pos.reshape(blocks, BLOCK)
                key_pos = jnp.concatenate([query_pos - BLOCK, query_pos], 1)
                tail_at += BLOCK
            else:
                query_blocks = query_list[height][:, None]
                query_pos = own_pos[None]
                need_devs = 2 * BLOCK // coarse_rows
                earlier_keys = rows_in[
                    rows_in.shape[0] - (need_devs - 1) :, 0, :, rough_at : rough_at + coarse_rows
                ]
                earlier_values = rows_in[
                    rows_in.shape[0] - (need_devs - 1) :, 1, :, rough_at : rough_at + coarse_rows
                ]
                key_win = jnp.concatenate(
                    [
                        earlier_keys.transpose(1, 0, 2, 3).reshape(
                            head_count, (need_devs - 1) * coarse_rows, -1
                        ),
                        key_list[height],
                    ],
                    1,
                )[:, None]
                value_win = jnp.concatenate(
                    [
                        earlier_values.transpose(1, 0, 2, 3).reshape(
                            head_count, (need_devs - 1) * coarse_rows, -1
                        ),
                        value_list[height],
                    ],
                    1,
                )[:, None]
                key_pos = (
                    (ctx_index + 1) * coarse_rows
                    - need_devs * coarse_rows
                    + jnp.arange(need_devs * coarse_rows, dtype=jnp.int32)
                )[None]
                rough_at += coarse_rows
            row_max, weighted, totals = head_stats(
                query_blocks,
                key_win,
                value_win,
                query_pos,
                key_pos,
                height,
                BLOCK,
                float(group_size),
            )
            stats_list.append(
                (
                    jnp.repeat(row_max.reshape(head_count, coarse_rows), group_size, 1),
                    jnp.repeat(weighted.reshape(head_count, coarse_rows, -1), group_size, 1),
                    jnp.repeat(totals.reshape(head_count, coarse_rows), group_size, 1),
                )
            )
        return merge_levels(stats_list)

    attended, attend_pull = jax.vjp(
        attend_local, coarse_query, coarse_key, coarse_value, prior_tails, prior_in
    )
    mixed_heads = join_heads(attended).astype(jnp.bfloat16)
    positions = ctx_index * local_rows + jnp.arange(local_rows, dtype=jnp.int32)
    valid_rows = positions < lengths[0] * BLOCK
    cotangent = jnp.where(valid_rows[:, None], grad_out[0], jnp.zeros_like(grad_out[0]))
    grad_mixed = jnp.dot(cotangent, w_out.T, preferred_element_type=jnp.float32)
    grad_cquery, grad_ckey, grad_cvalue, grad_tails, grad_prior = attend_pull(
        split_heads(grad_mixed)
    )
    grad_cquery = list(grad_cquery)
    grad_ckey = list(grad_ckey)
    grad_cvalue = list(grad_cvalue)
    gradient = jnp.concatenate([grad_prior, jnp.zeros_like(coarse_pack)[None]], 0)
    for bit_pos in range(step_count - 1, 0, -1):
        distance = 2**bit_pos
        upper_part = gradient[distance:]
        if distance < devices:
            upper_part = upper_part + returned(gradient[:distance], distance)
        gradient = upper_part
    sent_back = returned(jnp.concatenate([grad_tails, gradient[0]], 2), 1)
    tails_back = sent_back[:, :, :tail_count]
    pack_back = sent_back[:, :, tail_count:] + gradient[1]
    tail_at = 0
    for height in fine_levels:
        grad_ckey[height] = (
            grad_ckey[height].at[:, -BLOCK:].add(tails_back[0, :, tail_at : tail_at + BLOCK])
        )
        grad_cvalue[height] = (
            grad_cvalue[height].at[:, -BLOCK:].add(tails_back[1, :, tail_at : tail_at + BLOCK])
        )
        tail_at += BLOCK
    rough_at = 0
    for height in rough_levels:
        coarse_rows = local_rows // group_sizes[height]
        grad_ckey[height] = grad_ckey[height] + pack_back[0, :, rough_at : rough_at + coarse_rows]
        grad_cvalue[height] = (
            grad_cvalue[height] + pack_back[1, :, rough_at : rough_at + coarse_rows]
        )
        rough_at += coarse_rows
    grad_q, grad_k, grad_v = coarse_pull((grad_cquery, grad_ckey, grad_cvalue))
    rounded_q = join_heads(grad_q).astype(jnp.bfloat16)
    rounded_k = join_heads(grad_k).astype(jnp.bfloat16)
    rounded_v = join_heads(grad_v).astype(jnp.bfloat16)
    partial_term = (
        jnp.dot(rounded_q, w_query.T, preferred_element_type=jnp.float32)
        + jnp.dot(rounded_k, w_key.T, preferred_element_type=jnp.float32)
        + jnp.dot(rounded_v, w_value.T, preferred_element_type=jnp.float32)
    )
    grad_tokens = lax.psum_scatter(
        partial_term.astype(jnp.bfloat16), "tp", scatter_dimension=0, tiled=True
    )[None]
    stacked_in = jnp.concatenate([rounded_q, rounded_k, rounded_v], 1)
    grads_in = jnp.einsum("rc,rh->ch", flat_tokens, stacked_in, preferred_element_type=jnp.float32)
    grads_out = jnp.einsum("rc,rh->ch", cotangent, mixed_heads, preferred_element_type=jnp.float32)
    summed = lax.psum(jnp.concatenate([grads_in, grads_out], 1) * grad_scale, ("dp", "ctx"))
    head_cols = head_count * HEAD
    grad_query = summed[:, :head_cols]
    grad_key = summed[:, head_cols : 2 * head_cols]
    grad_value = summed[:, 2 * head_cols : 3 * head_cols]
    grad_w_out = summed[:, 3 * head_cols :].T
    return (grad_tokens, grad_query, grad_key, grad_value, grad_w_out)


F32 = jnp.float32
BF16 = jnp.bfloat16
NT = (((1,), (1,)), ((), ()))
NN = (((1,), (0,)), ((), ()))
TN = (((0,), (0,)), ((), ()))


def mm(a, b, dims):
    return lax.dot_general(a.astype(BF16), b.astype(BF16), dims, preferred_element_type=F32)


def split(value):
    high = value.astype(BF16)
    return high, (value - high.astype(F32)).astype(BF16)


def mm3(a, b, dims):
    dot = partial(lax.dot_general, dimension_numbers=dims, preferred_element_type=F32)
    result = dot(a[1], b[0])
    if b[1] is not None:
        result = result + dot(a[0], b[1])
    return dot(a[0], b[0]) + result


def window_of(h, block, high, low):
    window = pl.ds(block * BLOCK, span(h))
    exact = h > 0 and block == 0
    return high[h][window, :], None if exact else low[h][window, :]


def pairs(ref, start, count):
    return ref[pl.ds(start, count, stride=2), :], ref[pl.ds(start + 1, count, stride=2), :]


def doubled(ref, value):
    count = value.shape[0]
    ref[pl.ds(0, count, stride=2), :] = value
    ref[pl.ds(1, count, stride=2), :] = value
    return ref[pl.ds(0, 2 * count), :]


def halved(ref, value):
    count = value.shape[0]
    ref[pl.ds(0, count), :] = value
    first, second = pairs(ref, 0, count // 2)
    return first + second


def level_sizes(rows, total):
    return [rows >> h for h in range(LEVELS) if h == 0 or (total >> h) > BLOCK]


def coarsen_keys(sizes, kw, vw):
    for h in range(1, len(sizes)):
        first, second = pairs(kw[h - 1], BLOCK, sizes[h])
        kw[h][pl.ds(BLOCK, sizes[h]), :] = (first + second) * 0.5
        first, second = pairs(vw[h - 1], BLOCK, sizes[h])
        vw[h][pl.ds(BLOCK, sizes[h]), :] = first + second


def coarsen_queries(sizes, qs):
    for h in range(1, len(sizes)):
        first, second = pairs(qs[h - 1], 0, sizes[h])
        qs[h][...] = (first + second) * 0.5


def span(h):
    return 2 * BLOCK if h == 0 else BLOCK


def block_mask(h, block, has_prior):
    row = lax.broadcasted_iota(jnp.int32, (BLOCK, span(h)), 0)
    col = lax.broadcasted_iota(jnp.int32, (BLOCK, span(h)), 1)
    if h == 0:
        allowed = col <= row + BLOCK
        if block == 0:
            allowed = allowed & ((col >= BLOCK) | has_prior)
    else:
        allowed = (row >= BLOCK // 2) | (col < BLOCK // 2)
        if block == 0:
            allowed = allowed & has_prior
    return allowed


def attend_block(h, block, has_prior, q2, k2, v2, probs, tops, nums, dens):
    rows = pl.ds(block * BLOCK, BLOCK)
    allowed = block_mask(h, block, has_prior)
    scores = mm3((q2[0][h][rows, :], q2[1][h][rows, :]), window_of(h, block, *k2), NT)
    masked = jnp.where(allowed, scores, very_low)
    top = jnp.max(masked, axis=-1, keepdims=True)
    p = jnp.where(allowed, jnp.exp(masked - top), 0.0)
    probs[h][block] = p
    tops[h][rows, :] = jnp.broadcast_to(top, (BLOCK, HEAD))
    nums[h][rows, :] = mm3(split(p), window_of(h, block, *v2), NN)
    dens[h][rows, :] = jnp.broadcast_to(
        jnp.sum(p, axis=-1, keepdims=True) * float(2**h), (BLOCK, HEAD)
    )


def merge(sizes, tops, nums, dens, keeps, gains, temp):
    last = len(sizes) - 1
    top, num, den = tops[last][...], nums[last][...], dens[last][...]
    keeps[last][...] = jnp.ones_like(top)
    for h in range(last - 1, -1, -1):
        top, num, den = (doubled(t, x) for t, x in zip(temp, (top, num, den)))
        own = tops[h][...]
        best = jnp.maximum(own, top)
        keep, gain = jnp.exp(own - best), jnp.exp(top - best)
        keeps[h][...] = keep
        gains[h][...] = gain
        num = nums[h][...] * keep + num * gain
        den = dens[h][...] * keep + den * gain
        top = best
    inverse = 1.0 / den
    return num * inverse, inverse


def back_stats(sizes, attended, inverse, grad_mixed, keeps, gains, gs, ds, temp):
    delta = jnp.sum(attended * grad_mixed, axis=-1, keepdims=True)
    flow, part = grad_mixed * inverse, delta * inverse
    for h in range(len(sizes)):
        gs[h][...] = flow * keeps[h][...]
        ds[h][...] = part * keeps[h][...]
        if h + 1 < len(sizes):
            flow = halved(temp[0], flow * gains[h][...])
            part = halved(temp[1], part * gains[h][...])


def back_block(h, block, q2, k2, v2, probs, gs, ds, dq, dk, dv):
    rows = pl.ds(block * BLOCK, BLOCK)
    window = pl.ds(block * BLOCK, span(h))
    p, grad = probs[h][block], split(gs[h][rows, :])
    loss = ds[h][rows, :] * float(2**h)
    if h == 0:
        loss = jnp.concatenate([loss, loss], 1)
    dscore = (p * (mm3(grad, window_of(h, block, *v2), NT) - loss)).astype(BF16)
    dq[h][rows, :] = mm(dscore, k2[0][h][window, :], NN) * HEAD ** (-0.5)
    dk[h][window, :] += mm(dscore, q2[0][h][rows, :], TN)
    dv[h][window, :] += mm(p, grad[0], TN)


def spread_down(sizes, own, factor, temp):
    total = own(len(sizes) - 1)
    for h in range(len(sizes) - 2, -1, -1):
        total = own(h) + doubled(temp, total * factor)
    return total


def level_scratch(sizes, extra=0, kind=F32):
    return [pltpu.VMEM((size + extra, HEAD), kind) for size in sizes]


def attend_scratch(sizes):
    per_level = lambda extra=0: level_scratch(sizes, extra)
    return dict(
        qs=per_level(),
        kw=per_level(BLOCK),
        vw=per_level(BLOCK),
        probs=[
            pltpu.VMEM((size // BLOCK, BLOCK, span(h)), F32) for h, size in enumerate(sizes)
        ],
        tops=per_level(),
        nums=per_level(),
        dens=per_level(),
        keeps=per_level(),
        gains=per_level(),
        gs=per_level(),
        ds=per_level(),
        dq=per_level(),
        dk=per_level(BLOCK),
        dv=per_level(BLOCK),
        temp=[pltpu.VMEM((sizes[0], HEAD), F32)] * 3,
    )
MESH = pl.DeviceIdType.MESH
PIECES = 4
TOKEN_LOADS = 2
PART_CHUNKS = 2
GRAD_GROUPS = 2
ORDER = (3, 2, 2, 3)


def at(index, size):
    return pl.ds(pl.multiple_of(index * size, size), size)


def layer_kernel(
    sizes, scale, n_dp, n_tp,
    length, tok_h, wq_h, wk_h, wv_h, wo_h, grad_h,
    tokens_out, query_out, key_out, value_out, wout_out,
    *, q2, k2, v2, tok, tok_t, weights, w_out, cot, r_s, load_sem, qs, kw, vw, probs, tops, nums, dens, keeps, gains, gs, ds, dq, dk, dv, temp,
    tails_s, tails_r, back_s, back_r, part_s, lines, acc, line_send, line_recv, groups, send_sem, recv_sem,
):
    rows, width = tok.shape
    levels = len(sizes)
    dp, me, tp = lax.axis_index("dp"), lax.axis_index("ctx"), lax.axis_index("tp")
    other = 1 - me
    has_prior = me > 0
    barrier = pltpu.get_barrier_semaphore()
    dp_peers = [lax.rem(dp + o, n_dp) for o in range(1, n_dp)]
    tp_peers = [lax.rem(tp + o, n_tp) for o in range(1, n_tp)]
    everyone = [{"ctx": other}] + [{"dp": p} for p in dp_peers] + [{"tp": p} for p in tp_peers]
    for device in everyone:
        pl.semaphore_signal(barrier, inc=1, device_id=device, device_id_type=MESH)
    chunk = rows // TOKEN_LOADS
    column = lambda o: weights.at[:, pl.ds(o * HEAD, HEAD)]
    moves = [(wk_h, column(1)), (wv_h, column(2))]
    for part in range(TOKEN_LOADS):
        here = pl.ds(part * chunk, chunk)
        moves.append((tok_h.at[here, :], tok.at[here, :]))
    moves += [(wq_h, column(0)), (grad_h, cot), (wo_h, w_out)]
    loads = [
        pltpu.make_async_copy(source, target, load_sem.at[o])
        for o, (source, target) in enumerate(moves)
    ]
    for load in loads:
        load.start()
    started = []
    share = rows // n_tp
    flows = ((0, tp, tp + 1), (1, n_tp - 1 - tp, tp - 1))

    def line_copy(flow, source, slot, piece, onto):
        return pltpu.make_async_remote_copy(
            src_ref=source, dst_ref=lines[2 * flow].at[slot, piece],
            send_sem=line_send.at[flow, slot, piece], recv_sem=line_recv.at[flow, slot, piece],
            device_id={"tp": onto}, device_id_type=MESH,
        )

    def line_piece(flow, slot, piece):
        mine = slot if flow else n_tp - 1 - slot
        return at(mine * PIECES + piece, share // PIECES)

    def line_start(slot):
        for piece in range(PIECES):
            for flow, place, onto in flows:

                @pl.when(place == 0)
                def _():
                    own = part_s.at[line_piece(flow, slot, piece), :]
                    line_copy(flow, own, slot, piece, onto).start()

    def line_step(step, pieces=range(PIECES)):
        for piece in pieces:
            for flow, place, onto in flows:
                slot = step - place
                arrived, summed = lines[2 * flow], lines[2 * flow + 1]

                @pl.when((slot >= 0) & (place > 0))
                def _():
                    line_copy(flow, arrived.at[slot, piece], slot, piece, onto).wait_recv()
                    if step < n_tp - 1:
                        own = part_s[line_piece(flow, slot, piece), :].astype(F32)
                        summed[slot, piece] = (own + arrived[slot, piece].astype(F32)).astype(BF16)
                        line_copy(flow, summed.at[slot, piece], slot, piece, onto).start()
                    else:
                        acc[at(piece, share // PIECES), :] += arrived[slot, piece].astype(F32)

    def line_end():
        for step in range(n_tp - 1):
            for piece in range(PIECES):
                for flow, place, onto in flows:
                    slot = step - place

                    @pl.when(slot >= 0)
                    def _():
                        source = lines[2 * flow + 1].at[slot, piece]
                        line_copy(flow, source, slot, piece, onto).wait_send()

    def send(src, dst, **device):
        slot = len(started)
        copy = pltpu.make_async_remote_copy(
            src_ref=src, dst_ref=dst, send_sem=send_sem.at[slot], recv_sem=recv_sem.at[slot],
            device_id=device, device_id_type=MESH,
        )
        copy.start()
        started.append(copy)
        return copy

    def swap_cores(group, full):
        group["full"][...] = full
        half = group["full"].shape[0] // 2
        group["s1"][...] = group["full"][at(other, half), :].astype(BF16)
        return [send(group["s1"], group["r1"], ctx=other)]

    def swap_chips(group, copies):
        half = group["full"].shape[0] // 2
        size = half // n_dp
        copies[0].wait_recv()
        total = group["full"][at(me, half), :] + group["r1"][...].astype(F32)
        group["sum"][...] = total
        group["s2"][...] = total.astype(BF16)
        return [
            send(group["s2"].at[at(p, size), :], group["r2"].at[o], dp=p)
            for o, p in enumerate(dp_peers)
        ]

    def gather_chips(group, copies):
        size = group["sum"].shape[0] // n_dp
        total = group["sum"][at(dp, size), :]
        for o, copy in enumerate(copies):
            copy.wait_recv()
            total = total + group["r2"][o].astype(F32)
        mine = at(me * n_dp + dp, size)
        group["res"][mine, :] = total.astype(BF16)
        piece = group["res"].at[mine, :]
        return [send(piece, piece, dp=p) for p in dp_peers], [send(piece, piece, ctx=other)]

    def gather_cores(group, copies):
        size = group["sum"].shape[0] // n_dp
        around, across = copies
        for o, copy in enumerate(around):
            copy.wait_recv()
            owner = lax.rem(dp + n_dp - 1 - o, n_dp)
            piece = group["res"].at[at(me * n_dp + owner, size), :]
            across.append(send(piece, piece, ctx=other))
        return across

    def gathered(group, copies):
        for copy in copies:
            copy.wait_recv()
        return group["res"][...]

    for load in loads[:2]:
        load.wait()
    for part in range(TOKEN_LOADS):
        loads[2 + part].wait()
        chunk = rows // TOKEN_LOADS
        here = pl.ds(part * chunk, chunk)
        both = jnp.dot(tok[here, :], weights[:, HEAD:], preferred_element_type=F32)
        kw[0][pl.ds(BLOCK + part * chunk, chunk), :] = both[:, :HEAD]
        vw[0][pl.ds(BLOCK + part * chunk, chunk), :] = both[:, HEAD:]
    coarsen_keys(sizes, kw, vw)
    for h, size in enumerate(sizes):
        here = pl.ds(BLOCK, size)
        for pair, source in ((k2, kw), (v2, vw)):
            pair[0][h][here, :], pair[1][h][here, :] = split(source[h][here, :])
        tails_s[h] = k2[0][h][pl.ds(size, BLOCK), :]
        tails_s[levels + h] = v2[0][h][pl.ds(size, BLOCK), :]
    loads[-3].wait()
    qs[0][...] = jnp.dot(tok[...], weights[:, :HEAD], preferred_element_type=F32)
    coarsen_queries(sizes, qs)
    for h in range(levels):
        q2[0][h][...], q2[1][h][...] = split(qs[h][...] * HEAD ** (-0.5))
    pl.semaphore_wait(barrier, len(everyone))
    tails = send(tails_s, tails_r, ctx=other)
    later = [(h, b) for h, size in enumerate(sizes) for b in range(1, size // BLOCK)]
    first = [(h, 0) for h in range(levels)]
    for h, block in later:
        attend_block(h, block, has_prior, q2, k2, v2, probs, tops, nums, dens)

    loads[-2].wait()
    loads[-1].wait()
    positions = me * rows + lax.broadcasted_iota(jnp.int32, (rows, width), 0)
    cot[...] = jnp.where(positions < length[0] * BLOCK, cot[...], jnp.zeros((), BF16))
    grad_mixed = mm(cot[...], w_out[...], NT)
    for h in range(levels):
        dk[h][...] = jnp.zeros_like(dk[h])
        dv[h][...] = jnp.zeros_like(dv[h])
        for pair in (k2, v2):
            for part in pair:
                part[h][pl.ds(0, BLOCK), :] = jnp.zeros((BLOCK, HEAD), BF16)

    @pl.when(has_prior)
    def _():
        tails.wait_recv()
        for h in range(levels):
            k2[0][h][pl.ds(0, BLOCK), :] = tails_r[h]
            v2[0][h][pl.ds(0, BLOCK), :] = tails_r[levels + h]

    for h, block in first:
        attend_block(h, block, has_prior, q2, k2, v2, probs, tops, nums, dens)
    attended, inverse = merge(sizes, tops, nums, dens, keeps, gains, temp)
    back_stats(sizes, attended, inverse, grad_mixed, keeps, gains, gs, ds, temp)
    for h, block in first:
        back_block(h, block, q2, k2, v2, probs, gs, ds, dq, dk, dv)
        back_s[h] = dk[h][pl.ds(0, BLOCK), :].astype(BF16)
        back_s[levels + h] = dv[h][pl.ds(0, BLOCK), :].astype(BF16)
    back = send(back_s, back_r, ctx=other)
    tok_t[...] = tok[...].T
    outs = groups[0]
    out_copies = swap_cores(outs, mm(attended, cot[...], TN) * scale)
    for h, block in later:
        back_block(h, block, q2, k2, v2, probs, gs, ds, dq, dk, dv)
    out_copies = swap_chips(outs, out_copies)
    r_s[:, :HEAD] = spread_down(sizes, lambda h: dq[h][...], 0.5, temp[0]).astype(BF16)

    @pl.when(jnp.logical_not(has_prior))
    def _():
        back.wait_recv()
        for h, size in enumerate(sizes):
            dk[h][pl.ds(size, BLOCK), :] += back_r[h].astype(F32)
            dv[h][pl.ds(size, BLOCK), :] += back_r[levels + h].astype(F32)

    own = lambda d: lambda h: d[h][pl.ds(BLOCK, sizes[h]), :]
    r_s[:, HEAD : 2 * HEAD] = spread_down(sizes, own(dk), 0.5, temp[0]).astype(BF16)
    r_s[:, 2 * HEAD :] = spread_down(sizes, own(dv), 1.0, temp[1]).astype(BF16)
    chunk = rows // PART_CHUNKS
    slots = n_tp // PART_CHUNKS
    for part in range(PART_CHUNKS):
        here = at(jnp.where(2 * tp < n_tp, PART_CHUNKS - 1 - part, part), chunk)
        part_s[here, :] = mm(r_s[here, :], weights[...], NT).astype(BF16)
        for slot in range(part * slots, min((part + 1) * slots, n_tp - 1)):
            line_start(slot)
    acc[...] = part_s[at(tp, share), :].astype(F32)
    copies = []
    for o, group in enumerate(groups[1:]):
        size = group["full"].shape[0]
        copies.append(swap_cores(group, jnp.dot(
            tok_t[pl.ds(o * size, size), :], r_s[...], preferred_element_type=F32
        ) * scale))
    copies = [swap_chips(group, c) for group, c in zip(groups[1:], copies)]
    out_copies = gather_chips(outs, out_copies)
    rounds = [(step, piece) for step in range(1, n_tp) for piece in range(PIECES)]

    def advance(count):
        for step, piece in rounds[:count]:
            line_step(step, [piece])
        del rounds[:count]

    advance(len(rounds) - 3 * PIECES + ORDER[0])
    copies[0] = gather_chips(groups[1], copies[0])
    advance(ORDER[1])
    for o in range(1, GRAD_GROUPS):
        copies[o] = gather_chips(groups[1 + o], copies[o])
    out_copies = gather_cores(outs, out_copies)
    advance(ORDER[2])
    copies[0] = gather_cores(groups[1], copies[0])
    advance(ORDER[3])
    for o in range(1, GRAD_GROUPS):
        copies[o] = gather_cores(groups[1 + o], copies[o])
    wout_out[...] = gathered(outs, out_copies).astype(F32)
    for o, group in enumerate(groups[1:]):
        size = group["full"].shape[0]
        here = pl.ds(o * size, size)
        result = gathered(group, copies[o]).astype(F32)
        query_out[here, :] = result[:, :HEAD]
        key_out[here, :] = result[:, HEAD : 2 * HEAD]
        value_out[here, :] = result[:, 2 * HEAD :]
    advance(len(rounds))
    tokens_out[...] = acc[...].astype(BF16)

    @pl.when(has_prior)
    def _():
        back.wait_recv()

    @pl.when(jnp.logical_not(has_prior))
    def _():
        tails.wait_recv()

    for copy in started:
        copy.wait_send()
    line_end()


def store_kernel(*refs):
    sem = refs[-1]
    copies = [pltpu.make_async_copy(refs[i], refs[5 + i], sem.at[i]) for i in range(5)]
    for copy in copies:
        copy.start()
    for copy in copies:
        copy.wait()


def fast(tokens, lengths, w_query, w_key, w_value, w_out, grad_out):
    rows, width = tokens.shape[1:]
    n_dp, n_tp = lax.axis_size("dp"), lax.axis_size("tp")
    total = rows * lax.axis_size("ctx")
    sizes = level_sizes(rows, total)
    levels = len(sizes)
    scale = float(n_dp * total) ** (-0.5)
    tail = pltpu.VMEM((2 * levels, BLOCK, HEAD), BF16)

    def group(count, columns):
        half = count // 2
        return dict(
            full=pltpu.VMEM((count, columns), F32),
            s1=pltpu.VMEM((half, columns), BF16),
            r1=pltpu.VMEM((half, columns), BF16),
            sum=pltpu.VMEM((half, columns), F32),
            s2=pltpu.VMEM((half, columns), BF16),
            r2=pltpu.VMEM((n_dp - 1, half // n_dp, columns), BF16),
            res=pltpu.VMEM((count, columns), BF16),
        )

    copies = 2 + (1 + GRAD_GROUPS) * (1 + 3 * (n_dp - 1) + 1)
    vm = pl.BlockSpec(memory_space=pltpu.VMEM)
    hbm = pl.BlockSpec(memory_space=pl.ANY)
    shapes = [((rows // n_tp, width), BF16)] + [((width, HEAD), F32)] * 3 + [((HEAD, width), F32)]
    summed = pl.pallas_call(
        partial(layer_kernel, sizes, scale, n_dp, n_tp),
        out_shape=tuple(pltpu.VMEM(*s) for s in shapes),
        in_specs=[pl.BlockSpec(memory_space=pltpu.SMEM)] + [hbm] * 6,
        out_specs=[vm] * 5,
        scratch_shapes=dict(
            attend_scratch(sizes),
            q2=[level_scratch(sizes, 0, BF16)] * 2,
            k2=[level_scratch(sizes, BLOCK, BF16)] * 2,
            v2=[level_scratch(sizes, BLOCK, BF16)] * 2,
            tok=pltpu.VMEM((rows, width), BF16),
            tok_t=pltpu.VMEM((width, rows), BF16),
            weights=pltpu.VMEM((width, 3 * HEAD), BF16),
            w_out=pltpu.VMEM((HEAD, width), BF16),
            cot=pltpu.VMEM((rows, width), BF16),
            r_s=pltpu.VMEM((rows, 3 * HEAD), BF16),
            load_sem=pltpu.SemaphoreType.DMA((5 + TOKEN_LOADS,)),
            tails_s=tail,
            tails_r=tail,
            back_s=tail,
            back_r=tail,
            part_s=pltpu.VMEM((rows, width), BF16),
            lines=[pltpu.VMEM((n_tp, PIECES, rows // n_tp // PIECES, width), BF16)] * 4,
            acc=pltpu.VMEM((rows // n_tp, width), F32),
            line_send=pltpu.SemaphoreType.DMA((2, n_tp, PIECES)),
            line_recv=pltpu.SemaphoreType.DMA((2, n_tp, PIECES)),
            groups=[group(HEAD, width)] + [group(width // GRAD_GROUPS, 3 * HEAD)] * GRAD_GROUPS,
            send_sem=pltpu.SemaphoreType.DMA((copies,)),
            recv_sem=pltpu.SemaphoreType.DMA((copies,)),
        ),
        compiler_params=pltpu.CompilerParams(
            vmem_limit_bytes=58 * 2**20, collective_id=0, has_side_effects=True
        ),
    )(lengths, tokens[0], w_query, w_key, w_value, w_out, grad_out[0])
    grad_tokens, grad_query, grad_key, grad_value, grad_w_out = pl.pallas_call(
        store_kernel,
        out_shape=tuple(jax.ShapeDtypeStruct(*s) for s in shapes),
        in_specs=[hbm] * 5,
        out_specs=[hbm] * 5,
        scratch_shapes=[pltpu.SemaphoreType.DMA((5,))],
        compiler_params=pltpu.CompilerParams(vmem_limit_bytes=2 * 2**20),
    )(*summed)
    return (grad_tokens[None], grad_query, grad_key, grad_value, grad_w_out)


def body(*args):
    rows = args[0].shape[1]
    sizes = level_sizes(rows, rows * lax.axis_size("ctx"))
    if sizes[-1] < BLOCK or sizes[0] % BLOCK or lax.axis_size("ctx") != 2:
        return local(*args)
    return fast(*args)

def solution(mesh):
    placed = (
        P("dp", "ctx", None),
        P("dp"),
        P(None, "tp"),
        P(None, "tp"),
        P(None, "tp"),
        P("tp", None),
        P("dp", "ctx", None),
    )
    return jax.shard_map(
        body,
        mesh=mesh,
        in_specs=placed,
        out_specs=(
            P("dp", ("ctx", "tp"), None),
            P(None, "tp"),
            P(None, "tp"),
            P(None, "tp"),
            P("tp", None),
        ),
        check_vma=False,
    )
```

```python
from functools import partial

import jax
import jax.numpy as jnp
from jax import lax
from jax.experimental import pallas as pl
from jax.experimental.pallas import tpu as pltpu
from jax.sharding import PartitionSpec as P

HEAD = 128
BLOCK = 128
LEVELS = 8


precise = lax.Precision.HIGHEST
very_low = -1e30


def passed_along(value, axis, steps):
    count = lax.axis_size(axis)
    first, last = (max(0, -steps), min(count, count - steps))
    return lax.ppermute(value, axis, [(source, source + steps) for source in range(first, last)])


def level_stats(queries, key_rows, values, query_pos, key_pos, height, block, weight):
    scores = jnp.einsum("nqe,nke->nqk", queries, key_rows, precision=precise) * queries.shape[
        -1
    ] ** (-0.5)
    query_at = query_pos[:, :, None]
    key_at = key_pos[:, None, :]
    allowed = (query_at // block - key_at // block <= 1) & (key_at >= 0)
    if height == 0:
        allowed = allowed & (key_at <= query_at)
    else:
        half_block = block // 2
        allowed = allowed & (query_at // half_block - key_at // half_block >= 2)
    masked = jnp.where(allowed, scores, very_low)
    row_max = jnp.max(masked, axis=-1)
    exp_scores = jnp.where(allowed, jnp.exp(masked - row_max[..., None]), 0.0)
    weighted = jnp.einsum("nqk,nke->nqe", exp_scores, values, precision=precise)
    totals = jnp.sum(exp_scores, axis=-1) * weight
    return (row_max, weighted, totals)


def head_stats(queries, key_rows, values, query_pos, key_pos, height, block, weight):
    single = partial(level_stats, height=height, block=block, weight=weight)
    return jax.vmap(single, in_axes=(0, 0, 0, None, None))(
        queries, key_rows, values, query_pos, key_pos
    )


def coarse(field_data, group_size, summed):
    grouped = field_data.reshape(
        field_data.shape[:-2]
        + (field_data.shape[-2] // group_size, group_size, field_data.shape[-1])
    )
    if summed:
        return jnp.sum(grouped, axis=-2)
    return jnp.mean(grouped, axis=-2)


def merge_levels(stats_list):
    best_max, running, mass_sum = stats_list[0]
    for row_max, weighted, totals in stats_list[1:]:
        new_best = jnp.maximum(best_max, row_max)
        keep_old = jnp.exp(best_max - new_best)
        gain_new = jnp.exp(row_max - new_best)
        running = running * keep_old[..., None] + weighted * gain_new[..., None]
        mass_sum = mass_sum * keep_old + totals * gain_new
        best_max = new_best
    return running / mass_sum[..., None]


def earlier(payload, distance):
    return passed_along(payload.astype(jnp.bfloat16), "ctx", distance).astype(payload.dtype)


def returned(payload, distance):
    return passed_along(payload.astype(jnp.bfloat16), "ctx", -distance).astype(payload.dtype)


def local(tokens, lengths, w_query, w_key, w_value, w_out, grad_out):
    devices = lax.axis_size("ctx")
    ctx_index = lax.axis_index("ctx")
    local_rows = tokens.shape[1]
    token_total = lax.axis_size("dp") * devices * local_rows
    grad_scale = float(token_total) ** (-0.5)
    flat_tokens = tokens[0]
    head_count = w_query.shape[1] // HEAD

    def split_heads(matrix):
        return matrix.reshape(local_rows, head_count, HEAD).transpose(1, 0, 2)

    def join_heads(field_data):
        return field_data.transpose(1, 0, 2).reshape(local_rows, head_count * HEAD)

    queries = split_heads(jnp.dot(flat_tokens, w_query, preferred_element_type=jnp.float32))
    key_rows = split_heads(jnp.dot(flat_tokens, w_key, preferred_element_type=jnp.float32))
    values = split_heads(jnp.dot(flat_tokens, w_value, preferred_element_type=jnp.float32))
    group_sizes = [2**height for height in range(LEVELS)]
    fine_levels = [height for height in range(LEVELS) if local_rows // group_sizes[height] >= BLOCK]
    rough_levels = [height for height in range(LEVELS) if local_rows // group_sizes[height] < BLOCK]

    def coarsen(all_queries, all_keys, all_values):
        return (
            [coarse(all_queries, group_sizes[height], False) for height in range(LEVELS)],
            [coarse(all_keys, group_sizes[height], False) for height in range(LEVELS)],
            [coarse(all_values, group_sizes[height], True) for height in range(LEVELS)],
        )

    (coarse_query, coarse_key, coarse_value), coarse_pull = jax.vjp(
        coarsen, queries, key_rows, values
    )
    tail_rows = jnp.stack(
        [
            jnp.concatenate([coarse_key[height][:, -BLOCK:] for height in fine_levels], 1),
            jnp.concatenate([coarse_value[height][:, -BLOCK:] for height in fine_levels], 1),
        ],
        0,
    )
    coarse_pack = jnp.stack(
        [
            jnp.concatenate([coarse_key[height] for height in rough_levels], 1),
            jnp.concatenate([coarse_value[height] for height in rough_levels], 1),
        ],
        0,
    )
    tail_count = tail_rows.shape[2]
    reach_devs = 2 * BLOCK // (local_rows // group_sizes[rough_levels[-1]])
    step_count = reach_devs.bit_length() - 1
    first_move = earlier(jnp.concatenate([tail_rows, coarse_pack], 2), 1)
    prior_tails = first_move[:, :, :tail_count]
    window = jnp.stack([first_move[:, :, tail_count:], coarse_pack], 0)
    for bit_pos in range(1, step_count):
        distance = 2**bit_pos
        if distance < devices:
            moved_rows = earlier(window, distance)
        else:
            moved_rows = jnp.zeros_like(window)
        window = jnp.concatenate([moved_rows, window], 0)
    prior_in = window[:-1]

    def attend_local(query_list, key_list, value_list, tails_in, rows_in):
        stats_list = []
        tail_at = 0
        rough_at = 0
        for height in range(LEVELS):
            group_size = group_sizes[height]
            coarse_rows = local_rows // group_size
            own_pos = ctx_index * coarse_rows + jnp.arange(coarse_rows, dtype=jnp.int32)
            if height in fine_levels:
                blocks = coarse_rows // BLOCK
                query_blocks = query_list[height].reshape(head_count, blocks, BLOCK, -1)
                key_blocks = key_list[height].reshape(head_count, blocks, BLOCK, -1)
                value_blocks = value_list[height].reshape(head_count, blocks, BLOCK, -1)
                prev_keys = tails_in[0][:, tail_at : tail_at + BLOCK][:, None]
                prev_values = tails_in[1][:, tail_at : tail_at + BLOCK][:, None]
                key_win = jnp.concatenate(
                    [jnp.concatenate([prev_keys, key_blocks[:, :-1]], 1), key_blocks], 2
                )
                value_win = jnp.concatenate(
                    [jnp.concatenate([prev_values, value_blocks[:, :-1]], 1), value_blocks], 2
                )
                query_pos = own_pos.reshape(blocks, BLOCK)
                key_pos = jnp.concatenate([query_pos - BLOCK, query_pos], 1)
                tail_at += BLOCK
            else:
                query_blocks = query_list[height][:, None]
                query_pos = own_pos[None]
                need_devs = 2 * BLOCK // coarse_rows
                earlier_keys = rows_in[
                    rows_in.shape[0] - (need_devs - 1) :, 0, :, rough_at : rough_at + coarse_rows
                ]
                earlier_values = rows_in[
                    rows_in.shape[0] - (need_devs - 1) :, 1, :, rough_at : rough_at + coarse_rows
                ]
                key_win = jnp.concatenate(
                    [
                        earlier_keys.transpose(1, 0, 2, 3).reshape(
                            head_count, (need_devs - 1) * coarse_rows, -1
                        ),
                        key_list[height],
                    ],
                    1,
                )[:, None]
                value_win = jnp.concatenate(
                    [
                        earlier_values.transpose(1, 0, 2, 3).reshape(
                            head_count, (need_devs - 1) * coarse_rows, -1
                        ),
                        value_list[height],
                    ],
                    1,
                )[:, None]
                key_pos = (
                    (ctx_index + 1) * coarse_rows
                    - need_devs * coarse_rows
                    + jnp.arange(need_devs * coarse_rows, dtype=jnp.int32)
                )[None]
                rough_at += coarse_rows
            row_max, weighted, totals = head_stats(
                query_blocks,
                key_win,
                value_win,
                query_pos,
                key_pos,
                height,
                BLOCK,
                float(group_size),
            )
            stats_list.append(
                (
                    jnp.repeat(row_max.reshape(head_count, coarse_rows), group_size, 1),
                    jnp.repeat(weighted.reshape(head_count, coarse_rows, -1), group_size, 1),
                    jnp.repeat(totals.reshape(head_count, coarse_rows), group_size, 1),
                )
            )
        return merge_levels(stats_list)

    attended, attend_pull = jax.vjp(
        attend_local, coarse_query, coarse_key, coarse_value, prior_tails, prior_in
    )
    mixed_heads = join_heads(attended).astype(jnp.bfloat16)
    positions = ctx_index * local_rows + jnp.arange(local_rows, dtype=jnp.int32)
    valid_rows = positions < lengths[0] * BLOCK
    cotangent = jnp.where(valid_rows[:, None], grad_out[0], jnp.zeros_like(grad_out[0]))
    grad_mixed = jnp.dot(cotangent, w_out.T, preferred_element_type=jnp.float32)
    grad_cquery, grad_ckey, grad_cvalue, grad_tails, grad_prior = attend_pull(
        split_heads(grad_mixed)
    )
    grad_cquery = list(grad_cquery)
    grad_ckey = list(grad_ckey)
    grad_cvalue = list(grad_cvalue)
    gradient = jnp.concatenate([grad_prior, jnp.zeros_like(coarse_pack)[None]], 0)
    for bit_pos in range(step_count - 1, 0, -1):
        distance = 2**bit_pos
        upper_part = gradient[distance:]
        if distance < devices:
            upper_part = upper_part + returned(gradient[:distance], distance)
        gradient = upper_part
    sent_back = returned(jnp.concatenate([grad_tails, gradient[0]], 2), 1)
    tails_back = sent_back[:, :, :tail_count]
    pack_back = sent_back[:, :, tail_count:] + gradient[1]
    tail_at = 0
    for height in fine_levels:
        grad_ckey[height] = (
            grad_ckey[height].at[:, -BLOCK:].add(tails_back[0, :, tail_at : tail_at + BLOCK])
        )
        grad_cvalue[height] = (
            grad_cvalue[height].at[:, -BLOCK:].add(tails_back[1, :, tail_at : tail_at + BLOCK])
        )
        tail_at += BLOCK
    rough_at = 0
    for height in rough_levels:
        coarse_rows = local_rows // group_sizes[height]
        grad_ckey[height] = grad_ckey[height] + pack_back[0, :, rough_at : rough_at + coarse_rows]
        grad_cvalue[height] = (
            grad_cvalue[height] + pack_back[1, :, rough_at : rough_at + coarse_rows]
        )
        rough_at += coarse_rows
    grad_q, grad_k, grad_v = coarse_pull((grad_cquery, grad_ckey, grad_cvalue))
    rounded_q = join_heads(grad_q).astype(jnp.bfloat16)
    rounded_k = join_heads(grad_k).astype(jnp.bfloat16)
    rounded_v = join_heads(grad_v).astype(jnp.bfloat16)
    partial_term = (
        jnp.dot(rounded_q, w_query.T, preferred_element_type=jnp.float32)
        + jnp.dot(rounded_k, w_key.T, preferred_element_type=jnp.float32)
        + jnp.dot(rounded_v, w_value.T, preferred_element_type=jnp.float32)
    )
    grad_tokens = lax.psum_scatter(
        partial_term.astype(jnp.bfloat16), "tp", scatter_dimension=0, tiled=True
    )[None]
    stacked_in = jnp.concatenate([rounded_q, rounded_k, rounded_v], 1)
    grads_in = jnp.einsum("rc,rh->ch", flat_tokens, stacked_in, preferred_element_type=jnp.float32)
    grads_out = jnp.einsum("rc,rh->ch", cotangent, mixed_heads, preferred_element_type=jnp.float32)
    summed = lax.psum(jnp.concatenate([grads_in, grads_out], 1) * grad_scale, ("dp", "ctx"))
    head_cols = head_count * HEAD
    grad_query = summed[:, :head_cols]
    grad_key = summed[:, head_cols : 2 * head_cols]
    grad_value = summed[:, 2 * head_cols : 3 * head_cols]
    grad_w_out = summed[:, 3 * head_cols :].T
    return (grad_tokens, grad_query, grad_key, grad_value, grad_w_out)


F32 = jnp.float32
BF16 = jnp.bfloat16
NT = (((1,), (1,)), ((), ()))
NN = (((1,), (0,)), ((), ()))
TN = (((0,), (0,)), ((), ()))


def mm(a, b, dims):
    return lax.dot_general(a.astype(BF16), b.astype(BF16), dims, preferred_element_type=F32)


def split(value):
    high = value.astype(BF16)
    return high, (value - high.astype(F32)).astype(BF16)


def mm3(a, b, dims):
    dot = partial(lax.dot_general, dimension_numbers=dims, preferred_element_type=F32)
    result = dot(a[1], b[0])
    if b[1] is not None:
        result = result + dot(a[0], b[1])
    return dot(a[0], b[0]) + result


def window_of(h, block, high, low):
    window = pl.ds(block * BLOCK, span(h))
    exact = h > 0 and block == 0
    return high[h][window, :], None if exact else low[h][window, :]


def pairs(ref, start, count):
    return ref[pl.ds(start, count, stride=2), :], ref[pl.ds(start + 1, count, stride=2), :]


def doubled(ref, value):
    count = value.shape[0]
    ref[pl.ds(0, count, stride=2), :] = value
    ref[pl.ds(1, count, stride=2), :] = value
    return ref[pl.ds(0, 2 * count), :]


def halved(ref, value):
    count = value.shape[0]
    ref[pl.ds(0, count), :] = value
    first, second = pairs(ref, 0, count // 2)
    return first + second


def level_sizes(rows, total):
    return [rows >> h for h in range(LEVELS) if h == 0 or (total >> h) > BLOCK]


def coarsen_keys(sizes, kw, vw):
    for h in range(1, len(sizes)):
        first, second = pairs(kw[h - 1], BLOCK, sizes[h])
        kw[h][pl.ds(BLOCK, sizes[h]), :] = (first + second) * 0.5
        first, second = pairs(vw[h - 1], BLOCK, sizes[h])
        vw[h][pl.ds(BLOCK, sizes[h]), :] = first + second


def coarsen_queries(sizes, qs):
    for h in range(1, len(sizes)):
        first, second = pairs(qs[h - 1], 0, sizes[h])
        qs[h][...] = (first + second) * 0.5


def span(h):
    return 2 * BLOCK if h == 0 else BLOCK


def block_mask(h, block, has_prior):
    row = lax.broadcasted_iota(jnp.int32, (BLOCK, span(h)), 0)
    col = lax.broadcasted_iota(jnp.int32, (BLOCK, span(h)), 1)
    if h == 0:
        allowed = col <= row + BLOCK
        if block == 0:
            allowed = allowed & ((col >= BLOCK) | has_prior)
    else:
        allowed = (row >= BLOCK // 2) | (col < BLOCK // 2)
        if block == 0:
            allowed = allowed & has_prior
    return allowed


def attend_block(h, block, has_prior, q2, k2, v2, probs, tops, nums, dens):
    rows = pl.ds(block * BLOCK, BLOCK)
    allowed = block_mask(h, block, has_prior)
    scores = mm3((q2[0][h][rows, :], q2[1][h][rows, :]), window_of(h, block, *k2), NT)
    masked = jnp.where(allowed, scores, very_low)
    top = jnp.max(masked, axis=-1, keepdims=True)
    p = jnp.where(allowed, jnp.exp(masked - top), 0.0)
    probs[h][block] = p
    tops[h][rows, :] = jnp.broadcast_to(top, (BLOCK, HEAD))
    nums[h][rows, :] = mm3(split(p), window_of(h, block, *v2), NN)
    dens[h][rows, :] = jnp.broadcast_to(
        jnp.sum(p, axis=-1, keepdims=True) * float(2**h), (BLOCK, HEAD)
    )


def merge(sizes, tops, nums, dens, keeps, gains, temp):
    last = len(sizes) - 1
    top, num, den = tops[last][...], nums[last][...], dens[last][...]
    keeps[last][...] = jnp.ones_like(top)
    for h in range(last - 1, -1, -1):
        top, num, den = (doubled(t, x) for t, x in zip(temp, (top, num, den)))
        own = tops[h][...]
        best = jnp.maximum(own, top)
        keep, gain = jnp.exp(own - best), jnp.exp(top - best)
        keeps[h][...] = keep
        gains[h][...] = gain
        num = nums[h][...] * keep + num * gain
        den = dens[h][...] * keep + den * gain
        top = best
    inverse = 1.0 / den
    return num * inverse, inverse


def back_stats(sizes, attended, inverse, grad_mixed, keeps, gains, gs, ds, temp):
    delta = jnp.sum(attended * grad_mixed, axis=-1, keepdims=True)
    flow, part = grad_mixed * inverse, delta * inverse
    for h in range(len(sizes)):
        gs[h][...] = flow * keeps[h][...]
        ds[h][...] = part * keeps[h][...]
        if h + 1 < len(sizes):
            flow = halved(temp[0], flow * gains[h][...])
            part = halved(temp[1], part * gains[h][...])


def back_block(h, block, q2, k2, v2, probs, gs, ds, dq, dk, dv):
    rows = pl.ds(block * BLOCK, BLOCK)
    window = pl.ds(block * BLOCK, span(h))
    p, grad = probs[h][block], split(gs[h][rows, :])
    loss = ds[h][rows, :] * float(2**h)
    if h == 0:
        loss = jnp.concatenate([loss, loss], 1)
    dscore = (p * (mm3(grad, window_of(h, block, *v2), NT) - loss)).astype(BF16)
    dq[h][rows, :] = mm(dscore, k2[0][h][window, :], NN) * HEAD ** (-0.5)
    dk[h][window, :] += mm(dscore, q2[0][h][rows, :], TN)
    dv[h][window, :] += mm(p, grad[0], TN)


def spread_down(sizes, own, factor, temp):
    total = own(len(sizes) - 1)
    for h in range(len(sizes) - 2, -1, -1):
        total = own(h) + doubled(temp, total * factor)
    return total


def level_scratch(sizes, extra=0, kind=F32):
    return [pltpu.VMEM((size + extra, HEAD), kind) for size in sizes]


def attend_scratch(sizes):
    per_level = lambda extra=0: level_scratch(sizes, extra)
    return dict(
        qs=per_level(),
        kw=per_level(BLOCK),
        vw=per_level(BLOCK),
        probs=[
            pltpu.VMEM((size // BLOCK, BLOCK, span(h)), F32) for h, size in enumerate(sizes)
        ],
        tops=per_level(),
        nums=per_level(),
        dens=per_level(),
        keeps=per_level(),
        gains=per_level(),
        gs=per_level(),
        ds=per_level(),
        dq=per_level(),
        dk=per_level(BLOCK),
        dv=per_level(BLOCK),
        temp=[pltpu.VMEM((sizes[0], HEAD), F32)] * 3,
    )
MESH = pl.DeviceIdType.MESH
PIECES = 4
TOKEN_LOADS = 1
PART_CHUNKS = 2
GRAD_GROUPS = 2
ORDER = (3, 2, 2, 3)


def at(index, size):
    return pl.ds(pl.multiple_of(index * size, size), size)


def layer_kernel(
    sizes, scale, n_dp, n_tp,
    length, tok_h, wq_h, wk_h, wv_h, wo_h, grad_h,
    tokens_out, query_out, key_out, value_out, wout_out,
    *, q2, k2, v2, tok, tok_t, weights, w_out, cot, r_s, load_sem, qs, kw, vw, probs, tops, nums, dens, keeps, gains, gs, ds, dq, dk, dv, temp,
    tails_s, tails_r, back_s, back_r, part_s, lines, acc, line_send, line_recv, groups, send_sem, recv_sem,
):
    rows, width = tok.shape
    levels = len(sizes)
    dp, me, tp = lax.axis_index("dp"), lax.axis_index("ctx"), lax.axis_index("tp")
    other = 1 - me
    has_prior = me > 0
    barrier = pltpu.get_barrier_semaphore()
    dp_peers = [lax.rem(dp + o, n_dp) for o in range(1, n_dp)]
    for device in [{"ctx": other}] + [{"dp": p} for p in dp_peers]:
        pl.semaphore_signal(barrier, inc=1, device_id=device, device_id_type=MESH)
    for there, beside in ((tp > 0, tp - 1), (tp < n_tp - 1, tp + 1)):

        @pl.when(there)
        def _():
            pl.semaphore_signal(barrier, inc=1, device_id={"tp": beside}, device_id_type=MESH)

    arrivals = n_dp + (tp > 0).astype(jnp.int32) + (tp < n_tp - 1).astype(jnp.int32)
    chunk = rows // TOKEN_LOADS
    column = lambda o: weights.at[:, pl.ds(o * HEAD, HEAD)]
    moves = [(wk_h, column(1)), (wv_h, column(2))]
    for part in range(TOKEN_LOADS):
        here = pl.ds(part * chunk, chunk)
        moves.append((tok_h.at[here, :], tok.at[here, :]))
    moves += [(wq_h, column(0)), (grad_h, cot), (wo_h, w_out)]
    loads = [
        pltpu.make_async_copy(source, target, load_sem.at[o])
        for o, (source, target) in enumerate(moves)
    ]
    for load in loads:
        load.start()
    started = []
    share = rows // n_tp
    flows = ((0, tp, tp + 1), (1, n_tp - 1 - tp, tp - 1))

    def line_copy(flow, source, slot, piece, onto):
        return pltpu.make_async_remote_copy(
            src_ref=source, dst_ref=lines[2 * flow].at[slot, piece],
            send_sem=line_send.at[flow, slot, piece], recv_sem=line_recv.at[flow, slot, piece],
            device_id={"tp": onto}, device_id_type=MESH,
        )

    def line_piece(flow, slot, piece):
        mine = slot if flow else n_tp - 1 - slot
        return at(mine * PIECES + piece, share // PIECES)

    def line_start(slot):
        for piece in range(PIECES):
            for flow, place, onto in flows:

                @pl.when(place == 0)
                def _():
                    own = part_s.at[line_piece(flow, slot, piece), :]
                    line_copy(flow, own, slot, piece, onto).start()

    def line_step(step, pieces=range(PIECES)):
        for piece in pieces:
            for flow, place, onto in flows:
                slot = step - place
                arrived, summed = lines[2 * flow], lines[2 * flow + 1]

                @pl.when((slot >= 0) & (place > 0))
                def _():
                    line_copy(flow, arrived.at[slot, piece], slot, piece, onto).wait_recv()
                    if step < n_tp - 1:
                        own = part_s[line_piece(flow, slot, piece), :].astype(F32)
                        summed[slot, piece] = (own + arrived[slot, piece].astype(F32)).astype(BF16)
                        line_copy(flow, summed.at[slot, piece], slot, piece, onto).start()
                    else:
                        acc[at(piece, share // PIECES), :] += arrived[slot, piece].astype(F32)

    def line_end():
        for step in range(n_tp - 1):
            for piece in range(PIECES):
                for flow, place, onto in flows:
                    slot = step - place

                    @pl.when(slot >= 0)
                    def _():
                        source = lines[2 * flow + 1].at[slot, piece]
                        line_copy(flow, source, slot, piece, onto).wait_send()

    def send(src, dst, **device):
        slot = len(started)
        copy = pltpu.make_async_remote_copy(
            src_ref=src, dst_ref=dst, send_sem=send_sem.at[slot], recv_sem=recv_sem.at[slot],
            device_id=device, device_id_type=MESH,
        )
        copy.start()
        started.append(copy)
        return copy

    def swap_cores(group, full):
        group["full"][...] = full
        half = group["full"].shape[0] // 2
        group["s1"][...] = group["full"][at(other, half), :].astype(BF16)
        return [send(group["s1"], group["r1"], ctx=other)]

    def swap_chips(group, copies):
        half = group["full"].shape[0] // 2
        size = half // n_dp
        copies[0].wait_recv()
        total = group["full"][at(me, half), :] + group["r1"][...].astype(F32)
        group["sum"][...] = total
        group["s2"][...] = total.astype(BF16)
        return [
            send(group["s2"].at[at(p, size), :], group["r2"].at[o], dp=p)
            for o, p in enumerate(dp_peers)
        ]

    def gather_chips(group, copies):
        size = group["sum"].shape[0] // n_dp
        total = group["sum"][at(dp, size), :]
        for o, copy in enumerate(copies):
            copy.wait_recv()
            total = total + group["r2"][o].astype(F32)
        mine = at(me * n_dp + dp, size)
        group["res"][mine, :] = total.astype(BF16)
        piece = group["res"].at[mine, :]
        return [send(piece, piece, dp=p) for p in dp_peers], [send(piece, piece, ctx=other)]

    def gather_cores(group, copies):
        size = group["sum"].shape[0] // n_dp
        around, across = copies
        for o, copy in enumerate(around):
            copy.wait_recv()
            owner = lax.rem(dp + n_dp - 1 - o, n_dp)
            piece = group["res"].at[at(me * n_dp + owner, size), :]
            across.append(send(piece, piece, ctx=other))
        return across

    def gathered(group, copies):
        for copy in copies:
            copy.wait_recv()
        return group["res"][...]

    for load in loads[:2]:
        load.wait()
    for part in range(TOKEN_LOADS):
        loads[2 + part].wait()
        chunk = rows // TOKEN_LOADS
        here = pl.ds(part * chunk, chunk)
        both = jnp.dot(tok[here, :], weights[:, HEAD:], preferred_element_type=F32)
        kw[0][pl.ds(BLOCK + part * chunk, chunk), :] = both[:, :HEAD]
        vw[0][pl.ds(BLOCK + part * chunk, chunk), :] = both[:, HEAD:]
    coarsen_keys(sizes, kw, vw)
    for h, size in enumerate(sizes):
        here = pl.ds(BLOCK, size)
        for pair, source in ((k2, kw), (v2, vw)):
            pair[0][h][here, :], pair[1][h][here, :] = split(source[h][here, :])
        tails_s[h] = k2[0][h][pl.ds(size, BLOCK), :]
        tails_s[levels + h] = v2[0][h][pl.ds(size, BLOCK), :]
    pl.semaphore_wait(barrier, arrivals)
    tails = send(tails_s, tails_r, ctx=other)
    loads[-3].wait()
    qs[0][...] = jnp.dot(tok[...], weights[:, :HEAD], preferred_element_type=F32)
    coarsen_queries(sizes, qs)
    for h in range(levels):
        q2[0][h][...], q2[1][h][...] = split(qs[h][...] * HEAD ** (-0.5))
    later = [(h, b) for h, size in enumerate(sizes) for b in range(1, size // BLOCK)]
    first = [(h, 0) for h in range(levels)]
    for h, block in later:
        attend_block(h, block, has_prior, q2, k2, v2, probs, tops, nums, dens)

    loads[-2].wait()
    loads[-1].wait()
    positions = me * rows + lax.broadcasted_iota(jnp.int32, (rows, width), 0)
    cot[...] = jnp.where(positions < length[0] * BLOCK, cot[...], jnp.zeros((), BF16))
    grad_mixed = mm(cot[...], w_out[...], NT)
    for h in range(levels):
        dk[h][...] = jnp.zeros_like(dk[h])
        dv[h][...] = jnp.zeros_like(dv[h])
        for pair in (k2, v2):
            for part in pair:
                part[h][pl.ds(0, BLOCK), :] = jnp.zeros((BLOCK, HEAD), BF16)

    @pl.when(has_prior)
    def _():
        tails.wait_recv()
        for h in range(levels):
            k2[0][h][pl.ds(0, BLOCK), :] = tails_r[h]
            v2[0][h][pl.ds(0, BLOCK), :] = tails_r[levels + h]

    for h, block in first:
        attend_block(h, block, has_prior, q2, k2, v2, probs, tops, nums, dens)
    attended, inverse = merge(sizes, tops, nums, dens, keeps, gains, temp)
    back_stats(sizes, attended, inverse, grad_mixed, keeps, gains, gs, ds, temp)
    for h, block in first:
        back_block(h, block, q2, k2, v2, probs, gs, ds, dq, dk, dv)
        back_s[h] = dk[h][pl.ds(0, BLOCK), :].astype(BF16)
        back_s[levels + h] = dv[h][pl.ds(0, BLOCK), :].astype(BF16)
    back = send(back_s, back_r, ctx=other)
    tok_t[...] = tok[...].T
    outs = groups[0]
    out_copies = swap_cores(outs, mm(attended, cot[...], TN) * scale)
    for h, block in later:
        back_block(h, block, q2, k2, v2, probs, gs, ds, dq, dk, dv)
    out_copies = swap_chips(outs, out_copies)
    r_s[:, :HEAD] = spread_down(sizes, lambda h: dq[h][...], 0.5, temp[0]).astype(BF16)

    @pl.when(jnp.logical_not(has_prior))
    def _():
        back.wait_recv()
        for h, size in enumerate(sizes):
            dk[h][pl.ds(size, BLOCK), :] += back_r[h].astype(F32)
            dv[h][pl.ds(size, BLOCK), :] += back_r[levels + h].astype(F32)

    own = lambda d: lambda h: d[h][pl.ds(BLOCK, sizes[h]), :]
    r_s[:, HEAD : 2 * HEAD] = spread_down(sizes, own(dk), 0.5, temp[0]).astype(BF16)
    r_s[:, 2 * HEAD :] = spread_down(sizes, own(dv), 1.0, temp[1]).astype(BF16)
    chunk = rows // PART_CHUNKS
    slots = n_tp // PART_CHUNKS
    for part in range(PART_CHUNKS):
        here = at(jnp.where(2 * tp < n_tp, PART_CHUNKS - 1 - part, part), chunk)
        part_s[here, :] = mm(r_s[here, :], weights[...], NT).astype(BF16)
        for slot in range(part * slots, min((part + 1) * slots, n_tp - 1)):
            line_start(slot)
    acc[...] = part_s[at(tp, share), :].astype(F32)
    copies = []
    for o, group in enumerate(groups[1:]):
        size = group["full"].shape[0]
        copies.append(swap_cores(group, jnp.dot(
            tok_t[pl.ds(o * size, size), :], r_s[...], preferred_element_type=F32
        ) * scale))
    copies = [swap_chips(group, c) for group, c in zip(groups[1:], copies)]
    out_copies = gather_chips(outs, out_copies)
    rounds = [(step, piece) for step in range(1, n_tp) for piece in range(PIECES)]

    def advance(count):
        for step, piece in rounds[:count]:
            line_step(step, [piece])
        del rounds[:count]

    advance(len(rounds) - 3 * PIECES + ORDER[0])
    copies[0] = gather_chips(groups[1], copies[0])
    advance(ORDER[1])
    for o in range(1, GRAD_GROUPS):
        copies[o] = gather_chips(groups[1 + o], copies[o])
    out_copies = gather_cores(outs, out_copies)
    advance(ORDER[2])
    copies[0] = gather_cores(groups[1], copies[0])
    advance(ORDER[3])
    for o in range(1, GRAD_GROUPS):
        copies[o] = gather_cores(groups[1 + o], copies[o])
    wout_out[...] = gathered(outs, out_copies).astype(F32)
    for o, group in enumerate(groups[1:]):
        size = group["full"].shape[0]
        here = pl.ds(o * size, size)
        result = gathered(group, copies[o]).astype(F32)
        query_out[here, :] = result[:, :HEAD]
        key_out[here, :] = result[:, HEAD : 2 * HEAD]
        value_out[here, :] = result[:, 2 * HEAD :]
    advance(len(rounds))
    tokens_out[...] = acc[...].astype(BF16)

    @pl.when(has_prior)
    def _():
        back.wait_recv()

    @pl.when(jnp.logical_not(has_prior))
    def _():
        tails.wait_recv()

    for copy in started:
        copy.wait_send()
    line_end()


def store_kernel(*refs):
    sem = refs[-1]
    copies = [pltpu.make_async_copy(refs[i], refs[5 + i], sem.at[i]) for i in range(5)]
    for copy in copies:
        copy.start()
    for copy in copies:
        copy.wait()


def fast(tokens, lengths, w_query, w_key, w_value, w_out, grad_out):
    rows, width = tokens.shape[1:]
    n_dp, n_tp = lax.axis_size("dp"), lax.axis_size("tp")
    total = rows * lax.axis_size("ctx")
    sizes = level_sizes(rows, total)
    levels = len(sizes)
    scale = float(n_dp * total) ** (-0.5)
    tail = pltpu.VMEM((2 * levels, BLOCK, HEAD), BF16)

    def group(count, columns):
        half = count // 2
        return dict(
            full=pltpu.VMEM((count, columns), F32),
            s1=pltpu.VMEM((half, columns), BF16),
            r1=pltpu.VMEM((half, columns), BF16),
            sum=pltpu.VMEM((half, columns), F32),
            s2=pltpu.VMEM((half, columns), BF16),
            r2=pltpu.VMEM((n_dp - 1, half // n_dp, columns), BF16),
            res=pltpu.VMEM((count, columns), BF16),
        )

    copies = 2 + (1 + GRAD_GROUPS) * (1 + 3 * (n_dp - 1) + 1)
    vm = pl.BlockSpec(memory_space=pltpu.VMEM)
    hbm = pl.BlockSpec(memory_space=pl.ANY)
    shapes = [((rows // n_tp, width), BF16)] + [((width, HEAD), F32)] * 3 + [((HEAD, width), F32)]
    summed = pl.pallas_call(
        partial(layer_kernel, sizes, scale, n_dp, n_tp),
        out_shape=tuple(pltpu.VMEM(*s) for s in shapes),
        in_specs=[pl.BlockSpec(memory_space=pltpu.SMEM)] + [hbm] * 6,
        out_specs=[vm] * 5,
        scratch_shapes=dict(
            attend_scratch(sizes),
            q2=[level_scratch(sizes, 0, BF16)] * 2,
            k2=[level_scratch(sizes, BLOCK, BF16)] * 2,
            v2=[level_scratch(sizes, BLOCK, BF16)] * 2,
            tok=pltpu.VMEM((rows, width), BF16),
            tok_t=pltpu.VMEM((width, rows), BF16),
            weights=pltpu.VMEM((width, 3 * HEAD), BF16),
            w_out=pltpu.VMEM((HEAD, width), BF16),
            cot=pltpu.VMEM((rows, width), BF16),
            r_s=pltpu.VMEM((rows, 3 * HEAD), BF16),
            load_sem=pltpu.SemaphoreType.DMA((5 + TOKEN_LOADS,)),
            tails_s=tail,
            tails_r=tail,
            back_s=tail,
            back_r=tail,
            part_s=pltpu.VMEM((rows, width), BF16),
            lines=[pltpu.VMEM((n_tp, PIECES, rows // n_tp // PIECES, width), BF16)] * 4,
            acc=pltpu.VMEM((rows // n_tp, width), F32),
            line_send=pltpu.SemaphoreType.DMA((2, n_tp, PIECES)),
            line_recv=pltpu.SemaphoreType.DMA((2, n_tp, PIECES)),
            groups=[group(HEAD, width)] + [group(width // GRAD_GROUPS, 3 * HEAD)] * GRAD_GROUPS,
            send_sem=pltpu.SemaphoreType.DMA((copies,)),
            recv_sem=pltpu.SemaphoreType.DMA((copies,)),
        ),
        compiler_params=pltpu.CompilerParams(
            vmem_limit_bytes=58 * 2**20, collective_id=0, has_side_effects=True
        ),
    )(lengths, tokens[0], w_query, w_key, w_value, w_out, grad_out[0])
    grad_tokens, grad_query, grad_key, grad_value, grad_w_out = pl.pallas_call(
        store_kernel,
        out_shape=tuple(jax.ShapeDtypeStruct(*s) for s in shapes),
        in_specs=[hbm] * 5,
        out_specs=[hbm] * 5,
        scratch_shapes=[pltpu.SemaphoreType.DMA((5,))],
        compiler_params=pltpu.CompilerParams(vmem_limit_bytes=2 * 2**20),
    )(*summed)
    return (grad_tokens[None], grad_query, grad_key, grad_value, grad_w_out)


def body(*args):
    rows = args[0].shape[1]
    sizes = level_sizes(rows, rows * lax.axis_size("ctx"))
    if sizes[-1] < BLOCK or sizes[0] % BLOCK or lax.axis_size("ctx") != 2:
        return local(*args)
    return fast(*args)

def solution(mesh):
    placed = (
        P("dp", "ctx", None),
        P("dp"),
        P(None, "tp"),
        P(None, "tp"),
        P(None, "tp"),
        P("tp", None),
        P("dp", "ctx", None),
    )
    return jax.shard_map(
        body,
        mesh=mesh,
        in_specs=placed,
        out_specs=(
            P("dp", ("ctx", "tp"), None),
            P(None, "tp"),
            P(None, "tp"),
            P(None, "tp"),
            P("tp", None),
        ),
        check_vma=False,
    )
```

```python
from functools import partial

import jax
import jax.numpy as jnp
from jax import lax
from jax.experimental import pallas as pl
from jax.experimental.pallas import tpu as pltpu
from jax.sharding import PartitionSpec as P

HEAD = 128
BLOCK = 128
LEVELS = 8


precise = lax.Precision.HIGHEST
very_low = -1e30


def passed_along(value, axis, steps):
    count = lax.axis_size(axis)
    first, last = (max(0, -steps), min(count, count - steps))
    return lax.ppermute(value, axis, [(source, source + steps) for source in range(first, last)])


def level_stats(queries, key_rows, values, query_pos, key_pos, height, block, weight):
    scores = jnp.einsum("nqe,nke->nqk", queries, key_rows, precision=precise) * queries.shape[
        -1
    ] ** (-0.5)
    query_at = query_pos[:, :, None]
    key_at = key_pos[:, None, :]
    allowed = (query_at // block - key_at // block <= 1) & (key_at >= 0)
    if height == 0:
        allowed = allowed & (key_at <= query_at)
    else:
        half_block = block // 2
        allowed = allowed & (query_at // half_block - key_at // half_block >= 2)
    masked = jnp.where(allowed, scores, very_low)
    row_max = jnp.max(masked, axis=-1)
    exp_scores = jnp.where(allowed, jnp.exp(masked - row_max[..., None]), 0.0)
    weighted = jnp.einsum("nqk,nke->nqe", exp_scores, values, precision=precise)
    totals = jnp.sum(exp_scores, axis=-1) * weight
    return (row_max, weighted, totals)


def head_stats(queries, key_rows, values, query_pos, key_pos, height, block, weight):
    single = partial(level_stats, height=height, block=block, weight=weight)
    return jax.vmap(single, in_axes=(0, 0, 0, None, None))(
        queries, key_rows, values, query_pos, key_pos
    )


def coarse(field_data, group_size, summed):
    grouped = field_data.reshape(
        field_data.shape[:-2]
        + (field_data.shape[-2] // group_size, group_size, field_data.shape[-1])
    )
    if summed:
        return jnp.sum(grouped, axis=-2)
    return jnp.mean(grouped, axis=-2)


def merge_levels(stats_list):
    best_max, running, mass_sum = stats_list[0]
    for row_max, weighted, totals in stats_list[1:]:
        new_best = jnp.maximum(best_max, row_max)
        keep_old = jnp.exp(best_max - new_best)
        gain_new = jnp.exp(row_max - new_best)
        running = running * keep_old[..., None] + weighted * gain_new[..., None]
        mass_sum = mass_sum * keep_old + totals * gain_new
        best_max = new_best
    return running / mass_sum[..., None]


def earlier(payload, distance):
    return passed_along(payload.astype(jnp.bfloat16), "ctx", distance).astype(payload.dtype)


def returned(payload, distance):
    return passed_along(payload.astype(jnp.bfloat16), "ctx", -distance).astype(payload.dtype)


def local(tokens, lengths, w_query, w_key, w_value, w_out, grad_out):
    devices = lax.axis_size("ctx")
    ctx_index = lax.axis_index("ctx")
    local_rows = tokens.shape[1]
    token_total = lax.axis_size("dp") * devices * local_rows
    grad_scale = float(token_total) ** (-0.5)
    flat_tokens = tokens[0]
    head_count = w_query.shape[1] // HEAD

    def split_heads(matrix):
        return matrix.reshape(local_rows, head_count, HEAD).transpose(1, 0, 2)

    def join_heads(field_data):
        return field_data.transpose(1, 0, 2).reshape(local_rows, head_count * HEAD)

    queries = split_heads(jnp.dot(flat_tokens, w_query, preferred_element_type=jnp.float32))
    key_rows = split_heads(jnp.dot(flat_tokens, w_key, preferred_element_type=jnp.float32))
    values = split_heads(jnp.dot(flat_tokens, w_value, preferred_element_type=jnp.float32))
    group_sizes = [2**height for height in range(LEVELS)]
    fine_levels = [height for height in range(LEVELS) if local_rows // group_sizes[height] >= BLOCK]
    rough_levels = [height for height in range(LEVELS) if local_rows // group_sizes[height] < BLOCK]

    def coarsen(all_queries, all_keys, all_values):
        return (
            [coarse(all_queries, group_sizes[height], False) for height in range(LEVELS)],
            [coarse(all_keys, group_sizes[height], False) for height in range(LEVELS)],
            [coarse(all_values, group_sizes[height], True) for height in range(LEVELS)],
        )

    (coarse_query, coarse_key, coarse_value), coarse_pull = jax.vjp(
        coarsen, queries, key_rows, values
    )
    tail_rows = jnp.stack(
        [
            jnp.concatenate([coarse_key[height][:, -BLOCK:] for height in fine_levels], 1),
            jnp.concatenate([coarse_value[height][:, -BLOCK:] for height in fine_levels], 1),
        ],
        0,
    )
    coarse_pack = jnp.stack(
        [
            jnp.concatenate([coarse_key[height] for height in rough_levels], 1),
            jnp.concatenate([coarse_value[height] for height in rough_levels], 1),
        ],
        0,
    )
    tail_count = tail_rows.shape[2]
    reach_devs = 2 * BLOCK // (local_rows // group_sizes[rough_levels[-1]])
    step_count = reach_devs.bit_length() - 1
    first_move = earlier(jnp.concatenate([tail_rows, coarse_pack], 2), 1)
    prior_tails = first_move[:, :, :tail_count]
    window = jnp.stack([first_move[:, :, tail_count:], coarse_pack], 0)
    for bit_pos in range(1, step_count):
        distance = 2**bit_pos
        if distance < devices:
            moved_rows = earlier(window, distance)
        else:
            moved_rows = jnp.zeros_like(window)
        window = jnp.concatenate([moved_rows, window], 0)
    prior_in = window[:-1]

    def attend_local(query_list, key_list, value_list, tails_in, rows_in):
        stats_list = []
        tail_at = 0
        rough_at = 0
        for height in range(LEVELS):
            group_size = group_sizes[height]
            coarse_rows = local_rows // group_size
            own_pos = ctx_index * coarse_rows + jnp.arange(coarse_rows, dtype=jnp.int32)
            if height in fine_levels:
                blocks = coarse_rows // BLOCK
                query_blocks = query_list[height].reshape(head_count, blocks, BLOCK, -1)
                key_blocks = key_list[height].reshape(head_count, blocks, BLOCK, -1)
                value_blocks = value_list[height].reshape(head_count, blocks, BLOCK, -1)
                prev_keys = tails_in[0][:, tail_at : tail_at + BLOCK][:, None]
                prev_values = tails_in[1][:, tail_at : tail_at + BLOCK][:, None]
                key_win = jnp.concatenate(
                    [jnp.concatenate([prev_keys, key_blocks[:, :-1]], 1), key_blocks], 2
                )
                value_win = jnp.concatenate(
                    [jnp.concatenate([prev_values, value_blocks[:, :-1]], 1), value_blocks], 2
                )
                query_pos = own_pos.reshape(blocks, BLOCK)
                key_pos = jnp.concatenate([query_pos - BLOCK, query_pos], 1)
                tail_at += BLOCK
            else:
                query_blocks = query_list[height][:, None]
                query_pos = own_pos[None]
                need_devs = 2 * BLOCK // coarse_rows
                earlier_keys = rows_in[
                    rows_in.shape[0] - (need_devs - 1) :, 0, :, rough_at : rough_at + coarse_rows
                ]
                earlier_values = rows_in[
                    rows_in.shape[0] - (need_devs - 1) :, 1, :, rough_at : rough_at + coarse_rows
                ]
                key_win = jnp.concatenate(
                    [
                        earlier_keys.transpose(1, 0, 2, 3).reshape(
                            head_count, (need_devs - 1) * coarse_rows, -1
                        ),
                        key_list[height],
                    ],
                    1,
                )[:, None]
                value_win = jnp.concatenate(
                    [
                        earlier_values.transpose(1, 0, 2, 3).reshape(
                            head_count, (need_devs - 1) * coarse_rows, -1
                        ),
                        value_list[height],
                    ],
                    1,
                )[:, None]
                key_pos = (
                    (ctx_index + 1) * coarse_rows
                    - need_devs * coarse_rows
                    + jnp.arange(need_devs * coarse_rows, dtype=jnp.int32)
                )[None]
                rough_at += coarse_rows
            row_max, weighted, totals = head_stats(
                query_blocks,
                key_win,
                value_win,
                query_pos,
                key_pos,
                height,
                BLOCK,
                float(group_size),
            )
            stats_list.append(
                (
                    jnp.repeat(row_max.reshape(head_count, coarse_rows), group_size, 1),
                    jnp.repeat(weighted.reshape(head_count, coarse_rows, -1), group_size, 1),
                    jnp.repeat(totals.reshape(head_count, coarse_rows), group_size, 1),
                )
            )
        return merge_levels(stats_list)

    attended, attend_pull = jax.vjp(
        attend_local, coarse_query, coarse_key, coarse_value, prior_tails, prior_in
    )
    mixed_heads = join_heads(attended).astype(jnp.bfloat16)
    positions = ctx_index * local_rows + jnp.arange(local_rows, dtype=jnp.int32)
    valid_rows = positions < lengths[0] * BLOCK
    cotangent = jnp.where(valid_rows[:, None], grad_out[0], jnp.zeros_like(grad_out[0]))
    grad_mixed = jnp.dot(cotangent, w_out.T, preferred_element_type=jnp.float32)
    grad_cquery, grad_ckey, grad_cvalue, grad_tails, grad_prior = attend_pull(
        split_heads(grad_mixed)
    )
    grad_cquery = list(grad_cquery)
    grad_ckey = list(grad_ckey)
    grad_cvalue = list(grad_cvalue)
    gradient = jnp.concatenate([grad_prior, jnp.zeros_like(coarse_pack)[None]], 0)
    for bit_pos in range(step_count - 1, 0, -1):
        distance = 2**bit_pos
        upper_part = gradient[distance:]
        if distance < devices:
            upper_part = upper_part + returned(gradient[:distance], distance)
        gradient = upper_part
    sent_back = returned(jnp.concatenate([grad_tails, gradient[0]], 2), 1)
    tails_back = sent_back[:, :, :tail_count]
    pack_back = sent_back[:, :, tail_count:] + gradient[1]
    tail_at = 0
    for height in fine_levels:
        grad_ckey[height] = (
            grad_ckey[height].at[:, -BLOCK:].add(tails_back[0, :, tail_at : tail_at + BLOCK])
        )
        grad_cvalue[height] = (
            grad_cvalue[height].at[:, -BLOCK:].add(tails_back[1, :, tail_at : tail_at + BLOCK])
        )
        tail_at += BLOCK
    rough_at = 0
    for height in rough_levels:
        coarse_rows = local_rows // group_sizes[height]
        grad_ckey[height] = grad_ckey[height] + pack_back[0, :, rough_at : rough_at + coarse_rows]
        grad_cvalue[height] = (
            grad_cvalue[height] + pack_back[1, :, rough_at : rough_at + coarse_rows]
        )
        rough_at += coarse_rows
    grad_q, grad_k, grad_v = coarse_pull((grad_cquery, grad_ckey, grad_cvalue))
    rounded_q = join_heads(grad_q).astype(jnp.bfloat16)
    rounded_k = join_heads(grad_k).astype(jnp.bfloat16)
    rounded_v = join_heads(grad_v).astype(jnp.bfloat16)
    partial_term = (
        jnp.dot(rounded_q, w_query.T, preferred_element_type=jnp.float32)
        + jnp.dot(rounded_k, w_key.T, preferred_element_type=jnp.float32)
        + jnp.dot(rounded_v, w_value.T, preferred_element_type=jnp.float32)
    )
    grad_tokens = lax.psum_scatter(
        partial_term.astype(jnp.bfloat16), "tp", scatter_dimension=0, tiled=True
    )[None]
    stacked_in = jnp.concatenate([rounded_q, rounded_k, rounded_v], 1)
    grads_in = jnp.einsum("rc,rh->ch", flat_tokens, stacked_in, preferred_element_type=jnp.float32)
    grads_out = jnp.einsum("rc,rh->ch", cotangent, mixed_heads, preferred_element_type=jnp.float32)
    summed = lax.psum(jnp.concatenate([grads_in, grads_out], 1) * grad_scale, ("dp", "ctx"))
    head_cols = head_count * HEAD
    grad_query = summed[:, :head_cols]
    grad_key = summed[:, head_cols : 2 * head_cols]
    grad_value = summed[:, 2 * head_cols : 3 * head_cols]
    grad_w_out = summed[:, 3 * head_cols :].T
    return (grad_tokens, grad_query, grad_key, grad_value, grad_w_out)


F32 = jnp.float32
BF16 = jnp.bfloat16
NT = (((1,), (1,)), ((), ()))
NN = (((1,), (0,)), ((), ()))
TN = (((0,), (0,)), ((), ()))


def mm(a, b, dims):
    return lax.dot_general(a.astype(BF16), b.astype(BF16), dims, preferred_element_type=F32)


def split(value):
    high = value.astype(BF16)
    return high, (value - high.astype(F32)).astype(BF16)


def mm3(a, b, dims):
    dot = partial(lax.dot_general, dimension_numbers=dims, preferred_element_type=F32)
    result = dot(a[1], b[0])
    if b[1] is not None:
        result = result + dot(a[0], b[1])
    return dot(a[0], b[0]) + result


def window_of(h, block, high, low):
    window = pl.ds(block * BLOCK, span(h))
    exact = h > 0 and block == 0
    return high[h][window, :], None if exact else low[h][window, :]


def pairs(ref, start, count):
    return ref[pl.ds(start, count, stride=2), :], ref[pl.ds(start + 1, count, stride=2), :]


def doubled(ref, value):
    count = value.shape[0]
    ref[pl.ds(0, count, stride=2), :] = value
    ref[pl.ds(1, count, stride=2), :] = value
    return ref[pl.ds(0, 2 * count), :]


def halved(ref, value):
    count = value.shape[0]
    ref[pl.ds(0, count), :] = value
    first, second = pairs(ref, 0, count // 2)
    return first + second


def level_sizes(rows, total):
    return [rows >> h for h in range(LEVELS) if h == 0 or (total >> h) > BLOCK]


def coarsen_keys(sizes, kw, vw):
    for h in range(1, len(sizes)):
        first, second = pairs(kw[h - 1], BLOCK, sizes[h])
        kw[h][pl.ds(BLOCK, sizes[h]), :] = (first + second) * 0.5
        first, second = pairs(vw[h - 1], BLOCK, sizes[h])
        vw[h][pl.ds(BLOCK, sizes[h]), :] = first + second


def coarsen_queries(sizes, qs):
    for h in range(1, len(sizes)):
        first, second = pairs(qs[h - 1], 0, sizes[h])
        qs[h][...] = (first + second) * 0.5


def span(h):
    return 2 * BLOCK if h == 0 else BLOCK


def block_mask(h, block, has_prior):
    row = lax.broadcasted_iota(jnp.int32, (BLOCK, span(h)), 0)
    col = lax.broadcasted_iota(jnp.int32, (BLOCK, span(h)), 1)
    if h == 0:
        allowed = col <= row + BLOCK
        if block == 0:
            allowed = allowed & ((col >= BLOCK) | has_prior)
    else:
        allowed = (row >= BLOCK // 2) | (col < BLOCK // 2)
        if block == 0:
            allowed = allowed & has_prior
    return allowed


def attend_blocks(places, has_prior, q2, k2, v2, probs, tops, nums, dens):
    rows = [pl.ds(block * BLOCK, BLOCK) for _, block in places]
    scores = [
        mm3((q2[0][h][r, :], q2[1][h][r, :]), window_of(h, block, *k2), NT)
        for (h, block), r in zip(places, rows)
    ]
    allowed = [block_mask(h, block, has_prior) for h, block in places]
    masked = [jnp.where(a, x, very_low) for a, x in zip(allowed, scores)]
    highest = [jnp.max(x, axis=-1, keepdims=True) for x in masked]
    weights = [
        jnp.where(a, jnp.exp(x - top), 0.0) for a, x, top in zip(allowed, masked, highest)
    ]
    for (h, block), r, p, top in zip(places, rows, weights, highest):
        probs[h][block] = p
        tops[h][r, :] = jnp.broadcast_to(top, (BLOCK, HEAD))
    for (h, block), r, p in zip(places, rows, weights):
        nums[h][r, :] = mm3(split(p), window_of(h, block, *v2), NN)
        dens[h][r, :] = jnp.broadcast_to(
            jnp.sum(p, axis=-1, keepdims=True) * float(2**h), (BLOCK, HEAD)
        )


def merge(sizes, tops, nums, dens, keeps, gains, temp):
    last = len(sizes) - 1
    top, num, den = tops[last][...], nums[last][...], dens[last][...]
    keeps[last][...] = jnp.ones_like(top)
    for h in range(last - 1, -1, -1):
        top, num, den = (doubled(t, x) for t, x in zip(temp, (top, num, den)))
        own = tops[h][...]
        best = jnp.maximum(own, top)
        keep, gain = jnp.exp(own - best), jnp.exp(top - best)
        keeps[h][...] = keep
        gains[h][...] = gain
        num = nums[h][...] * keep + num * gain
        den = dens[h][...] * keep + den * gain
        top = best
    inverse = 1.0 / den
    return num * inverse, inverse


def back_stats(sizes, attended, inverse, grad_mixed, keeps, gains, gs, ds, temp):
    delta = jnp.sum(attended * grad_mixed, axis=-1, keepdims=True)
    flow, part = grad_mixed * inverse, delta * inverse
    for h in range(len(sizes)):
        gs[h][...] = flow * keeps[h][...]
        ds[h][...] = part * keeps[h][...]
        if h + 1 < len(sizes):
            flow = halved(temp[0], flow * gains[h][...])
            part = halved(temp[1], part * gains[h][...])


def back_blocks(places, q2, k2, v2, probs, gs, ds, dq, dk, dv):
    rows = [pl.ds(block * BLOCK, BLOCK) for _, block in places]
    grads = [split(gs[h][r, :]) for (h, _), r in zip(places, rows)]
    along = [
        mm3(grad, window_of(h, block, *v2), NT) for (h, block), grad in zip(places, grads)
    ]
    for (h, block), r, grad in zip(places, rows, grads):
        dv[h][pl.ds(block * BLOCK, span(h)), :] += mm(probs[h][block], grad[0], TN)
    dscores = []
    for (h, block), r, x in zip(places, rows, along):
        loss = ds[h][r, :] * float(2**h)
        if h == 0:
            loss = jnp.concatenate([loss, loss], 1)
        dscores.append((probs[h][block] * (x - loss)).astype(BF16))
    for (h, block), r, dscore in zip(places, rows, dscores):
        window = pl.ds(block * BLOCK, span(h))
        dk[h][window, :] += mm(dscore, q2[0][h][r, :], TN)
        dq[h][r, :] = mm(dscore, k2[0][h][window, :], NN) * HEAD ** (-0.5)


def spread_down(sizes, own, factor, temp):
    total = own(len(sizes) - 1)
    for h in range(len(sizes) - 2, -1, -1):
        total = own(h) + doubled(temp, total * factor)
    return total


def level_scratch(sizes, extra=0, kind=F32):
    return [pltpu.VMEM((size + extra, HEAD), kind) for size in sizes]


def attend_scratch(sizes):
    per_level = lambda extra=0: level_scratch(sizes, extra)
    return dict(
        qs=per_level(),
        kw=per_level(BLOCK),
        vw=per_level(BLOCK),
        probs=[
            pltpu.VMEM((size // BLOCK, BLOCK, span(h)), F32) for h, size in enumerate(sizes)
        ],
        tops=per_level(),
        nums=per_level(),
        dens=per_level(),
        keeps=per_level(),
        gains=per_level(),
        gs=per_level(),
        ds=per_level(),
        dq=per_level(),
        dk=per_level(BLOCK),
        dv=per_level(BLOCK),
        temp=[pltpu.VMEM((sizes[0], HEAD), F32)] * 3,
    )
MESH = pl.DeviceIdType.MESH
PIECES = 4
TOKEN_LOADS = 1
PART_CHUNKS = 2
GRAD_GROUPS = 2
ORDER = (3, 2, 2, 3)


def at(index, size):
    return pl.ds(pl.multiple_of(index * size, size), size)


def layer_kernel(
    sizes, scale, n_dp, n_tp,
    length, tok_h, wq_h, wk_h, wv_h, wo_h, grad_h,
    tokens_out, query_out, key_out, value_out, wout_out,
    *, q2, k2, v2, tok, tok_t, weights, w_out, cot, r_s, load_sem, qs, kw, vw, probs, tops, nums, dens, keeps, gains, gs, ds, dq, dk, dv, temp,
    tails_s, tails_r, back_s, back_r, part_s, lines, acc, line_send, line_recv, groups, send_sem, recv_sem,
):
    rows, width = tok.shape
    levels = len(sizes)
    dp, me, tp = lax.axis_index("dp"), lax.axis_index("ctx"), lax.axis_index("tp")
    other = 1 - me
    has_prior = me > 0
    barrier = pltpu.get_barrier_semaphore()
    if n_dp == 4:
        dp_peers = [3 - dp, dp + 1 - 2 * lax.rem(dp, 2), lax.rem(dp + 2, 4)]
        owners = dp_peers
    else:
        dp_peers = [lax.rem(dp + o, n_dp) for o in range(1, n_dp)]
        owners = [lax.rem(dp + n_dp - o, n_dp) for o in range(1, n_dp)]
    for device in [{"ctx": other}] + [{"dp": p} for p in dp_peers]:
        pl.semaphore_signal(barrier, inc=1, device_id=device, device_id_type=MESH)
    for there, beside in ((tp > 0, tp - 1), (tp < n_tp - 1, tp + 1)):

        @pl.when(there)
        def _():
            pl.semaphore_signal(barrier, inc=1, device_id={"tp": beside}, device_id_type=MESH)

    arrivals = n_dp + (tp > 0).astype(jnp.int32) + (tp < n_tp - 1).astype(jnp.int32)
    chunk = rows // TOKEN_LOADS
    column = lambda o: weights.at[:, pl.ds(o * HEAD, HEAD)]
    moves = [(wk_h, column(1)), (wv_h, column(2))]
    for part in range(TOKEN_LOADS):
        here = pl.ds(part * chunk, chunk)
        moves.append((tok_h.at[here, :], tok.at[here, :]))
    moves += [(wq_h, column(0)), (grad_h, cot), (wo_h, w_out)]
    loads = [
        pltpu.make_async_copy(source, target, load_sem.at[o])
        for o, (source, target) in enumerate(moves)
    ]
    for load in loads:
        load.start()
    started = []
    share = rows // n_tp
    flows = ((0, tp, tp + 1), (1, n_tp - 1 - tp, tp - 1))

    def line_copy(flow, source, slot, piece, onto):
        return pltpu.make_async_remote_copy(
            src_ref=source, dst_ref=lines[2 * flow].at[slot, piece],
            send_sem=line_send.at[flow, slot, piece], recv_sem=line_recv.at[flow, slot, piece],
            device_id={"tp": onto}, device_id_type=MESH,
        )

    def line_piece(flow, slot, piece):
        mine = slot if flow else n_tp - 1 - slot
        return at(mine * PIECES + piece, share // PIECES)

    def line_start(slot):
        for piece in range(PIECES):
            for flow, place, onto in flows:

                @pl.when(place == 0)
                def _():
                    own = part_s.at[line_piece(flow, slot, piece), :]
                    line_copy(flow, own, slot, piece, onto).start()

    def line_step(step, pieces=range(PIECES)):
        for piece in pieces:
            for flow, place, onto in flows:
                slot = step - place
                arrived, summed = lines[2 * flow], lines[2 * flow + 1]

                @pl.when((slot >= 0) & (place > 0))
                def _():
                    line_copy(flow, arrived.at[slot, piece], slot, piece, onto).wait_recv()
                    if step < n_tp - 1:
                        own = part_s[line_piece(flow, slot, piece), :].astype(F32)
                        summed[slot, piece] = (own + arrived[slot, piece].astype(F32)).astype(BF16)
                        line_copy(flow, summed.at[slot, piece], slot, piece, onto).start()
                    else:
                        acc[at(piece, share // PIECES), :] += arrived[slot, piece].astype(F32)

    def line_end():
        for step in range(n_tp - 1):
            for piece in range(PIECES):
                for flow, place, onto in flows:
                    slot = step - place

                    @pl.when(slot >= 0)
                    def _():
                        source = lines[2 * flow + 1].at[slot, piece]
                        line_copy(flow, source, slot, piece, onto).wait_send()

    def send(src, dst, **device):
        slot = len(started)
        copy = pltpu.make_async_remote_copy(
            src_ref=src, dst_ref=dst, send_sem=send_sem.at[slot], recv_sem=recv_sem.at[slot],
            device_id=device, device_id_type=MESH,
        )
        copy.start()
        started.append(copy)
        return copy

    def swap_cores(group, full):
        group["full"][...] = full
        half = group["full"].shape[0] // 2
        group["s1"][...] = group["full"][at(other, half), :].astype(BF16)
        return [send(group["s1"], group["r1"], ctx=other)]

    def swap_chips(group, copies):
        half = group["full"].shape[0] // 2
        size = half // n_dp
        copies[0].wait_recv()
        total = group["full"][at(me, half), :] + group["r1"][...].astype(F32)
        group["sum"][...] = total
        group["s2"][...] = total.astype(BF16)
        return [
            send(group["s2"].at[at(p, size), :], group["r2"].at[o], dp=p)
            for o, p in enumerate(dp_peers)
        ]

    def gather_chips(group, copies):
        size = group["sum"].shape[0] // n_dp
        total = group["sum"][at(dp, size), :]
        for o, copy in enumerate(copies):
            copy.wait_recv()
            total = total + group["r2"][o].astype(F32)
        mine = at(me * n_dp + dp, size)
        group["res"][mine, :] = total.astype(BF16)
        piece = group["res"].at[mine, :]
        return [send(piece, piece, dp=p) for p in dp_peers], [send(piece, piece, ctx=other)]

    def gather_cores(group, copies):
        size = group["sum"].shape[0] // n_dp
        around, across = copies
        for copy, owner in reversed(list(zip(around, owners))):
            copy.wait_recv()
            piece = group["res"].at[at(me * n_dp + owner, size), :]
            across.append(send(piece, piece, ctx=other))
        return across

    def gathered(group, copies):
        for copy in copies:
            copy.wait_recv()
        return group["res"][...]

    for load in loads[:2]:
        load.wait()
    for part in range(TOKEN_LOADS):
        loads[2 + part].wait()
        chunk = rows // TOKEN_LOADS
        here = pl.ds(part * chunk, chunk)
        both = jnp.dot(tok[here, :], weights[:, HEAD:], preferred_element_type=F32)
        kw[0][pl.ds(BLOCK + part * chunk, chunk), :] = both[:, :HEAD]
        vw[0][pl.ds(BLOCK + part * chunk, chunk), :] = both[:, HEAD:]
    coarsen_keys(sizes, kw, vw)
    for h, size in enumerate(sizes):
        here = pl.ds(BLOCK, size)
        for pair, source in ((k2, kw), (v2, vw)):
            pair[0][h][here, :], pair[1][h][here, :] = split(source[h][here, :])
        tails_s[h] = k2[0][h][pl.ds(size, BLOCK), :]
        tails_s[levels + h] = v2[0][h][pl.ds(size, BLOCK), :]
    pl.semaphore_wait(barrier, arrivals)
    tails = send(tails_s, tails_r, ctx=other)
    loads[-3].wait()
    qs[0][...] = jnp.dot(tok[...], weights[:, :HEAD], preferred_element_type=F32)
    coarsen_queries(sizes, qs)
    for h in range(levels):
        q2[0][h][...], q2[1][h][...] = split(qs[h][...] * HEAD ** (-0.5))
    later = [(h, b) for h, size in enumerate(sizes) for b in range(1, size // BLOCK)]
    first = [(h, 0) for h in range(levels)]
    attend_blocks(later, has_prior, q2, k2, v2, probs, tops, nums, dens)

    loads[-2].wait()
    loads[-1].wait()
    positions = me * rows + lax.broadcasted_iota(jnp.int32, (rows, width), 0)
    cot[...] = jnp.where(positions < length[0] * BLOCK, cot[...], jnp.zeros((), BF16))
    grad_mixed = mm(cot[...], w_out[...], NT)
    for h in range(levels):
        dk[h][...] = jnp.zeros_like(dk[h])
        dv[h][...] = jnp.zeros_like(dv[h])
        for pair in (k2, v2):
            for part in pair:
                part[h][pl.ds(0, BLOCK), :] = jnp.zeros((BLOCK, HEAD), BF16)

    @pl.when(has_prior)
    def _():
        tails.wait_recv()
        for h in range(levels):
            k2[0][h][pl.ds(0, BLOCK), :] = tails_r[h]
            v2[0][h][pl.ds(0, BLOCK), :] = tails_r[levels + h]

    attend_blocks(first, has_prior, q2, k2, v2, probs, tops, nums, dens)
    attended, inverse = merge(sizes, tops, nums, dens, keeps, gains, temp)
    back_stats(sizes, attended, inverse, grad_mixed, keeps, gains, gs, ds, temp)
    back_blocks(first, q2, k2, v2, probs, gs, ds, dq, dk, dv)
    for h in range(levels):
        back_s[h] = dk[h][pl.ds(0, BLOCK), :].astype(BF16)
        back_s[levels + h] = dv[h][pl.ds(0, BLOCK), :].astype(BF16)
    back = send(back_s, back_r, ctx=other)
    tok_t[...] = tok[...].T
    outs = groups[0]
    out_copies = swap_cores(outs, mm(attended, cot[...], TN) * scale)
    back_blocks(later, q2, k2, v2, probs, gs, ds, dq, dk, dv)
    out_copies = swap_chips(outs, out_copies)
    r_s[:, :HEAD] = spread_down(sizes, lambda h: dq[h][...], 0.5, temp[0]).astype(BF16)

    @pl.when(jnp.logical_not(has_prior))
    def _():
        back.wait_recv()
        for h, size in enumerate(sizes):
            dk[h][pl.ds(size, BLOCK), :] += back_r[h].astype(F32)
            dv[h][pl.ds(size, BLOCK), :] += back_r[levels + h].astype(F32)

    own = lambda d: lambda h: d[h][pl.ds(BLOCK, sizes[h]), :]
    r_s[:, HEAD : 2 * HEAD] = spread_down(sizes, own(dk), 0.5, temp[0]).astype(BF16)
    r_s[:, 2 * HEAD :] = spread_down(sizes, own(dv), 1.0, temp[1]).astype(BF16)
    chunk = rows // PART_CHUNKS
    slots = n_tp // PART_CHUNKS
    for part in range(PART_CHUNKS):
        here = at(jnp.where(2 * tp < n_tp, PART_CHUNKS - 1 - part, part), chunk)
        part_s[here, :] = mm(r_s[here, :], weights[...], NT).astype(BF16)
        for slot in range(part * slots, min((part + 1) * slots, n_tp - 1)):
            line_start(slot)
    acc[...] = part_s[at(tp, share), :].astype(F32)
    copies = []
    for o, group in enumerate(groups[1:]):
        size = group["full"].shape[0]
        copies.append(swap_cores(group, jnp.dot(
            tok_t[pl.ds(o * size, size), :], r_s[...], preferred_element_type=F32
        ) * scale))
    copies = [swap_chips(group, c) for group, c in zip(groups[1:], copies)]
    out_copies = gather_chips(outs, out_copies)
    rounds = [(step, piece) for step in range(1, n_tp) for piece in range(PIECES)]

    def advance(count):
        for step, piece in rounds[:count]:
            line_step(step, [piece])
        del rounds[:count]

    advance(len(rounds) - 3 * PIECES + ORDER[0])
    copies[0] = gather_chips(groups[1], copies[0])
    advance(ORDER[1])
    for o in range(1, GRAD_GROUPS):
        copies[o] = gather_chips(groups[1 + o], copies[o])
    out_copies = gather_cores(outs, out_copies)
    advance(ORDER[2])
    copies[0] = gather_cores(groups[1], copies[0])
    wout_out[...] = gathered(outs, out_copies).astype(F32)
    advance(ORDER[3])
    for o in range(1, GRAD_GROUPS):
        copies[o] = gather_cores(groups[1 + o], copies[o])
    for o, group in enumerate(groups[1:]):
        size = group["full"].shape[0]
        here = pl.ds(o * size, size)
        result = gathered(group, copies[o]).astype(F32)
        query_out[here, :] = result[:, :HEAD]
        key_out[here, :] = result[:, HEAD : 2 * HEAD]
        value_out[here, :] = result[:, 2 * HEAD :]
    advance(len(rounds))
    tokens_out[...] = acc[...].astype(BF16)

    @pl.when(has_prior)
    def _():
        back.wait_recv()

    @pl.when(jnp.logical_not(has_prior))
    def _():
        tails.wait_recv()

    for copy in started:
        copy.wait_send()
    line_end()


def store_kernel(*refs):
    sem = refs[-1]
    copies = [pltpu.make_async_copy(refs[i], refs[5 + i], sem.at[i]) for i in range(5)]
    for copy in copies:
        copy.start()
    for copy in copies:
        copy.wait()


def fast(tokens, lengths, w_query, w_key, w_value, w_out, grad_out):
    rows, width = tokens.shape[1:]
    n_dp, n_tp = lax.axis_size("dp"), lax.axis_size("tp")
    total = rows * lax.axis_size("ctx")
    sizes = level_sizes(rows, total)
    levels = len(sizes)
    scale = float(n_dp * total) ** (-0.5)
    tail = pltpu.VMEM((2 * levels, BLOCK, HEAD), BF16)

    def group(count, columns):
        half = count // 2
        return dict(
            full=pltpu.VMEM((count, columns), F32),
            s1=pltpu.VMEM((half, columns), BF16),
            r1=pltpu.VMEM((half, columns), BF16),
            sum=pltpu.VMEM((half, columns), F32),
            s2=pltpu.VMEM((half, columns), BF16),
            r2=pltpu.VMEM((n_dp - 1, half // n_dp, columns), BF16),
            res=pltpu.VMEM((count, columns), BF16),
        )

    copies = 2 + (1 + GRAD_GROUPS) * (1 + 3 * (n_dp - 1) + 1)
    vm = pl.BlockSpec(memory_space=pltpu.VMEM)
    hbm = pl.BlockSpec(memory_space=pl.ANY)
    shapes = [((rows // n_tp, width), BF16)] + [((width, HEAD), F32)] * 3 + [((HEAD, width), F32)]
    summed = pl.pallas_call(
        partial(layer_kernel, sizes, scale, n_dp, n_tp),
        out_shape=tuple(pltpu.VMEM(*s) for s in shapes),
        in_specs=[pl.BlockSpec(memory_space=pltpu.SMEM)] + [hbm] * 6,
        out_specs=[vm] * 5,
        scratch_shapes=dict(
            attend_scratch(sizes),
            q2=[level_scratch(sizes, 0, BF16)] * 2,
            k2=[level_scratch(sizes, BLOCK, BF16)] * 2,
            v2=[level_scratch(sizes, BLOCK, BF16)] * 2,
            tok=pltpu.VMEM((rows, width), BF16),
            tok_t=pltpu.VMEM((width, rows), BF16),
            weights=pltpu.VMEM((width, 3 * HEAD), BF16),
            w_out=pltpu.VMEM((HEAD, width), BF16),
            cot=pltpu.VMEM((rows, width), BF16),
            r_s=pltpu.VMEM((rows, 3 * HEAD), BF16),
            load_sem=pltpu.SemaphoreType.DMA((5 + TOKEN_LOADS,)),
            tails_s=tail,
            tails_r=tail,
            back_s=tail,
            back_r=tail,
            part_s=pltpu.VMEM((rows, width), BF16),
            lines=[pltpu.VMEM((n_tp, PIECES, rows // n_tp // PIECES, width), BF16)] * 4,
            acc=pltpu.VMEM((rows // n_tp, width), F32),
            line_send=pltpu.SemaphoreType.DMA((2, n_tp, PIECES)),
            line_recv=pltpu.SemaphoreType.DMA((2, n_tp, PIECES)),
            groups=[group(HEAD, width)] + [group(width // GRAD_GROUPS, 3 * HEAD)] * GRAD_GROUPS,
            send_sem=pltpu.SemaphoreType.DMA((copies,)),
            recv_sem=pltpu.SemaphoreType.DMA((copies,)),
        ),
        compiler_params=pltpu.CompilerParams(
            vmem_limit_bytes=58 * 2**20, collective_id=0, has_side_effects=True
        ),
    )(lengths, tokens[0], w_query, w_key, w_value, w_out, grad_out[0])
    grad_tokens, grad_query, grad_key, grad_value, grad_w_out = pl.pallas_call(
        store_kernel,
        out_shape=tuple(jax.ShapeDtypeStruct(*s) for s in shapes),
        in_specs=[hbm] * 5,
        out_specs=[hbm] * 5,
        scratch_shapes=[pltpu.SemaphoreType.DMA((5,))],
        compiler_params=pltpu.CompilerParams(vmem_limit_bytes=2 * 2**20),
    )(*summed)
    return (grad_tokens[None], grad_query, grad_key, grad_value, grad_w_out)


def body(*args):
    rows = args[0].shape[1]
    sizes = level_sizes(rows, rows * lax.axis_size("ctx"))
    if sizes[-1] < BLOCK or sizes[0] % BLOCK or lax.axis_size("ctx") != 2:
        return local(*args)
    return fast(*args)

def solution(mesh):
    placed = (
        P("dp", "ctx", None),
        P("dp"),
        P(None, "tp"),
        P(None, "tp"),
        P(None, "tp"),
        P("tp", None),
        P("dp", "ctx", None),
    )
    return jax.shard_map(
        body,
        mesh=mesh,
        in_specs=placed,
        out_specs=(
            P("dp", ("ctx", "tp"), None),
            P(None, "tp"),
            P(None, "tp"),
            P(None, "tp"),
            P("tp", None),
        ),
        check_vma=False,
    )
```

```python
from functools import partial

import jax
import jax.numpy as jnp
from jax import lax
from jax.experimental import pallas as pl
from jax.experimental.pallas import tpu as pltpu
from jax.sharding import PartitionSpec as P

HEAD = 128
BLOCK = 128
LEVELS = 8


precise = lax.Precision.HIGHEST
very_low = -1e30


def passed_along(value, axis, steps):
    count = lax.axis_size(axis)
    first, last = (max(0, -steps), min(count, count - steps))
    return lax.ppermute(value, axis, [(source, source + steps) for source in range(first, last)])


def level_stats(queries, key_rows, values, query_pos, key_pos, height, block, weight):
    scores = jnp.einsum("nqe,nke->nqk", queries, key_rows, precision=precise) * queries.shape[
        -1
    ] ** (-0.5)
    query_at = query_pos[:, :, None]
    key_at = key_pos[:, None, :]
    allowed = (query_at // block - key_at // block <= 1) & (key_at >= 0)
    if height == 0:
        allowed = allowed & (key_at <= query_at)
    else:
        half_block = block // 2
        allowed = allowed & (query_at // half_block - key_at // half_block >= 2)
    masked = jnp.where(allowed, scores, very_low)
    row_max = jnp.max(masked, axis=-1)
    exp_scores = jnp.where(allowed, jnp.exp(masked - row_max[..., None]), 0.0)
    weighted = jnp.einsum("nqk,nke->nqe", exp_scores, values, precision=precise)
    totals = jnp.sum(exp_scores, axis=-1) * weight
    return (row_max, weighted, totals)


def head_stats(queries, key_rows, values, query_pos, key_pos, height, block, weight):
    single = partial(level_stats, height=height, block=block, weight=weight)
    return jax.vmap(single, in_axes=(0, 0, 0, None, None))(
        queries, key_rows, values, query_pos, key_pos
    )


def coarse(field_data, group_size, summed):
    grouped = field_data.reshape(
        field_data.shape[:-2]
        + (field_data.shape[-2] // group_size, group_size, field_data.shape[-1])
    )
    if summed:
        return jnp.sum(grouped, axis=-2)
    return jnp.mean(grouped, axis=-2)


def merge_levels(stats_list):
    best_max, running, mass_sum = stats_list[0]
    for row_max, weighted, totals in stats_list[1:]:
        new_best = jnp.maximum(best_max, row_max)
        keep_old = jnp.exp(best_max - new_best)
        gain_new = jnp.exp(row_max - new_best)
        running = running * keep_old[..., None] + weighted * gain_new[..., None]
        mass_sum = mass_sum * keep_old + totals * gain_new
        best_max = new_best
    return running / mass_sum[..., None]


def earlier(payload, distance):
    return passed_along(payload.astype(jnp.bfloat16), "ctx", distance).astype(payload.dtype)


def returned(payload, distance):
    return passed_along(payload.astype(jnp.bfloat16), "ctx", -distance).astype(payload.dtype)


def local(tokens, lengths, w_query, w_key, w_value, w_out, grad_out):
    devices = lax.axis_size("ctx")
    ctx_index = lax.axis_index("ctx")
    local_rows = tokens.shape[1]
    token_total = lax.axis_size("dp") * devices * local_rows
    grad_scale = float(token_total) ** (-0.5)
    flat_tokens = tokens[0]
    head_count = w_query.shape[1] // HEAD

    def split_heads(matrix):
        return matrix.reshape(local_rows, head_count, HEAD).transpose(1, 0, 2)

    def join_heads(field_data):
        return field_data.transpose(1, 0, 2).reshape(local_rows, head_count * HEAD)

    queries = split_heads(jnp.dot(flat_tokens, w_query, preferred_element_type=jnp.float32))
    key_rows = split_heads(jnp.dot(flat_tokens, w_key, preferred_element_type=jnp.float32))
    values = split_heads(jnp.dot(flat_tokens, w_value, preferred_element_type=jnp.float32))
    group_sizes = [2**height for height in range(LEVELS)]
    fine_levels = [height for height in range(LEVELS) if local_rows // group_sizes[height] >= BLOCK]
    rough_levels = [height for height in range(LEVELS) if local_rows // group_sizes[height] < BLOCK]

    def coarsen(all_queries, all_keys, all_values):
        return (
            [coarse(all_queries, group_sizes[height], False) for height in range(LEVELS)],
            [coarse(all_keys, group_sizes[height], False) for height in range(LEVELS)],
            [coarse(all_values, group_sizes[height], True) for height in range(LEVELS)],
        )

    (coarse_query, coarse_key, coarse_value), coarse_pull = jax.vjp(
        coarsen, queries, key_rows, values
    )
    tail_rows = jnp.stack(
        [
            jnp.concatenate([coarse_key[height][:, -BLOCK:] for height in fine_levels], 1),
            jnp.concatenate([coarse_value[height][:, -BLOCK:] for height in fine_levels], 1),
        ],
        0,
    )
    coarse_pack = jnp.stack(
        [
            jnp.concatenate([coarse_key[height] for height in rough_levels], 1),
            jnp.concatenate([coarse_value[height] for height in rough_levels], 1),
        ],
        0,
    )
    tail_count = tail_rows.shape[2]
    reach_devs = 2 * BLOCK // (local_rows // group_sizes[rough_levels[-1]])
    step_count = reach_devs.bit_length() - 1
    first_move = earlier(jnp.concatenate([tail_rows, coarse_pack], 2), 1)
    prior_tails = first_move[:, :, :tail_count]
    window = jnp.stack([first_move[:, :, tail_count:], coarse_pack], 0)
    for bit_pos in range(1, step_count):
        distance = 2**bit_pos
        if distance < devices:
            moved_rows = earlier(window, distance)
        else:
            moved_rows = jnp.zeros_like(window)
        window = jnp.concatenate([moved_rows, window], 0)
    prior_in = window[:-1]

    def attend_local(query_list, key_list, value_list, tails_in, rows_in):
        stats_list = []
        tail_at = 0
        rough_at = 0
        for height in range(LEVELS):
            group_size = group_sizes[height]
            coarse_rows = local_rows // group_size
            own_pos = ctx_index * coarse_rows + jnp.arange(coarse_rows, dtype=jnp.int32)
            if height in fine_levels:
                blocks = coarse_rows // BLOCK
                query_blocks = query_list[height].reshape(head_count, blocks, BLOCK, -1)
                key_blocks = key_list[height].reshape(head_count, blocks, BLOCK, -1)
                value_blocks = value_list[height].reshape(head_count, blocks, BLOCK, -1)
                prev_keys = tails_in[0][:, tail_at : tail_at + BLOCK][:, None]
                prev_values = tails_in[1][:, tail_at : tail_at + BLOCK][:, None]
                key_win = jnp.concatenate(
                    [jnp.concatenate([prev_keys, key_blocks[:, :-1]], 1), key_blocks], 2
                )
                value_win = jnp.concatenate(
                    [jnp.concatenate([prev_values, value_blocks[:, :-1]], 1), value_blocks], 2
                )
                query_pos = own_pos.reshape(blocks, BLOCK)
                key_pos = jnp.concatenate([query_pos - BLOCK, query_pos], 1)
                tail_at += BLOCK
            else:
                query_blocks = query_list[height][:, None]
                query_pos = own_pos[None]
                need_devs = 2 * BLOCK // coarse_rows
                earlier_keys = rows_in[
                    rows_in.shape[0] - (need_devs - 1) :, 0, :, rough_at : rough_at + coarse_rows
                ]
                earlier_values = rows_in[
                    rows_in.shape[0] - (need_devs - 1) :, 1, :, rough_at : rough_at + coarse_rows
                ]
                key_win = jnp.concatenate(
                    [
                        earlier_keys.transpose(1, 0, 2, 3).reshape(
                            head_count, (need_devs - 1) * coarse_rows, -1
                        ),
                        key_list[height],
                    ],
                    1,
                )[:, None]
                value_win = jnp.concatenate(
                    [
                        earlier_values.transpose(1, 0, 2, 3).reshape(
                            head_count, (need_devs - 1) * coarse_rows, -1
                        ),
                        value_list[height],
                    ],
                    1,
                )[:, None]
                key_pos = (
                    (ctx_index + 1) * coarse_rows
                    - need_devs * coarse_rows
                    + jnp.arange(need_devs * coarse_rows, dtype=jnp.int32)
                )[None]
                rough_at += coarse_rows
            row_max, weighted, totals = head_stats(
                query_blocks,
                key_win,
                value_win,
                query_pos,
                key_pos,
                height,
                BLOCK,
                float(group_size),
            )
            stats_list.append(
                (
                    jnp.repeat(row_max.reshape(head_count, coarse_rows), group_size, 1),
                    jnp.repeat(weighted.reshape(head_count, coarse_rows, -1), group_size, 1),
                    jnp.repeat(totals.reshape(head_count, coarse_rows), group_size, 1),
                )
            )
        return merge_levels(stats_list)

    attended, attend_pull = jax.vjp(
        attend_local, coarse_query, coarse_key, coarse_value, prior_tails, prior_in
    )
    mixed_heads = join_heads(attended).astype(jnp.bfloat16)
    positions = ctx_index * local_rows + jnp.arange(local_rows, dtype=jnp.int32)
    valid_rows = positions < lengths[0] * BLOCK
    cotangent = jnp.where(valid_rows[:, None], grad_out[0], jnp.zeros_like(grad_out[0]))
    grad_mixed = jnp.dot(cotangent, w_out.T, preferred_element_type=jnp.float32)
    grad_cquery, grad_ckey, grad_cvalue, grad_tails, grad_prior = attend_pull(
        split_heads(grad_mixed)
    )
    grad_cquery = list(grad_cquery)
    grad_ckey = list(grad_ckey)
    grad_cvalue = list(grad_cvalue)
    gradient = jnp.concatenate([grad_prior, jnp.zeros_like(coarse_pack)[None]], 0)
    for bit_pos in range(step_count - 1, 0, -1):
        distance = 2**bit_pos
        upper_part = gradient[distance:]
        if distance < devices:
            upper_part = upper_part + returned(gradient[:distance], distance)
        gradient = upper_part
    sent_back = returned(jnp.concatenate([grad_tails, gradient[0]], 2), 1)
    tails_back = sent_back[:, :, :tail_count]
    pack_back = sent_back[:, :, tail_count:] + gradient[1]
    tail_at = 0
    for height in fine_levels:
        grad_ckey[height] = (
            grad_ckey[height].at[:, -BLOCK:].add(tails_back[0, :, tail_at : tail_at + BLOCK])
        )
        grad_cvalue[height] = (
            grad_cvalue[height].at[:, -BLOCK:].add(tails_back[1, :, tail_at : tail_at + BLOCK])
        )
        tail_at += BLOCK
    rough_at = 0
    for height in rough_levels:
        coarse_rows = local_rows // group_sizes[height]
        grad_ckey[height] = grad_ckey[height] + pack_back[0, :, rough_at : rough_at + coarse_rows]
        grad_cvalue[height] = (
            grad_cvalue[height] + pack_back[1, :, rough_at : rough_at + coarse_rows]
        )
        rough_at += coarse_rows
    grad_q, grad_k, grad_v = coarse_pull((grad_cquery, grad_ckey, grad_cvalue))
    rounded_q = join_heads(grad_q).astype(jnp.bfloat16)
    rounded_k = join_heads(grad_k).astype(jnp.bfloat16)
    rounded_v = join_heads(grad_v).astype(jnp.bfloat16)
    partial_term = (
        jnp.dot(rounded_q, w_query.T, preferred_element_type=jnp.float32)
        + jnp.dot(rounded_k, w_key.T, preferred_element_type=jnp.float32)
        + jnp.dot(rounded_v, w_value.T, preferred_element_type=jnp.float32)
    )
    grad_tokens = lax.psum_scatter(
        partial_term.astype(jnp.bfloat16), "tp", scatter_dimension=0, tiled=True
    )[None]
    stacked_in = jnp.concatenate([rounded_q, rounded_k, rounded_v], 1)
    grads_in = jnp.einsum("rc,rh->ch", flat_tokens, stacked_in, preferred_element_type=jnp.float32)
    grads_out = jnp.einsum("rc,rh->ch", cotangent, mixed_heads, preferred_element_type=jnp.float32)
    summed = lax.psum(jnp.concatenate([grads_in, grads_out], 1) * grad_scale, ("dp", "ctx"))
    head_cols = head_count * HEAD
    grad_query = summed[:, :head_cols]
    grad_key = summed[:, head_cols : 2 * head_cols]
    grad_value = summed[:, 2 * head_cols : 3 * head_cols]
    grad_w_out = summed[:, 3 * head_cols :].T
    return (grad_tokens, grad_query, grad_key, grad_value, grad_w_out)


F32 = jnp.float32
BF16 = jnp.bfloat16
NT = (((1,), (1,)), ((), ()))
NN = (((1,), (0,)), ((), ()))
TN = (((0,), (0,)), ((), ()))


def mm(a, b, dims):
    return lax.dot_general(a.astype(BF16), b.astype(BF16), dims, preferred_element_type=F32)


def split(value):
    high = value.astype(BF16)
    return high, (value - high.astype(F32)).astype(BF16)


def mm3(a, b, dims):
    dot = partial(lax.dot_general, dimension_numbers=dims, preferred_element_type=F32)
    result = dot(a[1], b[0])
    if b[1] is not None:
        result = result + dot(a[0], b[1])
    return dot(a[0], b[0]) + result


def window_of(h, block, high, low):
    window = pl.ds(block * BLOCK, span(h))
    exact = h > 0 and block == 0
    return high[h][window, :], None if exact else low[h][window, :]


def pairs(ref, start, count):
    return ref[pl.ds(start, count, stride=2), :], ref[pl.ds(start + 1, count, stride=2), :]


def doubled(ref, value):
    count = value.shape[0]
    ref[pl.ds(0, count, stride=2), :] = value
    ref[pl.ds(1, count, stride=2), :] = value
    return ref[pl.ds(0, 2 * count), :]


def halved(ref, value):
    count = value.shape[0]
    ref[pl.ds(0, count), :] = value
    first, second = pairs(ref, 0, count // 2)
    return first + second


def level_sizes(rows, total):
    return [rows >> h for h in range(LEVELS) if h == 0 or (total >> h) > BLOCK]


def coarsen_keys(sizes, kw, vw):
    for h in range(1, len(sizes)):
        first, second = pairs(kw[h - 1], BLOCK, sizes[h])
        kw[h][pl.ds(BLOCK, sizes[h]), :] = (first + second) * 0.5
        first, second = pairs(vw[h - 1], BLOCK, sizes[h])
        vw[h][pl.ds(BLOCK, sizes[h]), :] = first + second


def coarsen_queries(sizes, qs):
    for h in range(1, len(sizes)):
        first, second = pairs(qs[h - 1], 0, sizes[h])
        qs[h][...] = (first + second) * 0.5


def span(h):
    return 2 * BLOCK if h == 0 else BLOCK


def block_mask(h, block, has_prior):
    row = lax.broadcasted_iota(jnp.int32, (BLOCK, span(h)), 0)
    col = lax.broadcasted_iota(jnp.int32, (BLOCK, span(h)), 1)
    if h == 0:
        allowed = col <= row + BLOCK
        if block == 0:
            allowed = allowed & ((col >= BLOCK) | has_prior)
    else:
        allowed = (row >= BLOCK // 2) | (col < BLOCK // 2)
        if block == 0:
            allowed = allowed & has_prior
    return allowed


def attend_blocks(places, has_prior, q2, k2, v2, probs, tops, nums, dens):
    rows = [pl.ds(block * BLOCK, BLOCK) for _, block in places]
    scores = [
        mm3((q2[0][h][r, :], q2[1][h][r, :]), window_of(h, block, *k2), NT)
        for (h, block), r in zip(places, rows)
    ]
    allowed = [block_mask(h, block, has_prior) for h, block in places]
    masked = [jnp.where(a, x, very_low) for a, x in zip(allowed, scores)]
    highest = [jnp.max(x, axis=-1, keepdims=True) for x in masked]
    weights = [
        jnp.where(a, jnp.exp(x - top), 0.0) for a, x, top in zip(allowed, masked, highest)
    ]
    for (h, block), r, p, top in zip(places, rows, weights, highest):
        probs[h][block] = p
        tops[h][r, :] = jnp.broadcast_to(top, (BLOCK, HEAD))
    for (h, block), r, p in zip(places, rows, weights):
        nums[h][r, :] = mm3(split(p), window_of(h, block, *v2), NN)
        dens[h][r, :] = jnp.broadcast_to(
            jnp.sum(p, axis=-1, keepdims=True) * float(2**h), (BLOCK, HEAD)
        )


def merge(sizes, tops, nums, dens, keeps, gains, temp):
    last = len(sizes) - 1
    top, num, den = tops[last][...], nums[last][...], dens[last][...]
    keeps[last][...] = jnp.ones_like(top)
    for h in range(last - 1, -1, -1):
        top, num, den = (doubled(t, x) for t, x in zip(temp, (top, num, den)))
        own = tops[h][...]
        best = jnp.maximum(own, top)
        keep, gain = jnp.exp(own - best), jnp.exp(top - best)
        keeps[h][...] = keep
        gains[h][...] = gain
        num = nums[h][...] * keep + num * gain
        den = dens[h][...] * keep + den * gain
        top = best
    inverse = 1.0 / den
    return num * inverse, inverse


def back_stats(sizes, attended, inverse, grad_mixed, keeps, gains, gs, ds, temp):
    delta = jnp.sum(attended * grad_mixed, axis=-1, keepdims=True)
    flow, part = grad_mixed * inverse, delta * inverse
    for h in range(len(sizes)):
        gs[h][...] = flow * keeps[h][...]
        ds[h][...] = part * keeps[h][...]
        if h + 1 < len(sizes):
            flow = halved(temp[0], flow * gains[h][...])
            part = halved(temp[1], part * gains[h][...])


def back_blocks(places, q2, k2, v2, probs, gs, ds, dq, dk, dv):
    rows = [pl.ds(block * BLOCK, BLOCK) for _, block in places]
    grads = [split(gs[h][r, :]) for (h, _), r in zip(places, rows)]
    along = [
        mm3(grad, window_of(h, block, *v2), NT) for (h, block), grad in zip(places, grads)
    ]
    for (h, block), r, grad in zip(places, rows, grads):
        dv[h][pl.ds(block * BLOCK, span(h)), :] += mm(probs[h][block], grad[0], TN)
    dscores = []
    for (h, block), r, x in zip(places, rows, along):
        loss = ds[h][r, :] * float(2**h)
        if h == 0:
            loss = jnp.concatenate([loss, loss], 1)
        dscores.append((probs[h][block] * (x - loss)).astype(BF16))
    for (h, block), r, dscore in zip(places, rows, dscores):
        window = pl.ds(block * BLOCK, span(h))
        dk[h][window, :] += mm(dscore, q2[0][h][r, :], TN)
        dq[h][r, :] = mm(dscore, k2[0][h][window, :], NN) * HEAD ** (-0.5)


def spread_down(sizes, own, factor, temp):
    total = own(len(sizes) - 1)
    for h in range(len(sizes) - 2, -1, -1):
        total = own(h) + doubled(temp, total * factor)
    return total


def level_scratch(sizes, extra=0, kind=F32):
    return [pltpu.VMEM((size + extra, HEAD), kind) for size in sizes]


def attend_scratch(sizes):
    per_level = lambda extra=0: level_scratch(sizes, extra)
    return dict(
        qs=per_level(),
        kw=per_level(BLOCK),
        vw=per_level(BLOCK),
        probs=[
            pltpu.VMEM((size // BLOCK, BLOCK, span(h)), F32) for h, size in enumerate(sizes)
        ],
        tops=per_level(),
        nums=per_level(),
        dens=per_level(),
        keeps=per_level(),
        gains=per_level(),
        gs=per_level(),
        ds=per_level(),
        dq=per_level(),
        dk=per_level(BLOCK),
        dv=per_level(BLOCK),
        temp=[pltpu.VMEM((sizes[0], HEAD), F32)] * 3,
    )
MESH = pl.DeviceIdType.MESH
PIECES = 4
TOKEN_LOADS = 1
PART_CHUNKS = 2
GRAD_GROUPS = 2
ORDER = (3, 2, 2, 3)


def at(index, size):
    return pl.ds(pl.multiple_of(index * size, size), size)


def layer_kernel(
    sizes, scale, n_dp, n_tp,
    length, tok_h, wq_h, wk_h, wv_h, wo_h, grad_h,
    tokens_out, query_out, key_out, value_out, wout_out,
    *, q2, k2, v2, tok, tok_t, weights, w_out, cot, r_s, load_sem, qs, kw, vw, probs, tops, nums, dens, keeps, gains, gs, ds, dq, dk, dv, temp,
    tails_s, tails_r, back_s, back_r, part_s, lines, acc, line_send, line_recv, groups, send_sem, recv_sem,
):
    rows, width = tok.shape
    levels = len(sizes)
    dp, me, tp = lax.axis_index("dp"), lax.axis_index("ctx"), lax.axis_index("tp")
    other = 1 - me
    has_prior = me > 0
    barrier = pltpu.get_barrier_semaphore()
    if n_dp == 4:
        dp_peers = [3 - dp, dp + 1 - 2 * lax.rem(dp, 2), lax.rem(dp + 2, 4)]
        owners = dp_peers
    else:
        dp_peers = [lax.rem(dp + o, n_dp) for o in range(1, n_dp)]
        owners = [lax.rem(dp + n_dp - o, n_dp) for o in range(1, n_dp)]
    for device in [{"ctx": other}] + [{"dp": p} for p in dp_peers]:
        pl.semaphore_signal(barrier, inc=1, device_id=device, device_id_type=MESH)
    for there, beside in ((tp > 0, tp - 1), (tp < n_tp - 1, tp + 1)):

        @pl.when(there)
        def _():
            pl.semaphore_signal(barrier, inc=1, device_id={"tp": beside}, device_id_type=MESH)

    arrivals = n_dp + (tp > 0).astype(jnp.int32) + (tp < n_tp - 1).astype(jnp.int32)
    chunk = rows // TOKEN_LOADS
    column = lambda o: weights.at[:, pl.ds(o * HEAD, HEAD)]
    moves = [(wk_h, column(1)), (wv_h, column(2))]
    for part in range(TOKEN_LOADS):
        here = pl.ds(part * chunk, chunk)
        moves.append((tok_h.at[here, :], tok.at[here, :]))
    moves += [(wq_h, column(0)), (grad_h, cot), (wo_h, w_out)]
    loads = [
        pltpu.make_async_copy(source, target, load_sem.at[o])
        for o, (source, target) in enumerate(moves)
    ]
    for load in loads:
        load.start()
    started = []
    share = rows // n_tp
    flows = ((0, tp, tp + 1), (1, n_tp - 1 - tp, tp - 1))

    def line_copy(flow, source, slot, piece, onto):
        return pltpu.make_async_remote_copy(
            src_ref=source, dst_ref=lines[2 * flow].at[slot, piece],
            send_sem=line_send.at[flow, slot, piece], recv_sem=line_recv.at[flow, slot, piece],
            device_id={"tp": onto}, device_id_type=MESH,
        )

    def line_piece(flow, slot, piece):
        mine = slot if flow else n_tp - 1 - slot
        return at(mine * PIECES + piece, share // PIECES)

    def line_start(slot):
        for piece in range(PIECES):
            for flow, place, onto in flows:

                @pl.when(place == 0)
                def _():
                    own = part_s.at[line_piece(flow, slot, piece), :]
                    line_copy(flow, own, slot, piece, onto).start()

    def line_step(step, pieces=range(PIECES)):
        for piece in pieces:
            for flow, place, onto in flows:
                slot = step - place
                arrived, summed = lines[2 * flow], lines[2 * flow + 1]

                @pl.when((slot >= 0) & (place > 0))
                def _():
                    line_copy(flow, arrived.at[slot, piece], slot, piece, onto).wait_recv()
                    if step < n_tp - 1:
                        own = part_s[line_piece(flow, slot, piece), :].astype(F32)
                        summed[slot, piece] = (own + arrived[slot, piece].astype(F32)).astype(BF16)
                        line_copy(flow, summed.at[slot, piece], slot, piece, onto).start()
                    else:
                        acc[at(piece, share // PIECES), :] += arrived[slot, piece].astype(F32)

    def line_end():
        for step in range(n_tp - 1):
            for piece in range(PIECES):
                for flow, place, onto in flows:
                    slot = step - place

                    @pl.when(slot >= 0)
                    def _():
                        source = lines[2 * flow + 1].at[slot, piece]
                        line_copy(flow, source, slot, piece, onto).wait_send()

    def send(src, dst, **device):
        slot = len(started)
        copy = pltpu.make_async_remote_copy(
            src_ref=src, dst_ref=dst, send_sem=send_sem.at[slot], recv_sem=recv_sem.at[slot],
            device_id=device, device_id_type=MESH,
        )
        copy.start()
        started.append(copy)
        return copy

    def swap_cores(group, full):
        group["full"][...] = full
        half = group["full"].shape[0] // 2
        group["s1"][...] = group["full"][at(other, half), :].astype(BF16)
        return [send(group["s1"], group["r1"], ctx=other)]

    def swap_chips(group, copies):
        half = group["full"].shape[0] // 2
        size = half // n_dp
        copies[0].wait_recv()
        total = group["full"][at(me, half), :] + group["r1"][...].astype(F32)
        group["sum"][...] = total
        group["s2"][...] = total.astype(BF16)
        return [
            send(group["s2"].at[at(p, size), :], group["r2"].at[o], dp=p)
            for o, p in enumerate(dp_peers)
        ]

    def gather_chips(group, copies):
        size = group["sum"].shape[0] // n_dp
        total = group["sum"][at(dp, size), :]
        for o, copy in enumerate(copies):
            copy.wait_recv()
            total = total + group["r2"][o].astype(F32)
        mine = at(me * n_dp + dp, size)
        group["res"][mine, :] = total.astype(BF16)
        piece = group["res"].at[mine, :]
        return [send(piece, piece, dp=p) for p in dp_peers], [send(piece, piece, ctx=other)]

    def gather_cores(group, copies):
        size = group["sum"].shape[0] // n_dp
        around, across = copies
        for copy, owner in reversed(list(zip(around, owners))):
            copy.wait_recv()
            piece = group["res"].at[at(me * n_dp + owner, size), :]
            across.append(send(piece, piece, ctx=other))
        return across

    def gathered(group, copies):
        for copy in copies:
            copy.wait_recv()
        return group["res"][...]

    for load in loads[:2]:
        load.wait()
    for part in range(TOKEN_LOADS):
        loads[2 + part].wait()
        chunk = rows // TOKEN_LOADS
        here = pl.ds(part * chunk, chunk)
        both = jnp.dot(tok[here, :], weights[:, HEAD:], preferred_element_type=F32)
        kw[0][pl.ds(BLOCK + part * chunk, chunk), :] = both[:, :HEAD]
        vw[0][pl.ds(BLOCK + part * chunk, chunk), :] = both[:, HEAD:]
    coarsen_keys(sizes, kw, vw)
    for h, size in enumerate(sizes):
        here = pl.ds(BLOCK, size)
        for pair, source in ((k2, kw), (v2, vw)):
            pair[0][h][here, :], pair[1][h][here, :] = split(source[h][here, :])
        tails_s[h] = k2[0][h][pl.ds(size, BLOCK), :]
        tails_s[levels + h] = v2[0][h][pl.ds(size, BLOCK), :]
    pl.semaphore_wait(barrier, arrivals)
    tails = send(tails_s, tails_r, ctx=other)
    loads[-3].wait()
    qs[0][...] = jnp.dot(tok[...], weights[:, :HEAD], preferred_element_type=F32)
    coarsen_queries(sizes, qs)
    for h in range(levels):
        q2[0][h][...], q2[1][h][...] = split(qs[h][...] * HEAD ** (-0.5))
    later = [(h, b) for h, size in enumerate(sizes) for b in range(1, size // BLOCK)]
    first = [(h, 0) for h in range(levels)]
    attend_blocks(later, has_prior, q2, k2, v2, probs, tops, nums, dens)

    loads[-2].wait()
    loads[-1].wait()
    positions = me * rows + lax.broadcasted_iota(jnp.int32, (rows, width), 0)
    cot[...] = jnp.where(positions < length[0] * BLOCK, cot[...], jnp.zeros((), BF16))
    grad_mixed = mm(cot[...], w_out[...], NT)
    for h in range(levels):
        dk[h][...] = jnp.zeros_like(dk[h])
        dv[h][...] = jnp.zeros_like(dv[h])
        for pair in (k2, v2):
            for part in pair:
                part[h][pl.ds(0, BLOCK), :] = jnp.zeros((BLOCK, HEAD), BF16)

    @pl.when(has_prior)
    def _():
        tails.wait_recv()
        for h in range(levels):
            k2[0][h][pl.ds(0, BLOCK), :] = tails_r[h]
            v2[0][h][pl.ds(0, BLOCK), :] = tails_r[levels + h]

    attend_blocks(first, has_prior, q2, k2, v2, probs, tops, nums, dens)
    attended, inverse = merge(sizes, tops, nums, dens, keeps, gains, temp)
    back_stats(sizes, attended, inverse, grad_mixed, keeps, gains, gs, ds, temp)
    back_blocks(first, q2, k2, v2, probs, gs, ds, dq, dk, dv)
    for h in range(levels):
        back_s[h] = dk[h][pl.ds(0, BLOCK), :].astype(BF16)
        back_s[levels + h] = dv[h][pl.ds(0, BLOCK), :].astype(BF16)
    back = send(back_s, back_r, ctx=other)
    tok_t[...] = tok[...].T
    outs = groups[0]
    out_copies = swap_cores(outs, mm(attended, cot[...], TN) * scale)
    back_blocks(later, q2, k2, v2, probs, gs, ds, dq, dk, dv)
    out_copies = swap_chips(outs, out_copies)
    r_s[:, :HEAD] = spread_down(sizes, lambda h: dq[h][...], 0.5, temp[0]).astype(BF16)

    @pl.when(jnp.logical_not(has_prior))
    def _():
        back.wait_recv()
        for h, size in enumerate(sizes):
            dk[h][pl.ds(size, BLOCK), :] += back_r[h].astype(F32)
            dv[h][pl.ds(size, BLOCK), :] += back_r[levels + h].astype(F32)

    own = lambda d: lambda h: d[h][pl.ds(BLOCK, sizes[h]), :]
    k_sum, v_sum = own(dk)(levels - 1), own(dv)(levels - 1)
    for h in range(levels - 2, -1, -1):
        k_up, v_up = doubled(temp[0], k_sum * 0.5), doubled(temp[1], v_sum)
        k_sum, v_sum = own(dk)(h) + k_up, own(dv)(h) + v_up
    r_s[:, HEAD : 2 * HEAD] = k_sum.astype(BF16)
    r_s[:, 2 * HEAD :] = v_sum.astype(BF16)
    chunk = rows // PART_CHUNKS
    slots = n_tp // PART_CHUNKS
    for part in range(PART_CHUNKS):
        here = at(jnp.where(2 * tp < n_tp, PART_CHUNKS - 1 - part, part), chunk)
        part_s[here, :] = mm(r_s[here, :], weights[...], NT).astype(BF16)
        for slot in range(part * slots, min((part + 1) * slots, n_tp - 1)):
            line_start(slot)
    acc[...] = part_s[at(tp, share), :].astype(F32)
    copies = []
    for o, group in enumerate(groups[1:]):
        size = group["full"].shape[0]
        copies.append(swap_cores(group, jnp.dot(
            tok_t[pl.ds(o * size, size), :], r_s[...], preferred_element_type=F32
        ) * scale))
    copies = [swap_chips(group, c) for group, c in zip(groups[1:], copies)]
    out_copies = gather_chips(outs, out_copies)
    rounds = [(step, piece) for step in range(1, n_tp) for piece in range(PIECES)]

    def advance(count):
        for step, piece in rounds[:count]:
            line_step(step, [piece])
        del rounds[:count]

    advance(len(rounds) - 3 * PIECES + ORDER[0])
    copies[0] = gather_chips(groups[1], copies[0])
    advance(ORDER[1])
    for o in range(1, GRAD_GROUPS):
        copies[o] = gather_chips(groups[1 + o], copies[o])
    out_copies = gather_cores(outs, out_copies)
    advance(ORDER[2])
    copies[0] = gather_cores(groups[1], copies[0])
    wout_out[...] = gathered(outs, out_copies).astype(F32)
    advance(ORDER[3])
    for o in range(1, GRAD_GROUPS):
        copies[o] = gather_cores(groups[1 + o], copies[o])
    for o, group in enumerate(groups[1:]):
        size = group["full"].shape[0]
        here = pl.ds(o * size, size)
        result = gathered(group, copies[o]).astype(F32)
        query_out[here, :] = result[:, :HEAD]
        key_out[here, :] = result[:, HEAD : 2 * HEAD]
        value_out[here, :] = result[:, 2 * HEAD :]
    advance(len(rounds))
    tokens_out[...] = acc[...].astype(BF16)

    @pl.when(has_prior)
    def _():
        back.wait_recv()

    @pl.when(jnp.logical_not(has_prior))
    def _():
        tails.wait_recv()

    for copy in started:
        copy.wait_send()
    line_end()


def store_kernel(*refs):
    sem = refs[-1]
    copies = [pltpu.make_async_copy(refs[i], refs[5 + i], sem.at[i]) for i in range(5)]
    for copy in copies:
        copy.start()
    for copy in copies:
        copy.wait()


def fast(tokens, lengths, w_query, w_key, w_value, w_out, grad_out):
    rows, width = tokens.shape[1:]
    n_dp, n_tp = lax.axis_size("dp"), lax.axis_size("tp")
    total = rows * lax.axis_size("ctx")
    sizes = level_sizes(rows, total)
    levels = len(sizes)
    scale = float(n_dp * total) ** (-0.5)
    tail = pltpu.VMEM((2 * levels, BLOCK, HEAD), BF16)

    def group(count, columns):
        half = count // 2
        return dict(
            full=pltpu.VMEM((count, columns), F32),
            s1=pltpu.VMEM((half, columns), BF16),
            r1=pltpu.VMEM((half, columns), BF16),
            sum=pltpu.VMEM((half, columns), F32),
            s2=pltpu.VMEM((half, columns), BF16),
            r2=pltpu.VMEM((n_dp - 1, half // n_dp, columns), BF16),
            res=pltpu.VMEM((count, columns), BF16),
        )

    copies = 2 + (1 + GRAD_GROUPS) * (1 + 3 * (n_dp - 1) + 1)
    vm = pl.BlockSpec(memory_space=pltpu.VMEM)
    hbm = pl.BlockSpec(memory_space=pl.ANY)
    shapes = [((rows // n_tp, width), BF16)] + [((width, HEAD), F32)] * 3 + [((HEAD, width), F32)]
    summed = pl.pallas_call(
        partial(layer_kernel, sizes, scale, n_dp, n_tp),
        out_shape=tuple(pltpu.VMEM(*s) for s in shapes),
        in_specs=[pl.BlockSpec(memory_space=pltpu.SMEM)] + [hbm] * 6,
        out_specs=[vm] * 5,
        scratch_shapes=dict(
            attend_scratch(sizes),
            q2=[level_scratch(sizes, 0, BF16)] * 2,
            k2=[level_scratch(sizes, BLOCK, BF16)] * 2,
            v2=[level_scratch(sizes, BLOCK, BF16)] * 2,
            tok=pltpu.VMEM((rows, width), BF16),
            tok_t=pltpu.VMEM((width, rows), BF16),
            weights=pltpu.VMEM((width, 3 * HEAD), BF16),
            w_out=pltpu.VMEM((HEAD, width), BF16),
            cot=pltpu.VMEM((rows, width), BF16),
            r_s=pltpu.VMEM((rows, 3 * HEAD), BF16),
            load_sem=pltpu.SemaphoreType.DMA((5 + TOKEN_LOADS,)),
            tails_s=tail,
            tails_r=tail,
            back_s=tail,
            back_r=tail,
            part_s=pltpu.VMEM((rows, width), BF16),
            lines=[pltpu.VMEM((n_tp, PIECES, rows // n_tp // PIECES, width), BF16)] * 4,
            acc=pltpu.VMEM((rows // n_tp, width), F32),
            line_send=pltpu.SemaphoreType.DMA((2, n_tp, PIECES)),
            line_recv=pltpu.SemaphoreType.DMA((2, n_tp, PIECES)),
            groups=[group(HEAD, width)] + [group(width // GRAD_GROUPS, 3 * HEAD)] * GRAD_GROUPS,
            send_sem=pltpu.SemaphoreType.DMA((copies,)),
            recv_sem=pltpu.SemaphoreType.DMA((copies,)),
        ),
        compiler_params=pltpu.CompilerParams(
            vmem_limit_bytes=58 * 2**20, collective_id=0, has_side_effects=True
        ),
    )(lengths, tokens[0], w_query, w_key, w_value, w_out, grad_out[0])
    grad_tokens, grad_query, grad_key, grad_value, grad_w_out = pl.pallas_call(
        store_kernel,
        out_shape=tuple(jax.ShapeDtypeStruct(*s) for s in shapes),
        in_specs=[hbm] * 5,
        out_specs=[hbm] * 5,
        scratch_shapes=[pltpu.SemaphoreType.DMA((5,))],
        compiler_params=pltpu.CompilerParams(vmem_limit_bytes=2 * 2**20),
    )(*summed)
    return (grad_tokens[None], grad_query, grad_key, grad_value, grad_w_out)


def body(*args):
    rows = args[0].shape[1]
    sizes = level_sizes(rows, rows * lax.axis_size("ctx"))
    if sizes[-1] < BLOCK or sizes[0] % BLOCK or lax.axis_size("ctx") != 2:
        return local(*args)
    return fast(*args)

def solution(mesh):
    placed = (
        P("dp", "ctx", None),
        P("dp"),
        P(None, "tp"),
        P(None, "tp"),
        P(None, "tp"),
        P("tp", None),
        P("dp", "ctx", None),
    )
    return jax.shard_map(
        body,
        mesh=mesh,
        in_specs=placed,
        out_specs=(
            P("dp", ("ctx", "tp"), None),
            P(None, "tp"),
            P(None, "tp"),
            P(None, "tp"),
            P("tp", None),
        ),
        check_vma=False,
    )
```
